32 devices in a mesh: section: 2 (over core), dp: 4 (over y, x), tensor: 4 (over z).
Axes of the slice: x: 2, y: 2, z: 4, core: 2. Of those that a mesh axis runs over, the one named last changes fastest.
Arguments:
- layer_input: bfloat16 [6, 16, 128, 768], P(None, ('dp', 'tensor')), may hold values from -6 to 6
- out_grad: bfloat16 [6, 16, 128, 768], P(None, ('dp', 'tensor')), may hold values from -6 to 6
- loss_mask: int32 [6, 16, 128], P(None, ('dp', 'tensor')), may hold values from 0 to 1, as said below
- query_key_value_weight: bfloat16 [2, 768, 3, 768], P('section', None, None, 'tensor'), may hold values from -0.21875 to 0.21875
- attention_output_weight: bfloat16 [2, 768, 768], P('section', 'tensor'), may hold values from -0.875 to 0.875
- gate_up_weight: bfloat16 [2, 768, 2, 3072], P('section', None, None, 'tensor'), may hold values from -0.21875 to 0.21875
- down_weight: bfloat16 [2, 3072, 768], P('section', 'tensor'), may hold values from -0.109375 to 0.109375
- norm1_gain: float32 [2, 768], P('section'), may hold values from 0.1 to 1.9
- norm1_bias: float32 [2, 768], P('section'), may hold values from -2.5 to 2.5
- norm2_gain: float32 [2, 768], P('section'), may hold values from 0.1 to 1.9
- norm2_bias: float32 [2, 768], P('section'), may hold values from -2.5 to 2.5
Outputs:
- layer_out: bfloat16 [2, 6, 16, 128, 768], P('section', None, ('dp', 'tensor'))
- input_grad: float32 [2, 6, 16, 128, 768], P('section', None, ('dp', 'tensor'))
- grad_qkv: float32 [2, 768, 3, 768], P('section', None, None, 'tensor')
- grad_out: float32 [2, 768, 768], P('section', 'tensor')
- grad_in: float32 [2, 768, 2, 3072], P('section', None, None, 'tensor')
- grad_down: float32 [2, 3072, 768], P('section', 'tensor')
- grad_norm1_gain: float32 [2, 768], P('section', 'tensor')
- grad_norm1_bias: float32 [2, 768], P('section', 'tensor')
- grad_norm2_gain: float32 [2, 768], P('section', 'tensor')
- grad_norm2_bias: float32 [2, 768], P('section', 'tensor')
The draws below stay inside these ranges and needn't reach their ends.
Inputs may be any that keep to these rules, and one draw needn't show every extreme that they name: loss_mask holds 0 or 1; each sequence has 8 to 32 ones, and in every micro-batch some sequence has exactly 32.
All inputs are finite; a program needn't handle non-finite values.
Results may differ from the reference program's by a relative error of at most 0.034.
Values may be sent and summed in bfloat16 or wider, within the bound.
No kernel may reach another device: no remote copies, remote signals or barrier semaphores. Data moves between devices by JAX's collectives and lax.ppermute only.
A program may use at most 128 MiB of HBM per device.

```python
import math
import jax
import jax.numpy as jnp
import numpy as np
from jax import lax

D = 768
HEADS = 12
HEAD_DIM = 64
FF = 3072
LEN = 128
MB = 6
LAYERS = 2
SEQS_MB = 16
MASK_MOST = 32


def draw_loss_mask(key, part):
    count_key = jax.random.fold_in(key, 11)
    pick_key = jax.random.fold_in(key, 23)
    score_key = jax.random.fold_in(key, 37)
    counts = jax.random.randint(count_key, (MB, SEQS_MB), MASK_MOST // 4, MASK_MOST + 1)
    chosen = jax.random.randint(pick_key, (MB,), 0, SEQS_MB)
    counts = jnp.where(jnp.arange(SEQS_MB)[None, :] == chosen[:, None], MASK_MOST, counts)
    scores = jax.random.randint(score_key, (MB, SEQS_MB, LEN), 0, 1 << 20) * LEN + jnp.arange(LEN)[None, None, :]
    order = jnp.argsort(scores, axis=-1)
    ranks = jnp.argsort(order, axis=-1)
    return (ranks < counts[..., None]).astype(jnp.int32)


def level_of(rng, dims, pieces, least, largest):
    def one(axis_at, blocks):
        heights = jax.random.uniform(jax.random.fold_in(jax.random.fold_in(rng, 6), axis_at), (blocks,), jnp.float32, least / len(pieces), largest / len(pieces))
        return jnp.repeat(jnp.exp(heights), dims[axis_at] // blocks).reshape((-1,) + (1,) * (len(dims) - axis_at - 1))

    level = one(*pieces[0])
    for cut in pieces[1:]:
        level = level * one(*cut)
    return level


def normal_values(key, dims, scale, reach, split=(), kind=jnp.bfloat16):
    result = scale * jax.random.normal(key, dims, jnp.float32)
    if split:
        result = result * level_of(key, dims, split, -0.22, 0.18)
    return jnp.clip(result, -reach, reach).astype(kind)


def setup_inputs(seed: int = 0) -> dict:
    key_of = jax.random.split(jax.random.key(seed), 12)
    return {
        "layer_input": normal_values(key_of[0], (MB, SEQS_MB, LEN, D), 1.0, 6.0, ((1, 16),)),
        "out_grad": normal_values(key_of[1], (MB, SEQS_MB, LEN, D), 1.0, 6.0, ((1, 16),)),
        "loss_mask": draw_loss_mask(jax.random.fold_in(key_of[11], 71), 0),
        "query_key_value_weight": normal_values(key_of[3], (LAYERS, D, 3, D), D ** -0.5, 0.21875, ((0, 2), (3, 4))),
        "attention_output_weight": normal_values(key_of[4], (LAYERS, D, D), (D // 16) ** -0.5, 0.875, ((0, 2), (1, 4))),
        "gate_up_weight": normal_values(key_of[5], (LAYERS, D, 2, FF), D ** -0.5, 0.21875, ((0, 2), (3, 4))),
        "down_weight": normal_values(key_of[6], (LAYERS, FF, D), FF ** -0.5, 0.109375, ((0, 2), (1, 4))),
        "norm1_gain": jnp.clip(1.0 + 0.18 * jax.random.normal(key_of[7], (LAYERS, D), jnp.float32), 0.1, 1.9),
        "norm1_bias": normal_values(key_of[8], (LAYERS, D), 0.5, 2.5, ((0, 2),), jnp.float32),
        "norm2_gain": jnp.clip(1.0 + 0.18 * jax.random.normal(key_of[9], (LAYERS, D), jnp.float32), 0.1, 1.9),
        "norm2_bias": normal_values(key_of[10], (LAYERS, D), 0.5, 2.5, ((0, 2),), jnp.float32),
    }


NORM_EPSILON = 1e-05
MATMUL_PRECISION = lax.Precision.HIGHEST

@jax.custom_vjp
def low(v):
    return lax.optimization_barrier(v.astype(jnp.bfloat16)).astype(jnp.float32)

@jax.custom_vjp
def low_back(v):
    return v

def low_keep(v):
    return (low(v), None)

def low_pass(kept, grad):
    return (grad,)

def back_keep(v):
    return (v, None)

def back_low(kept, grad):
    return (low(grad),)
low.defvjp(low_keep, low_pass)
low_back.defvjp(back_keep, back_low)

def power_slopes(total_heads):
    return [2.0 ** (-8.0 * (index + 1) / total_heads) for index in range(total_heads)]

def alibi_table(number_heads):
    closest = 2 ** int(math.floor(math.log2(number_heads)))
    slopes = power_slopes(closest)
    if closest < number_heads:
        slopes = slopes + power_slopes(2 * closest)[0::2][:number_heads - closest]
    return np.array(slopes, dtype=np.float32)

def norm_rows(values, gain, offset):
    row_mean = lax.optimization_barrier(jnp.mean(values, axis=-1, keepdims=True))
    centred = values - row_mean
    row_var = lax.optimization_barrier(jnp.mean(centred * centred, axis=-1, keepdims=True))
    return centred * lax.rsqrt(row_var + NORM_EPSILON) * gain + offset

def block_forward(input_batch, params):
    query_key_value_weight, attention_output_weight, gate_up_weight, down_weight, gain_one, offset_one, gain_two, offset_two = params
    seq_count = input_batch.shape[0]
    length = input_batch.shape[1]
    projected_state = jnp.einsum('pex,xyn->peyn', input_batch, query_key_value_weight, precision=MATMUL_PRECISION)
    projected_state = low_back(low(projected_state))
    heads_view = projected_state.reshape(seq_count, length, 3, HEADS, HEAD_DIM)
    queries = heads_view[:, :, 0]
    key_heads = heads_view[:, :, 1]
    value_heads = heads_view[:, :, 2]
    scores = jnp.einsum('sqhe,skhe->shqk', queries, key_heads, precision=MATMUL_PRECISION) * HEAD_DIM ** (-0.5)
    positions = jnp.arange(length)
    distance = jnp.abs(positions[:, None] - positions[None, :]).astype(jnp.float32)
    slopes = jnp.asarray(alibi_table(HEADS)).astype(jnp.float32)
    scores = scores - slopes[:, None, None] * distance[None, :, :]
    scores = low_back(scores)
    attention = low(jax.nn.softmax(scores, axis=-1))
    context_vectors = jnp.einsum('shqk,skhe->sqhe', attention, value_heads, precision=MATMUL_PRECISION)
    context_vectors = low_back(low(context_vectors.reshape(seq_count, length, D)))
    attention_output = low_back(jnp.einsum('mjx,xg->mjg', context_vectors, attention_output_weight, precision=MATMUL_PRECISION))
    first_norm = norm_rows(input_batch + attention_output, gain_one, offset_one)
    first_lowered = low(first_norm)
    gated_product = low_back(jnp.einsum('pex,xyn->peyn', first_lowered, gate_up_weight, precision=MATMUL_PRECISION))
    hidden_state = low(jax.nn.gelu(gated_product[:, :, 0], approximate=False) * gated_product[:, :, 1])
    mixed_state = low_back(jnp.einsum('jvp,pb->jvb', hidden_state, down_weight, precision=MATMUL_PRECISION))
    return norm_rows(first_norm + mixed_state, gain_two, offset_two)

def send_block(input_batch, params):
    return low(block_forward(input_batch, params))

def add_pair(total, first_part, second_part):
    return total + jnp.stack([first_part, second_part])

def reference(layer_input, out_grad, loss_mask, query_key_value_weight, attention_output_weight, gate_up_weight, down_weight, norm1_gain, norm1_bias, norm2_gain, norm2_bias):
    weights_all = (query_key_value_weight.astype(jnp.float32), attention_output_weight.astype(jnp.float32), gate_up_weight.astype(jnp.float32), down_weight.astype(jnp.float32), norm1_gain.astype(jnp.float32), norm1_bias.astype(jnp.float32), norm2_gain.astype(jnp.float32), norm2_bias.astype(jnp.float32))
    first_params = tuple((weight_item[0] for weight_item in weights_all))
    second_params = tuple((weight_item[1] for weight_item in weights_all))

    def micro_step(totals, batch_items):
        input_batch, cotangent, selected = batch_items
        start_rows = input_batch.astype(jnp.float32)
        middle, back_first = jax.vjp(send_block, start_rows, first_params)
        final, back_second = jax.vjp(block_forward, middle, second_params)
        seed_grad = cotangent.astype(jnp.float32) * selected.astype(jnp.float32)[..., None]
        middle_grad, second_grads = back_second(seed_grad)
        start_grad, first_grads = back_first(middle_grad)
        totals = jax.tree.map(add_pair, totals, first_grads, second_grads)
        return (totals, (middle.astype(jnp.bfloat16), final.astype(jnp.bfloat16), start_grad, middle_grad))
    zero_totals = tuple((jnp.zeros_like(weight_item) for weight_item in weights_all))
    totals, outputs = lax.scan(micro_step, zero_totals, (layer_input, out_grad, loss_mask))
    middle_out, final_out, start_grads, middle_grads = outputs
    layer_out = jnp.stack([middle_out, final_out])
    input_grad = jnp.stack([start_grads, middle_grads])
    return (layer_out, input_grad, totals[0], totals[1], totals[2], totals[3], totals[4], totals[5], totals[6], totals[7])
```

```python
import math

import jax
import jax.numpy as jnp
import numpy as np
from jax import lax
from jax.sharding import PartitionSpec as P

HEADS = 12
HEAD_DIM = 64
NORM_EPSILON = 1e-05
AXES = ("section", "dp", "tensor")
FEED_CHUNKS = 2

F32 = jnp.float32
BF16 = jnp.bfloat16


def power_slopes(total_heads):
    return [2.0 ** (-8.0 * (index + 1) / total_heads) for index in range(total_heads)]


def alibi_table(number_heads):
    closest = 2 ** int(math.floor(math.log2(number_heads)))
    slopes = power_slopes(closest)
    slopes = slopes + power_slopes(2 * closest)[0::2][: number_heads - closest]
    return np.array(slopes, dtype=np.float32)


def norm_rows(values, gain, offset):
    row_mean = jnp.mean(values, axis=-1, keepdims=True)
    centred = values - row_mean
    row_var = jnp.mean(centred * centred, axis=-1, keepdims=True)
    return centred * lax.rsqrt(row_var + NORM_EPSILON) * gain + offset


def gelu_product(gate_part, up_part):
    return jax.nn.gelu(gate_part, approximate=False) * up_part


def dot(a, b, ca, cb):
    return lax.dot_general(a, b, (((ca,), (cb,)), ((), ())), preferred_element_type=F32)


def exchange(block, section_mask=0, dp_masks=(0, 0), tensor_mask=0):
    dp = lax.axis_size("dp")
    tensor = lax.axis_size("tensor")
    pairs = []
    for s in range(lax.axis_size("section")):
        for d in range(dp):
            for t in range(tensor):
                target = ((s ^ section_mask) * dp + (d ^ dp_masks[s])) * tensor + (t ^ tensor_mask)
                pairs.append(((s * dp + d) * tensor + t, target))
    return lax.ppermute(block, AXES, pairs)


def swap(block):
    return exchange(block, section_mask=1)


FIRST = (1, 2)
SECOND = (2, 1)
PLANE = 4
DEPTH = 4


def gather_pieces(own):
    mine = own[0]
    next_one = exchange(mine, tensor_mask=1)
    next_two = exchange(jnp.stack([mine, next_one]), tensor_mask=2)
    remote = jnp.concatenate([next_one[None], next_two])
    first = exchange(remote, dp_masks=FIRST)
    second = exchange(jnp.stack([remote, first]), dp_masks=SECOND)
    return [[own[0], remote], [own[1], first], [own[2], second[0]], [own[3], second[1]]]


def assemble(pieces):
    return jnp.stack([jnp.concatenate([own[None], rest]) for own, rest in pieces])


def add_low(a, b):
    return (a.astype(F32) + b.astype(F32)).astype(BF16)


def scatter_pieces(terms):
    half = add_low(terms[:2], exchange(terms[2:], dp_masks=SECOND))
    quarter = add_low(half[0], exchange(half[1], dp_masks=FIRST))
    pair = add_low(quarter[:2], exchange(quarter[2:], tensor_mask=2))
    one = add_low(pair[0], exchange(pair[1], tensor_mask=1))
    mask = PLANE
    while mask < lax.axis_size("dp"):
        one = add_low(one, exchange(one, dp_masks=(mask, mask)))
        mask *= 2
    return one


def attention_weights(queries, key_heads, slopes):
    length = queries.shape[1]
    scores = jnp.einsum(
        "sqhe,skhe->shqk", queries, key_heads, preferred_element_type=F32
    ) * HEAD_DIM ** (-0.5)
    positions = jnp.arange(length)
    distance = jnp.abs(positions[:, None] - positions[None, :]).astype(F32)
    scores = scores - slopes[:, None, None] * distance[None, :, :]
    return jax.nn.softmax(scores, axis=-1)


def layer_forward(own_low, attn, feed, norms, slopes, seqs):
    rows, features = own_low.shape
    length = rows // seqs
    gain_one, offset_one, gain_two, offset_two = norms
    own_in = own_low.astype(F32)
    wqkv, wo = attn
    projected = dot(own_low, wqkv, 1, 1).astype(BF16)
    split = projected.reshape(seqs, length, 3, -1, HEAD_DIM)
    queries, key_heads, value_heads = split[:, :, 0], split[:, :, 1], split[:, :, 2]
    attention = attention_weights(queries, key_heads, slopes)
    attention_low = attention.astype(BF16)
    context = jnp.einsum(
        "shqk,skhe->sqhe", attention_low, value_heads, preferred_element_type=F32
    ).astype(BF16).reshape(rows, -1)
    attended = dot(context, wo, 1, 0)
    first_sum = own_in + attended
    first_norm = norm_rows(first_sum, gain_one, offset_one)
    first_low = first_norm.astype(BF16)
    first_all = jnp.concatenate([first_low, swap(first_low)])
    gated, hidden, mixed_terms = [], [], 0.0
    for gate_up, down in feed:
        gated_rows = dot(first_all, gate_up, 1, 1)
        gate_part, up_part = jnp.split(gated_rows, 2, axis=-1)
        hidden_rows = gelu_product(gate_part, up_part).astype(BF16)
        gated.append(gated_rows)
        hidden.append(hidden_rows)
        mixed_terms = mixed_terms + dot(hidden_rows, down, 1, 0)
    mixed = mixed_terms[:rows] + swap(mixed_terms[rows:].astype(BF16)).astype(F32)
    second_sum = first_norm + mixed
    output = norm_rows(second_sum, gain_two, offset_two)
    saved = (queries, key_heads, value_heads, attention, attention_low, context, first_sum, first_all, gated, hidden, second_sum)
    return output, saved


def layer_backward(own_low, seed_grad, attn, feed, norms, saved, seqs):
    queries, key_heads, value_heads, attention, attention_low, context, first_sum, first_all, gated, hidden, second_sum = saved
    rows, features = own_low.shape
    length = rows // seqs
    gain_one, offset_one, gain_two, offset_two = norms
    wqkv, wo = attn
    _, norm_two_back = jax.vjp(norm_rows, second_sum, gain_two, offset_two)
    second_grad, gain_two_grad, offset_two_grad = norm_two_back(seed_grad)
    mixed_low = second_grad.astype(BF16)
    mixed_all = jnp.concatenate([mixed_low, swap(mixed_low)])
    feed_grads, first_terms = [], 0.0
    for (gate_up, down), gated_rows, hidden_rows in zip(feed, gated, hidden):
        hidden_grad = dot(mixed_all, down, 1, 1)
        down_grad = dot(hidden_rows, mixed_all, 0, 0).astype(BF16)
        gate_part, up_part = jnp.split(gated_rows, 2, axis=-1)
        _, gelu_back = jax.vjp(gelu_product, gate_part, up_part)
        gate_grad, up_grad = gelu_back(hidden_grad)
        gated_grad = jnp.concatenate([gate_grad, up_grad], axis=-1).astype(BF16)
        gate_up_grad = dot(gated_grad, first_all, 0, 0).astype(BF16)
        feed_grads.append((gate_up_grad, down_grad))
        first_terms = first_terms + dot(gated_grad, gate_up, 1, 0)
    first_grad = first_terms[:rows] + swap(first_terms[rows:].astype(BF16)).astype(F32) + second_grad
    _, norm_one_back = jax.vjp(norm_rows, first_sum, gain_one, offset_one)
    sum_grad, gain_one_grad, offset_one_grad = norm_one_back(first_grad)
    attended_low = sum_grad.astype(BF16)
    context_grad = dot(attended_low, wo, 1, 1).astype(BF16)
    out_grad = dot(context, attended_low, 0, 0).astype(BF16)
    context_heads = context_grad.reshape(seqs, length, -1, HEAD_DIM)
    weights_grad = jnp.einsum(
        "sqhe,skhe->shqk", context_heads, value_heads, preferred_element_type=F32
    )
    value_grad = jnp.einsum(
        "shqk,sqhe->skhe", attention_low, context_heads, preferred_element_type=F32
    )
    score_grad = attention * (
        weights_grad - jnp.sum(attention * weights_grad, axis=-1, keepdims=True)
    )
    score_grad = score_grad.astype(BF16)
    query_grad = jnp.einsum(
        "shqk,skhe->sqhe", score_grad, key_heads, preferred_element_type=F32
    ) * HEAD_DIM ** (-0.5)
    key_grad = jnp.einsum(
        "shqk,sqhe->skhe", score_grad, queries, preferred_element_type=F32
    ) * HEAD_DIM ** (-0.5)
    projected_grad = jnp.stack([query_grad, key_grad, value_grad], axis=2).reshape(rows, -1).astype(BF16)
    qkv_grad = dot(projected_grad, own_low, 0, 0).astype(BF16)
    input_grad = dot(projected_grad, wqkv, 1, 0) + sum_grad
    vectors = jnp.stack([gain_one_grad, offset_one_grad, gain_two_grad, offset_two_grad])
    return input_grad, feed_grads, (qkv_grad, out_grad), vectors


def body(
    layer_input,
    out_grad,
    loss_mask,
    query_key_value_weight,
    attention_output_weight,
    gate_up_weight,
    down_weight,
    norm1_gain,
    norm1_bias,
    norm2_gain,
    norm2_bias,
):
    core = lax.axis_index("section")
    plane = lax.axis_index("dp")
    depth = lax.axis_index("tensor")
    is_first = core == 0
    micro, own_seqs, length, features = layer_input.shape
    local = query_key_value_weight.shape[-1]
    local_heads = local // HEAD_DIM
    units = down_weight.shape[1]
    part = HEAD_DIM // PLANE
    unit_part = units // 2 // PLANE // FEED_CHUNKS
    seqs = micro * own_seqs // 2
    rows = seqs * length

    steps = jnp.where(is_first, jnp.array([0, 1, 2, 3]), jnp.array([0, 2, 1, 3]))
    in_plane = jnp.bitwise_and(plane, PLANE - 1)

    def relative(slab):
        return [
            lax.dynamic_index_in_dim(slab, jnp.bitwise_xor(in_plane, steps[e]), 0, keepdims=False)
            for e in range(PLANE)
        ]

    qkv_rows = jnp.transpose(query_key_value_weight[0], (1, 2, 0))
    attn_rows = jnp.concatenate([qkv_rows, attention_output_weight], axis=0)
    attn_slab = attn_rows.reshape(2, 2, local_heads, PLANE, part, features)
    attn_slab = jnp.transpose(attn_slab, (0, 3, 1, 2, 4, 5)).reshape(2, PLANE, -1, features)
    gate_up_rows = jnp.transpose(gate_up_weight[0], (1, 2, 0))
    feed_rows = jnp.concatenate([gate_up_rows, down_weight], axis=0)
    feed_slab = feed_rows.reshape(3, 2, FEED_CHUNKS, PLANE, unit_part, features)
    feed_slab = jnp.transpose(feed_slab, (2, 1, 3, 0, 4, 5)).reshape(FEED_CHUNKS, 2, PLANE, -1, features)

    def share(slab):
        keep = lax.dynamic_index_in_dim(slab, core, 0, keepdims=False)
        got = swap(lax.dynamic_index_in_dim(slab, 1 - core, 0, keepdims=False))
        return jnp.where(is_first, keep, got), jnp.where(is_first, got, keep)

    attn_own = share(attn_slab)
    feed_own = [share(feed_slab[k]) for k in range(FEED_CHUNKS)]

    def gather_attn(own):
        full = assemble(gather_pieces(relative(own)))
        full = full.reshape(PLANE, DEPTH, 2, local_heads, part, features)
        mine = jnp.transpose(full, (2, 1, 3, 0, 4, 5)).reshape(2, -1, features)
        other = swap(mine)
        qk = jnp.where(is_first, mine, other)
        vo = jnp.where(is_first, other, mine)
        wqkv = jnp.concatenate([qk.reshape(-1, features), vo[0]])
        return wqkv, vo[1]

    def gather_feed(own):
        full = assemble(gather_pieces(relative(own)))
        full = full.reshape(PLANE * DEPTH, 3, unit_part, features)
        full = jnp.transpose(full, (1, 0, 2, 3)).reshape(3, -1, features)
        return full[:2].reshape(-1, features), full[2]

    attns = []
    feeds = []
    for layer in range(2):
        attns.append(gather_attn(attn_own[layer]))
        feeds.append([gather_feed(feed_own[k][layer]) for k in range(FEED_CHUNKS)])

    norm_table = jnp.concatenate([norm1_gain, norm1_bias, norm2_gain, norm2_bias])
    norm_other = swap(norm_table)
    norm_first = jnp.where(is_first, norm_table, norm_other)
    norm_second = jnp.where(is_first, norm_other, norm_table)
    norms = [tuple(table[i] for i in range(4)) for table in (norm_first, norm_second)]

    slope_table = jnp.asarray(alibi_table(HEADS)).reshape(DEPTH, local_heads)
    slopes = jnp.concatenate(
        [lax.dynamic_index_in_dim(slope_table, jnp.bitwise_xor(depth, j), 0, keepdims=False) for j in range(DEPTH)]
    )

    def own_half(whole):
        flat = whole.reshape((2, rows) + whole.shape[3:])
        return lax.dynamic_index_in_dim(flat, core, 0, keepdims=False)

    start = own_half(layer_input)
    seed = own_half(out_grad).astype(F32) * own_half(loss_mask).astype(F32)[..., None]

    middle, saved_first = layer_forward(start, attns[0], feeds[0], norms[0], slopes, seqs)
    middle_low = middle.astype(BF16)
    final, saved_second = layer_forward(middle_low, attns[1], feeds[1], norms[1], slopes, seqs)
    final_low = final.astype(BF16)

    def reduce_feed(grads):
        gate_up, down = grads
        full = jnp.concatenate([gate_up, down]).reshape(3, PLANE, DEPTH, unit_part, features)
        full = jnp.transpose(full, (1, 2, 0, 3, 4)).reshape(PLANE, DEPTH, -1, features)
        return scatter_pieces(full)

    def reduce_attn(grads):
        qkv, out = grads
        full = jnp.concatenate([qkv, out]).reshape(2, -1, features)
        keep = lax.dynamic_index_in_dim(full, core, 0, keepdims=False)
        got = swap(lax.dynamic_index_in_dim(full, 1 - core, 0, keepdims=False))
        full = add_low(keep, got).reshape(2, DEPTH, local_heads, PLANE, part, features)
        full = jnp.transpose(full, (3, 1, 0, 2, 4, 5)).reshape(PLANE, DEPTH, -1, features)
        return scatter_pieces(full)

    middle_grad, feed_grads, attn_grads, vectors_second = layer_backward(
        middle_low, seed, attns[1], feeds[1], norms[1], saved_second, seqs
    )
    feed_second = [reduce_feed(g) for g in feed_grads]
    attn_second = reduce_attn(attn_grads)
    start_grad, feed_grads, attn_grads, vectors_first = layer_backward(
        start, middle_grad, attns[0], feeds[0], norms[0], saved_first, seqs
    )
    feed_first = [reduce_feed(g) for g in feed_grads]
    attn_first = reduce_attn(attn_grads)

    def finish(first, second):
        keep = jnp.where(is_first, first, second)
        got = swap(jnp.where(is_first, second, first))
        both = jnp.stack([jnp.where(is_first, keep, got), jnp.where(is_first, got, keep)])
        near = exchange(both, dp_masks=FIRST)
        pair = jnp.stack([both, near])
        far = exchange(pair, dp_masks=SECOND)
        every = jnp.concatenate([pair, far])
        return jnp.stack(
            [
                lax.dynamic_index_in_dim(
                    every, steps[jnp.bitwise_xor(in_plane, index)], 0, keepdims=False
                )
                for index in range(PLANE)
            ]
        )

    feed_total = jnp.stack([finish(a, b) for a, b in zip(feed_first, feed_second)])
    feed_total = feed_total.reshape(FEED_CHUNKS, PLANE, 2, 3, unit_part, features)
    feed_total = jnp.transpose(feed_total, (3, 2, 0, 1, 4, 5)).reshape(3, units, features).astype(F32)
    grad_in = jnp.transpose(feed_total[:2], (2, 0, 1))
    grad_down = feed_total[2]
    attn_total = finish(attn_first, attn_second)
    attn_total = attn_total.reshape(PLANE, 2, 2, local_heads, part, features)
    attn_total = jnp.transpose(attn_total, (1, 2, 3, 0, 4, 5)).reshape(4, local, features).astype(F32)
    grad_qkv = jnp.transpose(attn_total[:3], (2, 0, 1))
    grad_out = attn_total[3]

    vectors = lax.psum(jnp.stack([vectors_first, vectors_second]), AXES)
    vectors = lax.dynamic_index_in_dim(vectors, core, 0, keepdims=False)
    vectors = lax.dynamic_slice_in_dim(vectors, depth * local, local, 1)

    def give(first, second):
        mine = jnp.where(is_first, first, second)
        got = swap(jnp.where(is_first, second, first))
        both = jnp.concatenate([jnp.where(is_first, mine, got), jnp.where(is_first, got, mine)])
        return both.reshape((1, micro, own_seqs, length, features))

    return (
        give(middle_low, final_low),
        give(start_grad, middle_grad),
        grad_qkv[None],
        grad_out[None],
        grad_in[None],
        grad_down[None],
        vectors[0][None],
        vectors[1][None],
        vectors[2][None],
        vectors[3][None],
    )


def solution(mesh):
    placed = (
        P(None, ("dp", "tensor"), None, None),
        P(None, ("dp", "tensor"), None, None),
        P(None, ("dp", "tensor"), None),
        P("section", None, None, "tensor"),
        P("section", "tensor", None),
        P("section", None, None, "tensor"),
        P("section", "tensor", None),
        P("section", None),
        P("section", None),
        P("section", None),
        P("section", None),
    )
    return jax.shard_map(
        body,
        mesh=mesh,
        in_specs=placed,
        out_specs=(
            P("section", None, ("dp", "tensor"), None, None),
            P("section", None, ("dp", "tensor"), None, None),
            P("section", None, None, "tensor"),
            P("section", "tensor", None),
            P("section", None, None, "tensor"),
            P("section", "tensor", None),
            P("section", "tensor"),
            P("section", "tensor"),
            P("section", "tensor"),
            P("section", "tensor"),
        ),
        check_vma=False,
    )
```

```python
import functools
import math

import jax
import jax.numpy as jnp
import numpy as np
from jax import lax
from jax.experimental import pallas as pl
from jax.experimental.pallas import tpu as pltpu
from jax.sharding import PartitionSpec as P

HEADS = 12
HEAD_DIM = 64
NORM_EPSILON = 1e-05
AXES = ("section", "dp", "tensor")
FEED_CHUNKS = 2
LANES = 128
GROUP = 3
GROUP_BACK = 3

F32 = jnp.float32
BF16 = jnp.bfloat16


def power_slopes(total_heads):
    return [2.0 ** (-8.0 * (index + 1) / total_heads) for index in range(total_heads)]


def alibi_table(number_heads):
    closest = 2 ** int(math.floor(math.log2(number_heads)))
    slopes = power_slopes(closest)
    slopes = slopes + power_slopes(2 * closest)[0::2][: number_heads - closest]
    return np.array(slopes, dtype=np.float32)


def norm_rows(values, gain, offset):
    row_mean = jnp.mean(values, axis=-1, keepdims=True)
    centred = values - row_mean
    row_var = jnp.mean(centred * centred, axis=-1, keepdims=True)
    return centred * lax.rsqrt(row_var + NORM_EPSILON) * gain + offset


def gelu_product(gate_part, up_part):
    return jax.nn.gelu(gate_part, approximate=False) * up_part


def dot(a, b, ca, cb):
    return lax.dot_general(a, b, (((ca,), (cb,)), ((), ())), preferred_element_type=F32)


def exchange(block, section_mask=0, dp_masks=(0, 0), tensor_mask=0):
    dp = lax.axis_size("dp")
    tensor = lax.axis_size("tensor")
    pairs = []
    for s in range(lax.axis_size("section")):
        for d in range(dp):
            for t in range(tensor):
                target = ((s ^ section_mask) * dp + (d ^ dp_masks[s])) * tensor + (t ^ tensor_mask)
                pairs.append(((s * dp + d) * tensor + t, target))
    return lax.ppermute(block, AXES, pairs)


def swap(block):
    return exchange(block, section_mask=1)


FIRST = (1, 2)
SECOND = (2, 1)
PLANE = 4
DEPTH = 4


def contract(a, b, ca, cb):
    return lax.dot_general(a, b, (((ca,), (cb,)), ((), ())), preferred_element_type=F32)


def head_masks(length):
    lane = lax.broadcasted_iota(jnp.int32, (length, LANES), 1)
    return [lane // HEAD_DIM == index for index in range(LANES // HEAD_DIM)]


def distances(length):
    across = lax.broadcasted_iota(jnp.int32, (length, length), 0)
    along = lax.broadcasted_iota(jnp.int32, (length, length), 1)
    return jnp.abs(across - along).astype(F32)


def attend_kernel(group, slopes_ref, projected_ref, context_ref):
    length, features = context_ref.shape
    masks = head_masks(length)
    distance = distances(length)
    per = len(masks)
    pairs = features // LANES
    for first in range(0, pairs, group):
        heads = [(pair, index) for pair in range(first, first + group) for index in range(per)]
        parts = {p: [slice(i * features + p * LANES, i * features + (p + 1) * LANES) for i in range(3)] for p, _ in heads}
        scores = []
        for pair, index in heads:
            key = projected_ref[:, parts[pair][1]]
            own = jnp.where(masks[index], key, jnp.zeros_like(key))
            scores.append(contract(own, projected_ref[:, parts[pair][0]], 1, 1))
        weights = []
        for (pair, index), score in zip(heads, scores):
            score = score * HEAD_DIM ** (-0.5) - slopes_ref[pair * per + index] * distance
            weight = jnp.exp(score - jnp.max(score, axis=0, keepdims=True))
            weight = weight * (1.0 / jnp.sum(weight, axis=0, keepdims=True))
            weights.append(weight.astype(BF16))
        for pair in range(first, first + group):
            value = projected_ref[:, parts[pair][2]]
            context = jnp.zeros((length, LANES), F32)
            for (other, index), weight in zip(heads, weights):
                if other == pair:
                    context = jnp.where(masks[index], contract(weight, value, 0, 0), context)
            context_ref[:, parts[pair][0]] = context.astype(BF16)


def attend_back_kernel(group, slopes_ref, projected_ref, context_grad_ref, grad_ref):
    length, features = context_grad_ref.shape
    masks = head_masks(length)
    distance = distances(length)
    per = len(masks)
    pairs = features // LANES
    for first in range(0, pairs, group):
        heads = [(pair, index) for pair in range(first, first + group) for index in range(per)]
        parts = {p: [slice(i * features + p * LANES, i * features + (p + 1) * LANES) for i in range(3)] for p, _ in heads}
        scores, weights_grads = [], []
        for pair, index in heads:
            key, value = projected_ref[:, parts[pair][1]], projected_ref[:, parts[pair][2]]
            own = jnp.where(masks[index], key, jnp.zeros_like(key))
            scores.append(contract(own, projected_ref[:, parts[pair][0]], 1, 1))
            own = jnp.where(masks[index], value, jnp.zeros_like(value))
            weights_grads.append(contract(own, context_grad_ref[:, parts[pair][0]], 1, 1))
        weights, score_grads = [], []
        for (pair, index), score, weights_grad in zip(heads, scores, weights_grads):
            score = score * HEAD_DIM ** (-0.5) - slopes_ref[pair * per + index] * distance
            weight = jnp.exp(score - jnp.max(score, axis=0, keepdims=True))
            weight = weight * (1.0 / jnp.sum(weight, axis=0, keepdims=True))
            mean_grad = jnp.sum(weight * weights_grad, axis=0, keepdims=True)
            score_grads.append((weight * (weights_grad - mean_grad)).astype(BF16))
            weights.append(weight.astype(BF16))
        for pair in range(first, first + group):
            query, key = projected_ref[:, parts[pair][0]], projected_ref[:, parts[pair][1]]
            context_grad = context_grad_ref[:, parts[pair][0]]
            grads = [jnp.zeros((length, LANES), F32)] * 3
            for (other, index), weight, score_grad in zip(heads, weights, score_grads):
                if other == pair:
                    new = [
                        contract(score_grad, key, 0, 0) * HEAD_DIM ** (-0.5),
                        contract(score_grad, query, 1, 0) * HEAD_DIM ** (-0.5),
                        contract(weight, context_grad, 1, 0),
                    ]
                    grads = [jnp.where(masks[index], n, g) for n, g in zip(new, grads)]
            for part, grad in zip(parts[pair], grads):
                grad_ref[:, part] = grad.astype(BF16)


def row_block(length, width):
    return pl.BlockSpec((length, width), lambda index: (index, 0))


def attend(projected, slopes, seqs):
    rows, width = projected.shape
    length, features = rows // seqs, width // 3
    return pl.pallas_call(
        functools.partial(attend_kernel, GROUP),
        grid=(seqs,),
        in_specs=[pl.BlockSpec(memory_space=pltpu.SMEM), row_block(length, width)],
        out_specs=row_block(length, features),
        out_shape=jax.ShapeDtypeStruct((rows, features), BF16),
        cost_estimate=pl.CostEstimate(
            flops=4 * rows * length * features, bytes_accessed=2 * rows * (width + features), transcendentals=rows * length * features // HEAD_DIM
        ),
        name="attend",
    )(slopes, projected)


def attend_back(projected, context_grad, slopes, seqs):
    rows, width = projected.shape
    length, features = rows // seqs, width // 3
    return pl.pallas_call(
        functools.partial(attend_back_kernel, GROUP_BACK),
        grid=(seqs,),
        in_specs=[
            pl.BlockSpec(memory_space=pltpu.SMEM),
            row_block(length, width),
            row_block(length, features),
        ],
        out_specs=row_block(length, width),
        out_shape=jax.ShapeDtypeStruct((rows, width), BF16),
        cost_estimate=pl.CostEstimate(
            flops=10 * rows * length * features, bytes_accessed=2 * rows * (2 * width + features), transcendentals=rows * length * features // HEAD_DIM
        ),
        name="attend_back",
    )(slopes, projected, context_grad)


def together(*trees):
    return lax.optimization_barrier(trees)


def near(chunk):
    return dict(chunk, near=exchange(chunk["own"][0], tensor_mask=1))


def far(chunk):
    mine, next_one = chunk["own"][0], chunk["near"]
    next_two = exchange(jnp.stack([mine, next_one]), tensor_mask=2)
    return dict(chunk, remote=jnp.concatenate([next_one[None], next_two]))


def first(chunk):
    return dict(chunk, first=exchange(chunk["remote"], dp_masks=FIRST))


def second(chunk):
    return dict(chunk, second=exchange(jnp.stack([chunk["remote"], chunk["first"]]), dp_masks=SECOND))


def assemble(chunk):
    rest = [chunk["remote"], chunk["first"], chunk["second"][0], chunk["second"][1]]
    return jnp.stack([jnp.concatenate([own[None], r]) for own, r in zip(chunk["own"], rest)])


def add_low(a, b):
    return (a.astype(F32) + b.astype(F32)).astype(BF16)


def reduce_second(terms):
    return add_low(terms[:2], exchange(terms[2:], dp_masks=SECOND))


def reduce_first(terms):
    return add_low(terms[0], exchange(terms[1], dp_masks=FIRST))


def reduce_near(terms):
    pairs = terms.reshape((2, 2) + terms.shape[1:])
    return add_low(pairs[:, 0], exchange(pairs[:, 1], tensor_mask=1))


def reduce_far(terms):
    one = add_low(terms[0], exchange(terms[1], tensor_mask=2))
    mask = PLANE
    while mask < lax.axis_size("dp"):
        one = add_low(one, exchange(one, dp_masks=(mask, mask)))
        mask *= 2
    return one


def attn_forward(own_low, weights, norms, slopes, seqs):
    wqkv, wo = weights
    projected = dot(own_low, wqkv, 1, 1).astype(BF16)
    context = attend(projected, slopes, seqs)
    first_sum = own_low.astype(F32) + dot(context, wo, 1, 0)
    first_norm = norm_rows(first_sum, norms[0], norms[1])
    return projected, context, first_sum, first_norm


def both_rows(rows_low):
    return jnp.concatenate([rows_low, swap(rows_low)])


def join_rows(terms):
    rows = terms.shape[0] // 2
    return terms[:rows] + swap(terms[rows:].astype(BF16)).astype(F32)


def feed_forward(first_all, weights):
    gate_up, down = weights
    gated = dot(first_all, gate_up, 1, 1)
    gate_part, up_part = jnp.split(gated, 2, axis=-1)
    hidden = gelu_product(gate_part, up_part).astype(BF16)
    return gated, hidden, dot(hidden, down, 1, 0)


def feed_backward(mixed_all, first_all, weights, gated, hidden):
    gate_up, down = weights
    hidden_grad = dot(mixed_all, down, 1, 1)
    down_grad = dot(hidden, mixed_all, 0, 0).astype(BF16)
    gate_part, up_part = jnp.split(gated, 2, axis=-1)
    _, gelu_back = jax.vjp(gelu_product, gate_part, up_part)
    gate_grad, up_grad = gelu_back(hidden_grad)
    gated_grad = jnp.concatenate([gate_grad, up_grad], axis=-1).astype(BF16)
    gate_up_grad = dot(gated_grad, first_all, 0, 0).astype(BF16)
    return gate_up_grad, down_grad, dot(gated_grad, gate_up, 1, 0)


def norm_backward(total, gain, offset, grad):
    _, back = jax.vjp(norm_rows, total, gain, offset)
    return back(grad)


def attn_backward(own_low, sum_grad, weights, projected, context, slopes, seqs):
    wqkv, wo = weights
    attended_low = sum_grad.astype(BF16)
    context_grad = dot(attended_low, wo, 1, 1).astype(BF16)
    out_grad = dot(context, attended_low, 0, 0).astype(BF16)
    projected_grad = attend_back(projected, context_grad, slopes, seqs)
    qkv_grad = dot(projected_grad, own_low, 0, 0).astype(BF16)
    return projected_grad, qkv_grad, out_grad


def body(
    layer_input,
    out_grad,
    loss_mask,
    query_key_value_weight,
    attention_output_weight,
    gate_up_weight,
    down_weight,
    norm1_gain,
    norm1_bias,
    norm2_gain,
    norm2_bias,
):
    core = lax.axis_index("section")
    plane = lax.axis_index("dp")
    depth = lax.axis_index("tensor")
    is_first = core == 0
    micro, own_seqs, length, features = layer_input.shape
    local = query_key_value_weight.shape[-1]
    local_heads = local // HEAD_DIM
    units = down_weight.shape[1]
    part = HEAD_DIM // PLANE
    unit_part = units // 2 // PLANE // FEED_CHUNKS
    seqs = micro * own_seqs // 2
    rows = seqs * length

    orders = [jnp.array([0, 1, 2, 3]), jnp.array([0, 2, 1, 3])]
    steps = jnp.where(is_first, orders[0], orders[1])
    in_plane = jnp.bitwise_and(plane, PLANE - 1)

    def relative(slab):
        return [
            lax.dynamic_index_in_dim(slab, jnp.bitwise_xor(in_plane, steps[e]), 0, keepdims=False)
            for e in range(PLANE)
        ]

    qkv_rows = jnp.transpose(query_key_value_weight[0], (1, 2, 0))
    attn_rows = jnp.concatenate([qkv_rows, attention_output_weight], axis=0)
    attn_slab = attn_rows.reshape(2, 2, local_heads, PLANE, part, features)
    attn_slab = jnp.transpose(attn_slab, (0, 3, 1, 2, 4, 5)).reshape(2, PLANE, -1, features)
    gate_up_rows = jnp.transpose(gate_up_weight[0], (1, 2, 0))
    feed_rows = jnp.concatenate([gate_up_rows, down_weight], axis=0)
    feed_slab = feed_rows.reshape(3, 2, FEED_CHUNKS, PLANE, unit_part, features)
    feed_slab = jnp.transpose(feed_slab, (2, 1, 3, 0, 4, 5)).reshape(FEED_CHUNKS, 2, PLANE, -1, features)

    def share(slab):
        keep = lax.dynamic_index_in_dim(slab, core, 0, keepdims=False)
        got = swap(lax.dynamic_index_in_dim(slab, 1 - core, 0, keepdims=False))
        return jnp.where(is_first, keep, got), jnp.where(is_first, got, keep)

    attn_in = [{"own": relative(own)} for own in share(attn_slab)]
    feed_in = [[{"own": relative(own)} for own in share(feed_slab[k])] for k in range(FEED_CHUNKS)]
    a0, a1 = attn_in
    (p0, p1), (q0, q1) = feed_in


    norm_table = jnp.concatenate([norm1_gain, norm1_bias, norm2_gain, norm2_bias])
    norm_other = swap(norm_table)
    norm_first = jnp.where(is_first, norm_table, norm_other)
    norm_second = jnp.where(is_first, norm_other, norm_table)
    norms = [tuple(table[i] for i in range(4)) for table in (norm_first, norm_second)]

    slope_table = jnp.asarray(alibi_table(HEADS)).reshape(DEPTH, local_heads)
    slopes = jnp.concatenate(
        [lax.dynamic_index_in_dim(slope_table, jnp.bitwise_xor(depth, j), 0, keepdims=False) for j in range(DEPTH)]
    )

    def own_half(whole):
        flat = whole.reshape((2, rows) + whole.shape[3:])
        return lax.dynamic_index_in_dim(flat, core, 0, keepdims=False)

    start = own_half(layer_input)
    seed = own_half(out_grad).astype(F32) * own_half(loss_mask).astype(F32)[..., None]


    def attn_weights(chunk):
        full = assemble(chunk).reshape(PLANE, DEPTH, 2, local_heads, part, features)
        mine = jnp.transpose(full, (2, 1, 3, 0, 4, 5)).reshape(2, -1, features)
        other = swap(mine)
        qk = jnp.where(is_first, mine, other)
        vo = jnp.where(is_first, other, mine)
        wqkv = jnp.concatenate([qk.reshape(-1, features), vo[0]])
        return wqkv, vo[1]

    def feed_weights(chunk):
        full = assemble(chunk).reshape(PLANE * DEPTH, 3, unit_part, features)
        full = jnp.transpose(full, (1, 0, 2, 3)).reshape(3, -1, features)
        return full[:2].reshape(-1, features), full[2]

    a0 = near(a0)
    a0, p0 = together(a0, p0)
    a0, p0 = far(a0), near(p0)
    a0, p0, q0 = together(a0, p0, q0)
    a0, p0, q0 = first(a0), far(p0), near(q0)
    a0, p0, q0, a1 = together(a0, p0, q0, a1)
    a0, p0, q0, a1 = second(a0), first(p0), far(q0), near(a1)
    attn0 = attn_weights(a0)
    p0, q0, a1, p1 = together(p0, q0, a1, p1)
    p0, q0, a1, p1 = second(p0), first(q0), far(a1), near(p1)
    projected0, context0, sum0, norm0 = attn_forward(start, attn0, norms[0], slopes, seqs)
    all0 = both_rows(norm0.astype(BF16))
    all0, p0, q0, a1, p1, q1 = together(all0, p0, q0, a1, p1, q1)
    q0, a1, p1, q1 = second(q0), first(a1), far(p1), near(q1)
    feed_p0 = feed_weights(p0)
    gated_p0, hidden_p0, mixed = feed_forward(all0, feed_p0)
    mixed, q0, a1, p1, q1 = together(mixed, q0, a1, p1, q1)
    a1, p1, q1 = second(a1), first(p1), far(q1)
    feed_q0 = feed_weights(q0)
    gated_q0, hidden_q0, more = feed_forward(all0, feed_q0)
    mixed = mixed + more
    mixed, a1, p1, q1 = together(mixed, a1, p1, q1)
    p1, q1 = second(p1), first(q1)
    attn1 = attn_weights(a1)
    total0 = norm0 + join_rows(mixed)
    middle_low = norm_rows(total0, norms[0][2], norms[0][3]).astype(BF16)
    projected1, context1, sum1, norm1 = attn_forward(middle_low, attn1, norms[1], slopes, seqs)
    all1 = both_rows(norm1.astype(BF16))
    all1, p1, q1 = together(all1, p1, q1)
    q1 = second(q1)
    feed_p1 = feed_weights(p1)
    gated_p1, hidden_p1, mixed = feed_forward(all1, feed_p1)
    mixed, q1 = together(mixed, q1)
    feed_q1 = feed_weights(q1)
    gated_q1, hidden_q1, more = feed_forward(all1, feed_q1)
    total1 = norm1 + join_rows(mixed + more)
    final_low = norm_rows(total1, norms[1][2], norms[1][3]).astype(BF16)

    def give(early, late):
        mine = jnp.where(is_first, early, late)
        got = swap(jnp.where(is_first, late, early))
        both = jnp.concatenate([jnp.where(is_first, mine, got), jnp.where(is_first, got, mine)])
        return both.reshape((1, micro, own_seqs, length, features))

    def feed_terms(gate_up, down):
        full = jnp.concatenate([gate_up, down]).reshape(3, PLANE, DEPTH, unit_part, features)
        return jnp.transpose(full, (1, 2, 0, 3, 4)).reshape(PLANE, DEPTH, -1, features)

    def attn_terms(qkv, out):
        full = jnp.concatenate([qkv, out]).reshape(2, -1, features)
        keep = lax.dynamic_index_in_dim(full, core, 0, keepdims=False)
        got = swap(lax.dynamic_index_in_dim(full, 1 - core, 0, keepdims=False))
        full = add_low(keep, got).reshape(2, DEPTH, local_heads, PLANE, part, features)
        return jnp.transpose(full, (3, 1, 0, 2, 4, 5)).reshape(PLANE, DEPTH, -1, features)

    def spread_first(pieces):
        one = jnp.concatenate(pieces)
        return jnp.stack([one, exchange(one, dp_masks=FIRST)])

    def spread_second(pair):
        return jnp.concatenate([pair, exchange(pair, dp_masks=SECOND)])

    second_grad, gain_two1, offset_two1 = norm_backward(total1, norms[1][2], norms[1][3], seed)
    mixed_all = both_rows(second_grad.astype(BF16))
    gate_up, down, terms = feed_backward(mixed_all, all1, feed_p1, gated_p1, hidden_p1)
    p1 = feed_terms(gate_up, down)
    p1, terms = together(p1, terms)
    p1 = reduce_second(p1)
    gate_up, down, more = feed_backward(mixed_all, all1, feed_q1, gated_q1, hidden_q1)
    q1 = feed_terms(gate_up, down)
    terms = terms + more
    terms, p1, q1 = together(terms, p1, q1)
    p1, q1 = reduce_first(p1), reduce_second(q1)
    first_grad = join_rows(terms) + second_grad
    sum_grad, gain_one1, offset_one1 = norm_backward(sum1, norms[1][0], norms[1][1], first_grad)
    projected_grad, qkv, out = attn_backward(middle_low, sum_grad, attn1, projected1, context1, slopes, seqs)
    a1 = attn_terms(qkv, out)
    layer_out = give(middle_low, final_low)
    projected_grad, a1, p1, q1, layer_out = together(projected_grad, a1, p1, q1, layer_out)
    a1, p1, q1 = reduce_second(a1), reduce_near(p1), reduce_first(q1)
    middle_grad = dot(projected_grad, attn1[0], 1, 0) + sum_grad
    second_grad, gain_two0, offset_two0 = norm_backward(total0, norms[0][2], norms[0][3], middle_grad)
    mixed_all = both_rows(second_grad.astype(BF16))
    gate_up, down, terms = feed_backward(mixed_all, all0, feed_p0, gated_p0, hidden_p0)
    p0 = feed_terms(gate_up, down)
    terms, a1, p1, q1, p0 = together(terms, a1, p1, q1, p0)
    a1, p1, q1, p0 = reduce_first(a1), reduce_far(p1), reduce_near(q1), reduce_second(p0)
    gate_up, down, more = feed_backward(mixed_all, all0, feed_q0, gated_q0, hidden_q0)
    q0 = feed_terms(gate_up, down)
    terms = terms + more
    terms, a1, p1, q1, p0, q0 = together(terms, a1, p1, q1, p0, q0)
    a1, q1, p0, q0 = reduce_near(a1), reduce_far(q1), reduce_first(p0), reduce_second(q0)
    first_grad = join_rows(terms) + second_grad
    sum_grad, gain_one0, offset_one0 = norm_backward(sum0, norms[0][0], norms[0][1], first_grad)
    vectors = jnp.stack(
        [gain_one0, offset_one0, gain_two0, offset_two0, gain_one1, offset_one1, gain_two1, offset_two1]
    )
    projected_grad, qkv, out = attn_backward(start, sum_grad, attn0, projected0, context0, slopes, seqs)
    a0 = attn_terms(qkv, out)
    projected_grad, a0, a1, q1, p0, q0, vectors = together(projected_grad, a0, a1, q1, p0, q0, vectors)
    a0, a1, p0, q0 = reduce_second(a0), reduce_far(a1), reduce_near(p0), reduce_first(q0)
    vectors = vectors + swap(vectors)
    start_grad = dot(projected_grad, attn0[0], 1, 0) + sum_grad
    input_grad = give(start_grad, middle_grad)
    input_grad, a0, a1, p0, q0, vectors = together(input_grad, a0, a1, p0, q0, vectors)
    a0, p0, q0 = reduce_first(a0), reduce_far(p0), reduce_near(q0)
    late = spread_first([p1, q1, a1])
    mask = 1
    while mask < lax.axis_size("dp"):
        vectors = vectors + exchange(vectors, dp_masks=(mask, mask))
        mask *= 2
    a0, p0, q0, late, vectors = together(a0, p0, q0, late, vectors)
    a0, q0 = reduce_near(a0), reduce_far(q0)
    late = spread_second(late)
    mask = 1
    while mask < lax.axis_size("tensor"):
        vectors = vectors + exchange(vectors, tensor_mask=mask)
        mask *= 2
    a0, p0, q0, late, vectors = together(a0, p0, q0, late, vectors)
    a0 = reduce_far(a0)
    feed_early = spread_second(spread_first([p0, q0]))
    attn_early = spread_second(spread_first([a0]))
    early = jnp.concatenate([feed_early, attn_early], axis=1)

    mine = jnp.where(is_first, early, late)
    got = swap(jnp.where(is_first, late, early))
    halves = [jnp.where(is_first, mine, got), jnp.where(is_first, got, mine)]
    both = jnp.stack(
        [
            jnp.stack(
                [
                    lax.dynamic_index_in_dim(half, order[jnp.bitwise_xor(in_plane, index)], 0, keepdims=False)
                    for half, order in zip(halves, orders)
                ]
            )
            for index in range(PLANE)
        ]
    )
    feed_rows = FEED_CHUNKS * 3 * unit_part
    feed_total = both[:, :, :feed_rows].reshape(PLANE, 2, FEED_CHUNKS, 3, unit_part, features)
    feed_total = jnp.transpose(feed_total, (3, 1, 2, 0, 4, 5)).reshape(3, units, features).astype(F32)
    grad_in = jnp.transpose(feed_total[:2], (2, 0, 1))
    grad_down = feed_total[2]
    attn_total = both[:, :, feed_rows:].reshape(PLANE, 2, 2, local_heads, part, features)
    attn_total = jnp.transpose(attn_total, (1, 2, 3, 0, 4, 5)).reshape(4, local, features).astype(F32)
    grad_qkv = jnp.transpose(attn_total[:3], (2, 0, 1))
    grad_out = attn_total[3]

    vectors = lax.dynamic_index_in_dim(vectors.reshape(2, 4, features), core, 0, keepdims=False)
    vectors = lax.dynamic_slice_in_dim(vectors, depth * local, local, 1)

    return (
        layer_out,
        input_grad,
        grad_qkv[None],
        grad_out[None],
        grad_in[None],
        grad_down[None],
        vectors[0][None],
        vectors[1][None],
        vectors[2][None],
        vectors[3][None],
    )


def solution(mesh):
    placed = (
        P(None, ("dp", "tensor"), None, None),
        P(None, ("dp", "tensor"), None, None),
        P(None, ("dp", "tensor"), None),
        P("section", None, None, "tensor"),
        P("section", "tensor", None),
        P("section", None, None, "tensor"),
        P("section", "tensor", None),
        P("section", None),
        P("section", None),
        P("section", None),
        P("section", None),
    )
    return jax.shard_map(
        body,
        mesh=mesh,
        in_specs=placed,
        out_specs=(
            P("section", None, ("dp", "tensor"), None, None),
            P("section", None, ("dp", "tensor"), None, None),
            P("section", None, None, "tensor"),
            P("section", "tensor", None),
            P("section", None, None, "tensor"),
            P("section", "tensor", None),
            P("section", "tensor"),
            P("section", "tensor"),
            P("section", "tensor"),
            P("section", "tensor"),
        ),
        check_vma=False,
    )
```

```python
import functools
import math

import jax
import jax.numpy as jnp
import numpy as np
from jax import lax
from jax.experimental import pallas as pl
from jax.experimental.pallas import tpu as pltpu
from jax.sharding import PartitionSpec as P

HEADS = 12
HEAD_DIM = 64
NORM_EPSILON = 1e-05
AXES = ("section", "dp", "tensor")
FEED_CHUNKS = 2
LANES = 128
GROUP = 3
GROUP_BACK = 3

F32 = jnp.float32
BF16 = jnp.bfloat16


def power_slopes(total_heads):
    return [2.0 ** (-8.0 * (index + 1) / total_heads) for index in range(total_heads)]


def alibi_table(number_heads):
    closest = 2 ** int(math.floor(math.log2(number_heads)))
    slopes = power_slopes(closest)
    slopes = slopes + power_slopes(2 * closest)[0::2][: number_heads - closest]
    return np.array(slopes, dtype=np.float32)


def norm_rows(values, gain, offset):
    row_mean = jnp.mean(values, axis=-1, keepdims=True)
    centred = values - row_mean
    row_var = jnp.mean(centred * centred, axis=-1, keepdims=True)
    return centred * lax.rsqrt(row_var + NORM_EPSILON) * gain + offset


def gelu_product(gate_part, up_part):
    return jax.nn.gelu(gate_part, approximate=False) * up_part


def dot(a, b, ca, cb):
    return lax.dot_general(a, b, (((ca,), (cb,)), ((), ())), preferred_element_type=F32)


def exchange(block, section_mask=0, dp_masks=(0, 0), tensor_mask=0):
    dp = lax.axis_size("dp")
    tensor = lax.axis_size("tensor")
    pairs = []
    for s in range(lax.axis_size("section")):
        for d in range(dp):
            for t in range(tensor):
                target = ((s ^ section_mask) * dp + (d ^ dp_masks[s])) * tensor + (t ^ tensor_mask)
                pairs.append(((s * dp + d) * tensor + t, target))
    return lax.ppermute(block, AXES, pairs)


def swap(block):
    return exchange(block, section_mask=1)


FIRST = (1, 2)
SECOND = (2, 1)
PLANE = 4
DEPTH = 4


def contract(a, b, ca, cb):
    return lax.dot_general(a, b, (((ca,), (cb,)), ((), ())), preferred_element_type=F32)


def head_masks(length):
    lane = lax.broadcasted_iota(jnp.int32, (length, LANES), 1)
    return [lane // HEAD_DIM == index for index in range(LANES // HEAD_DIM)]


def distances(length):
    across = lax.broadcasted_iota(jnp.int32, (length, length), 0)
    along = lax.broadcasted_iota(jnp.int32, (length, length), 1)
    return jnp.abs(across - along).astype(F32)


def attend_kernel(group, slopes_ref, projected_ref, context_ref):
    length, features = context_ref.shape
    masks = head_masks(length)
    distance = distances(length)
    per = len(masks)
    pairs = features // LANES
    for first in range(0, pairs, group):
        heads = [(pair, index) for pair in range(first, first + group) for index in range(per)]
        parts = {p: [slice(i * features + p * LANES, i * features + (p + 1) * LANES) for i in range(3)] for p, _ in heads}
        scores = []
        for pair, index in heads:
            key = projected_ref[:, parts[pair][1]]
            own = jnp.where(masks[index], key, jnp.zeros_like(key))
            scores.append(contract(own, projected_ref[:, parts[pair][0]], 1, 1))
        weights = []
        for (pair, index), score in zip(heads, scores):
            score = score * HEAD_DIM ** (-0.5) - slopes_ref[pair * per + index] * distance
            weight = jnp.exp(score - jnp.max(score, axis=0, keepdims=True))
            weight = weight * (1.0 / jnp.sum(weight, axis=0, keepdims=True))
            weights.append(weight.astype(BF16))
        for pair in range(first, first + group):
            value = projected_ref[:, parts[pair][2]]
            context = jnp.zeros((length, LANES), F32)
            for (other, index), weight in zip(heads, weights):
                if other == pair:
                    context = jnp.where(masks[index], contract(weight, value, 0, 0), context)
            context_ref[:, parts[pair][0]] = context.astype(BF16)


def attend_back_kernel(group, slopes_ref, projected_ref, context_grad_ref, grad_ref):
    length, features = context_grad_ref.shape
    masks = head_masks(length)
    distance = distances(length)
    per = len(masks)
    pairs = features // LANES
    for first in range(0, pairs, group):
        heads = [(pair, index) for pair in range(first, first + group) for index in range(per)]
        parts = {p: [slice(i * features + p * LANES, i * features + (p + 1) * LANES) for i in range(3)] for p, _ in heads}
        scores, weights_grads = [], []
        for pair, index in heads:
            key, value = projected_ref[:, parts[pair][1]], projected_ref[:, parts[pair][2]]
            own = jnp.where(masks[index], key, jnp.zeros_like(key))
            scores.append(contract(own, projected_ref[:, parts[pair][0]], 1, 1))
            own = jnp.where(masks[index], value, jnp.zeros_like(value))
            weights_grads.append(contract(own, context_grad_ref[:, parts[pair][0]], 1, 1))
        weights, score_grads = [], []
        for (pair, index), score, weights_grad in zip(heads, scores, weights_grads):
            score = score * HEAD_DIM ** (-0.5) - slopes_ref[pair * per + index] * distance
            weight = jnp.exp(score - jnp.max(score, axis=0, keepdims=True))
            weight = weight * (1.0 / jnp.sum(weight, axis=0, keepdims=True))
            mean_grad = jnp.sum(weight * weights_grad, axis=0, keepdims=True)
            score_grads.append((weight * (weights_grad - mean_grad)).astype(BF16))
            weights.append(weight.astype(BF16))
        for pair in range(first, first + group):
            query, key = projected_ref[:, parts[pair][0]], projected_ref[:, parts[pair][1]]
            context_grad = context_grad_ref[:, parts[pair][0]]
            grads = [jnp.zeros((length, LANES), F32)] * 3
            for (other, index), weight, score_grad in zip(heads, weights, score_grads):
                if other == pair:
                    new = [
                        contract(score_grad, key, 0, 0) * HEAD_DIM ** (-0.5),
                        contract(score_grad, query, 1, 0) * HEAD_DIM ** (-0.5),
                        contract(weight, context_grad, 1, 0),
                    ]
                    grads = [jnp.where(masks[index], n, g) for n, g in zip(new, grads)]
            for part, grad in zip(parts[pair], grads):
                grad_ref[:, part] = grad.astype(BF16)


def row_block(length, width):
    return pl.BlockSpec((length, width), lambda index: (index, 0))


def attend(projected, slopes, seqs):
    rows, width = projected.shape
    length, features = rows // seqs, width // 3
    return pl.pallas_call(
        functools.partial(attend_kernel, GROUP),
        grid=(seqs,),
        in_specs=[pl.BlockSpec(memory_space=pltpu.SMEM), row_block(length, width)],
        out_specs=row_block(length, features),
        out_shape=jax.ShapeDtypeStruct((rows, features), BF16),
        cost_estimate=pl.CostEstimate(
            flops=4 * rows * length * features, bytes_accessed=2 * rows * (width + features), transcendentals=rows * length * features // HEAD_DIM
        ),
        name="attend",
    )(slopes, projected)


def attend_back(projected, context_grad, slopes, seqs):
    rows, width = projected.shape
    length, features = rows // seqs, width // 3
    return pl.pallas_call(
        functools.partial(attend_back_kernel, GROUP_BACK),
        grid=(seqs,),
        in_specs=[
            pl.BlockSpec(memory_space=pltpu.SMEM),
            row_block(length, width),
            row_block(length, features),
        ],
        out_specs=row_block(length, width),
        out_shape=jax.ShapeDtypeStruct((rows, width), BF16),
        cost_estimate=pl.CostEstimate(
            flops=10 * rows * length * features, bytes_accessed=2 * rows * (2 * width + features), transcendentals=rows * length * features // HEAD_DIM
        ),
        name="attend_back",
    )(slopes, projected, context_grad)


def together(*trees):
    return lax.optimization_barrier(trees)


def near(chunk):
    return dict(chunk, near=exchange(chunk["own"][0], tensor_mask=1))


def far(chunk):
    mine, next_one = chunk["own"][0], chunk["near"]
    next_two = exchange(jnp.stack([mine, next_one]), tensor_mask=2)
    return dict(chunk, remote=jnp.concatenate([next_one[None], next_two]))


def first(chunk):
    return dict(chunk, first=exchange(chunk["remote"], dp_masks=FIRST))


def second(chunk):
    return dict(chunk, second=exchange(jnp.stack([chunk["remote"], chunk["first"]]), dp_masks=SECOND))


def assemble(chunk):
    rest = [chunk["remote"], chunk["first"], chunk["second"][0], chunk["second"][1]]
    return jnp.stack([jnp.concatenate([own[None], r]) for own, r in zip(chunk["own"], rest)])


def add_low(a, b):
    return (a.astype(F32) + b.astype(F32)).astype(BF16)


def reduce_second(terms):
    return add_low(terms[:2], exchange(terms[2:], dp_masks=SECOND))


def reduce_first(terms):
    return add_low(terms[0], exchange(terms[1], dp_masks=FIRST))


def reduce_near(terms):
    pairs = terms.reshape((2, 2) + terms.shape[1:])
    return add_low(pairs[:, 0], exchange(pairs[:, 1], tensor_mask=1))


def reduce_far(terms):
    one = add_low(terms[0], exchange(terms[1], tensor_mask=2))
    mask = PLANE
    while mask < lax.axis_size("dp"):
        one = add_low(one, exchange(one, dp_masks=(mask, mask)))
        mask *= 2
    return one


def attn_forward(own_low, weights, norms, slopes, seqs):
    wqkv, wo = weights
    projected = dot(own_low, wqkv, 1, 1).astype(BF16)
    context = attend(projected, slopes, seqs)
    first_sum = own_low.astype(F32) + dot(context, wo, 1, 0)
    first_norm = norm_rows(first_sum, norms[0], norms[1])
    return projected, context, first_sum, first_norm


def both_rows(rows_low):
    return jnp.concatenate([rows_low, swap(rows_low)])


def join_rows(terms):
    rows = terms.shape[0] // 2
    return terms[:rows] + swap(terms[rows:].astype(BF16)).astype(F32)


def feed_forward(first_all, weights):
    gate_up, down = weights
    gated = dot(first_all, gate_up, 1, 1)
    gate_part, up_part = jnp.split(gated, 2, axis=-1)
    hidden = gelu_product(gate_part, up_part).astype(BF16)
    return gated, hidden, dot(hidden, down, 1, 0)


def feed_backward(mixed_all, first_all, weights, gated, hidden):
    gate_up, down = weights
    hidden_grad = dot(mixed_all, down, 1, 1)
    down_grad = dot(hidden, mixed_all, 0, 0).astype(BF16)
    gate_part, up_part = jnp.split(gated, 2, axis=-1)
    _, gelu_back = jax.vjp(gelu_product, gate_part, up_part)
    gate_grad, up_grad = gelu_back(hidden_grad)
    gated_grad = jnp.concatenate([gate_grad, up_grad], axis=-1).astype(BF16)
    gate_up_grad = dot(gated_grad, first_all, 0, 0).astype(BF16)
    return gate_up_grad, down_grad, dot(gated_grad, gate_up, 1, 0)


def norm_backward(total, gain, offset, grad):
    _, back = jax.vjp(norm_rows, total, gain, offset)
    return back(grad)


def attn_backward(own_low, sum_grad, weights, projected, context, slopes, seqs):
    wqkv, wo = weights
    attended_low = sum_grad.astype(BF16)
    context_grad = dot(attended_low, wo, 1, 1).astype(BF16)
    out_grad = dot(context, attended_low, 0, 0).astype(BF16)
    projected_grad = attend_back(projected, context_grad, slopes, seqs)
    qkv_grad = dot(projected_grad, own_low, 0, 0).astype(BF16)
    return projected_grad, qkv_grad, out_grad


def body(
    layer_input,
    out_grad,
    loss_mask,
    query_key_value_weight,
    attention_output_weight,
    gate_up_weight,
    down_weight,
    norm1_gain,
    norm1_bias,
    norm2_gain,
    norm2_bias,
):
    core = lax.axis_index("section")
    plane = lax.axis_index("dp")
    depth = lax.axis_index("tensor")
    is_first = core == 0
    micro, own_seqs, length, features = layer_input.shape
    local = query_key_value_weight.shape[-1]
    local_heads = local // HEAD_DIM
    units = down_weight.shape[1]
    part = HEAD_DIM // PLANE
    unit_part = units // 2 // PLANE // FEED_CHUNKS
    seqs = micro * own_seqs // 2
    rows = seqs * length

    orders = [jnp.array([0, 1, 2, 3]), jnp.array([0, 2, 1, 3])]
    steps = jnp.where(is_first, orders[0], orders[1])
    in_plane = jnp.bitwise_and(plane, PLANE - 1)

    def relative(slab):
        return [
            lax.dynamic_index_in_dim(slab, jnp.bitwise_xor(in_plane, steps[e]), 0, keepdims=False)
            for e in range(PLANE)
        ]

    qkv_rows = jnp.transpose(query_key_value_weight[0], (1, 2, 0))
    attn_rows = jnp.concatenate([qkv_rows, attention_output_weight], axis=0)
    attn_slab = attn_rows.reshape(2, 2, local_heads, PLANE, part, features)
    attn_slab = jnp.transpose(attn_slab, (0, 3, 1, 2, 4, 5)).reshape(2, PLANE, -1, features)
    gate_up_rows = jnp.transpose(gate_up_weight[0], (1, 2, 0))
    feed_rows = jnp.concatenate([gate_up_rows, down_weight], axis=0)
    feed_slab = feed_rows.reshape(3, 2, FEED_CHUNKS, PLANE, unit_part, features)
    feed_slab = jnp.transpose(feed_slab, (2, 1, 3, 0, 4, 5)).reshape(FEED_CHUNKS, 2, PLANE, -1, features)

    def share(slab):
        keep = lax.dynamic_index_in_dim(slab, core, 0, keepdims=False)
        got = swap(lax.dynamic_index_in_dim(slab, 1 - core, 0, keepdims=False))
        return jnp.where(is_first, keep, got), jnp.where(is_first, got, keep)

    attn_in = [{"own": relative(own)} for own in share(attn_slab)]
    feed_in = [[{"own": relative(own)} for own in share(feed_slab[k])] for k in range(FEED_CHUNKS)]
    a0, a1 = attn_in
    (p0, p1), (q0, q1) = feed_in


    norm_table = jnp.concatenate([norm1_gain, norm1_bias, norm2_gain, norm2_bias])
    norm_other = swap(norm_table)
    norm_first = jnp.where(is_first, norm_table, norm_other)
    norm_second = jnp.where(is_first, norm_other, norm_table)
    norms = [tuple(table[i] for i in range(4)) for table in (norm_first, norm_second)]

    slope_table = jnp.asarray(alibi_table(HEADS)).reshape(DEPTH, local_heads)
    slopes = jnp.concatenate(
        [lax.dynamic_index_in_dim(slope_table, jnp.bitwise_xor(depth, j), 0, keepdims=False) for j in range(DEPTH)]
    )

    def own_half(whole):
        flat = whole.reshape((2, rows) + whole.shape[3:])
        return lax.dynamic_index_in_dim(flat, core, 0, keepdims=False)

    start = own_half(layer_input)
    seed = own_half(out_grad).astype(F32) * own_half(loss_mask).astype(F32)[..., None]


    def attn_weights(chunk):
        full = assemble(chunk).reshape(PLANE, DEPTH, 2, local_heads, part, features)
        mine = jnp.transpose(full, (2, 1, 3, 0, 4, 5)).reshape(2, -1, features)
        other = swap(mine)
        qk = jnp.where(is_first, mine, other)
        vo = jnp.where(is_first, other, mine)
        wqkv = jnp.concatenate([qk.reshape(-1, features), vo[0]])
        return wqkv, vo[1]

    def feed_weights(chunk):
        full = assemble(chunk).reshape(PLANE * DEPTH, 3, unit_part, features)
        full = jnp.transpose(full, (1, 0, 2, 3)).reshape(3, -1, features)
        return full[:2].reshape(-1, features), full[2]

    a0 = near(a0)
    a0, p0 = together(a0, p0)
    a0, p0 = far(a0), near(p0)
    a0, p0, q0 = together(a0, p0, q0)
    a0, p0, q0 = first(a0), far(p0), near(q0)
    a0, p0, q0, a1 = together(a0, p0, q0, a1)
    a0, p0, q0, a1 = second(a0), first(p0), far(q0), near(a1)
    a0, p0, q0, a1, p1 = together(a0, p0, q0, a1, p1)
    p0, q0, a1, p1 = second(p0), first(q0), far(a1), near(p1)
    attn0 = attn_weights(a0)
    projected0, context0, sum0, norm0 = attn_forward(start, attn0, norms[0], slopes, seqs)
    low0, p0, q0, a1, p1, q1 = together(norm0.astype(BF16), p0, q0, a1, p1, q1)
    q0, a1, p1, q1 = second(q0), first(a1), far(p1), near(q1)
    all0 = both_rows(low0)
    feed_p0 = feed_weights(p0)
    gated_p0, hidden_p0, mixed = feed_forward(all0, feed_p0)
    mixed, q0, a1, p1, q1 = together(mixed, q0, a1, p1, q1)
    a1, p1, q1 = second(a1), first(p1), far(q1)
    feed_q0 = feed_weights(q0)
    gated_q0, hidden_q0, more = feed_forward(all0, feed_q0)
    mixed = mixed + more
    mixed, a1, p1, q1 = together(mixed, a1, p1, q1)
    p1, q1 = second(p1), first(q1)
    attn1 = attn_weights(a1)
    total0 = norm0 + join_rows(mixed)
    middle_low = norm_rows(total0, norms[0][2], norms[0][3]).astype(BF16)
    projected1, context1, sum1, norm1 = attn_forward(middle_low, attn1, norms[1], slopes, seqs)
    low1, p1, q1 = together(norm1.astype(BF16), p1, q1)
    q1 = second(q1)
    all1 = both_rows(low1)
    feed_p1 = feed_weights(p1)
    gated_p1, hidden_p1, mixed = feed_forward(all1, feed_p1)
    mixed, q1 = together(mixed, q1)
    feed_q1 = feed_weights(q1)
    gated_q1, hidden_q1, more = feed_forward(all1, feed_q1)
    total1 = norm1 + join_rows(mixed + more)
    final_low = norm_rows(total1, norms[1][2], norms[1][3]).astype(BF16)

    def give(early, late):
        mine = jnp.where(is_first, early, late)
        got = swap(jnp.where(is_first, late, early))
        both = jnp.concatenate([jnp.where(is_first, mine, got), jnp.where(is_first, got, mine)])
        return both.reshape((1, micro, own_seqs, length, features))

    def feed_terms(gate_up, down):
        full = jnp.concatenate([gate_up, down]).reshape(3, PLANE, DEPTH, unit_part, features)
        return jnp.transpose(full, (1, 2, 0, 3, 4)).reshape(PLANE, DEPTH, -1, features)

    def attn_terms(qkv, out):
        full = jnp.concatenate([qkv, out]).reshape(2, -1, features)
        keep = lax.dynamic_index_in_dim(full, core, 0, keepdims=False)
        got = swap(lax.dynamic_index_in_dim(full, 1 - core, 0, keepdims=False))
        full = add_low(keep, got).reshape(2, DEPTH, local_heads, PLANE, part, features)
        return jnp.transpose(full, (3, 1, 0, 2, 4, 5)).reshape(PLANE, DEPTH, -1, features)

    def hand_over(block, source):
        planes, depths = lax.axis_size("dp"), lax.axis_size("tensor")
        count = planes * depths
        pairs = [(source * count + i, (1 - source) * count + i) for i in range(count)]
        return lax.ppermute(block, AXES, pairs)

    def spread_first(pieces):
        one = jnp.concatenate(pieces)
        return jnp.stack([one, exchange(one, dp_masks=FIRST)])

    def spread_second(pair):
        return jnp.concatenate([pair, exchange(pair, dp_masks=SECOND)])

    second_grad, gain_two1, offset_two1 = norm_backward(total1, norms[1][2], norms[1][3], seed)
    mixed_all = both_rows(second_grad.astype(BF16))
    gate_up, down, terms = feed_backward(mixed_all, all1, feed_p1, gated_p1, hidden_p1)
    p1 = feed_terms(gate_up, down)
    p1, terms, mixed_all = together(p1, terms, mixed_all)
    p1 = reduce_second(p1)
    gate_up, down, more = feed_backward(mixed_all, all1, feed_q1, gated_q1, hidden_q1)
    q1 = feed_terms(gate_up, down)
    terms = terms + more
    terms, p1, q1 = together(terms, p1, q1)
    p1, q1 = reduce_first(p1), reduce_second(q1)
    first_grad = join_rows(terms) + second_grad
    sum_grad, gain_one1, offset_one1 = norm_backward(sum1, norms[1][0], norms[1][1], first_grad)
    projected_grad, qkv, out = attn_backward(middle_low, sum_grad, attn1, projected1, context1, slopes, seqs)
    layer_out = give(middle_low, final_low)
    projected_grad, qkv, out, p1, q1, layer_out = together(projected_grad, qkv, out, p1, q1, layer_out)
    projected_grad, a1 = together(projected_grad, attn_terms(qkv, out))
    a1, p1, q1 = reduce_second(a1), reduce_near(p1), reduce_first(q1)
    middle_grad = dot(projected_grad, attn1[0], 1, 0) + sum_grad
    second_grad, gain_two0, offset_two0 = norm_backward(total0, norms[0][2], norms[0][3], middle_grad)
    mixed_all = both_rows(second_grad.astype(BF16))
    gate_up, down, terms = feed_backward(mixed_all, all0, feed_p0, gated_p0, hidden_p0)
    p0 = feed_terms(gate_up, down)
    terms, mixed_all, a1, p1, q1, p0 = together(terms, mixed_all, a1, p1, q1, p0)
    a1, p1, q1, p0 = reduce_first(a1), reduce_far(p1), reduce_near(q1), reduce_second(p0)
    gate_up, down, more = feed_backward(mixed_all, all0, feed_q0, gated_q0, hidden_q0)
    q0 = feed_terms(gate_up, down)
    terms = terms + more
    terms, a1, p1, q1, p0, q0 = together(terms, a1, p1, q1, p0, q0)
    a1, q1, p0, q0 = reduce_near(a1), reduce_far(q1), reduce_first(p0), reduce_second(q0)
    first_grad = join_rows(terms) + second_grad
    sum_grad, gain_one0, offset_one0 = norm_backward(sum0, norms[0][0], norms[0][1], first_grad)
    vectors = jnp.stack(
        [gain_one0, offset_one0, gain_two0, offset_two0, gain_one1, offset_one1, gain_two1, offset_two1]
    )
    projected_grad, qkv, out = attn_backward(start, sum_grad, attn0, projected0, context0, slopes, seqs)
    projected_grad, qkv, out, a1, q1, p0, q0, vectors = together(projected_grad, qkv, out, a1, q1, p0, q0, vectors)
    a0, a1, p0, q0 = reduce_second(attn_terms(qkv, out)), reduce_far(a1), reduce_near(p0), reduce_first(q0)
    vectors = vectors + swap(vectors)
    start_grad = dot(projected_grad, attn0[0], 1, 0) + sum_grad
    input_grad = give(start_grad, middle_grad)
    input_grad, a0, a1, p0, q0, vectors = together(input_grad, a0, a1, p0, q0, vectors)
    a0, p0, q0 = reduce_first(a0), reduce_far(p0), reduce_near(q0)
    late = spread_first([p1, q1, a1])
    mask = 1
    while mask < lax.axis_size("dp"):
        vectors = vectors + exchange(vectors, dp_masks=(mask, mask))
        mask *= 2
    a0, p0, q0, late, vectors = together(a0, p0, q0, late, vectors)
    a0, q0 = reduce_near(a0), reduce_far(q0)
    late = spread_second(late)
    mask = 1
    while mask < lax.axis_size("tensor"):
        vectors = vectors + exchange(vectors, tensor_mask=mask)
        mask *= 2
    a0, p0, q0, late, vectors = together(a0, p0, q0, late, vectors)
    a0, feed_early = reduce_far(a0), spread_first([p0, q0])
    late_got = hand_over(late, 0)
    a0, feed_early, late_got = together(a0, feed_early, late_got)
    attn_early, feed_early = spread_first([a0]), spread_second(feed_early)
    attn_early, feed_early = together(attn_early, feed_early)
    attn_early, feed_got = spread_second(attn_early), hand_over(feed_early, 1)
    attn_got = hand_over(attn_early, 1)

    def settle(early, early_got, late, late_got):
        halves = [jnp.where(is_first, early, late_got), jnp.where(is_first, early_got, late)]
        return jnp.stack(
            [
                jnp.stack(
                    [
                        lax.dynamic_index_in_dim(half, order[jnp.bitwise_xor(in_plane, index)], 0, keepdims=False)
                        for half, order in zip(halves, orders)
                    ]
                )
                for index in range(PLANE)
            ]
        )

    feed_rows = FEED_CHUNKS * 3 * unit_part
    feed_both = settle(feed_early, feed_got, late[:, :feed_rows], late_got[:, :feed_rows])
    attn_both = settle(attn_early, attn_got, late[:, feed_rows:], late_got[:, feed_rows:])
    feed_total = feed_both.reshape(PLANE, 2, FEED_CHUNKS, 3, unit_part, features)
    feed_total = jnp.transpose(feed_total, (3, 1, 2, 0, 4, 5)).reshape(3, units, features).astype(F32)
    grad_in = jnp.transpose(feed_total[:2], (2, 0, 1))
    grad_down = feed_total[2]
    attn_total = attn_both.reshape(PLANE, 2, 2, local_heads, part, features)
    attn_total = jnp.transpose(attn_total, (1, 2, 3, 0, 4, 5)).reshape(4, local, features).astype(F32)
    grad_qkv = jnp.transpose(attn_total[:3], (2, 0, 1))
    grad_out = attn_total[3]

    vectors = lax.dynamic_index_in_dim(vectors.reshape(2, 4, features), core, 0, keepdims=False)
    vectors = lax.dynamic_slice_in_dim(vectors, depth * local, local, 1)

    return (
        layer_out,
        input_grad,
        grad_qkv[None],
        grad_out[None],
        grad_in[None],
        grad_down[None],
        vectors[0][None],
        vectors[1][None],
        vectors[2][None],
        vectors[3][None],
    )


def solution(mesh):
    placed = (
        P(None, ("dp", "tensor"), None, None),
        P(None, ("dp", "tensor"), None, None),
        P(None, ("dp", "tensor"), None),
        P("section", None, None, "tensor"),
        P("section", "tensor", None),
        P("section", None, None, "tensor"),
        P("section", "tensor", None),
        P("section", None),
        P("section", None),
        P("section", None),
        P("section", None),
    )
    return jax.shard_map(
        body,
        mesh=mesh,
        in_specs=placed,
        out_specs=(
            P("section", None, ("dp", "tensor"), None, None),
            P("section", None, ("dp", "tensor"), None, None),
            P("section", None, None, "tensor"),
            P("section", "tensor", None),
            P("section", None, None, "tensor"),
            P("section", "tensor", None),
            P("section", "tensor"),
            P("section", "tensor"),
            P("section", "tensor"),
            P("section", "tensor"),
        ),
        check_vma=False,
    )
```

```python
import functools
import math

import jax
import jax.numpy as jnp
import numpy as np
from jax import lax
from jax.experimental import pallas as pl
from jax.experimental.pallas import tpu as pltpu
from jax.sharding import PartitionSpec as P

HEADS = 12
HEAD_DIM = 64
NORM_EPSILON = 1e-05
AXES = ("section", "dp", "tensor")
FEED_CHUNKS = 2
LANES = 128
GROUP = 3
GROUP_BACK = 3

F32 = jnp.float32
BF16 = jnp.bfloat16


def power_slopes(total_heads):
    return [2.0 ** (-8.0 * (index + 1) / total_heads) for index in range(total_heads)]


def alibi_table(number_heads):
    closest = 2 ** int(math.floor(math.log2(number_heads)))
    slopes = power_slopes(closest)
    slopes = slopes + power_slopes(2 * closest)[0::2][: number_heads - closest]
    return np.array(slopes, dtype=np.float32)


def norm_rows(values, gain, offset):
    row_mean = jnp.mean(values, axis=-1, keepdims=True)
    centred = values - row_mean
    row_var = jnp.mean(centred * centred, axis=-1, keepdims=True)
    return centred * lax.rsqrt(row_var + NORM_EPSILON) * gain + offset


def gelu_product(gate_part, up_part):
    return jax.nn.gelu(gate_part, approximate=False) * up_part


def dot(a, b, ca, cb):
    return lax.dot_general(a, b, (((ca,), (cb,)), ((), ())), preferred_element_type=F32)


def exchange(block, section_mask=0, dp_masks=(0, 0), tensor_mask=0):
    dp = lax.axis_size("dp")
    tensor = lax.axis_size("tensor")
    pairs = []
    for s in range(lax.axis_size("section")):
        for d in range(dp):
            for t in range(tensor):
                target = ((s ^ section_mask) * dp + (d ^ dp_masks[s])) * tensor + (t ^ tensor_mask)
                pairs.append(((s * dp + d) * tensor + t, target))
    return lax.ppermute(block, AXES, pairs)


def swap(block):
    return exchange(block, section_mask=1)


FIRST = (1, 2)
SECOND = (2, 1)
PLANE = 4
DEPTH = 4


def contract(a, b, ca, cb):
    return lax.dot_general(a, b, (((ca,), (cb,)), ((), ())), preferred_element_type=F32)


def head_masks(length):
    lane = lax.broadcasted_iota(jnp.int32, (length, LANES), 1)
    return [lane // HEAD_DIM == index for index in range(LANES // HEAD_DIM)]


def distances(length):
    across = lax.broadcasted_iota(jnp.int32, (length, length), 0)
    along = lax.broadcasted_iota(jnp.int32, (length, length), 1)
    return jnp.abs(across - along).astype(F32)


def attend_kernel(group, slopes_ref, projected_ref, context_ref):
    length, features = context_ref.shape
    masks = head_masks(length)
    distance = distances(length)
    per = len(masks)
    pairs = features // LANES
    for first in range(0, pairs, group):
        heads = [(pair, index) for pair in range(first, first + group) for index in range(per)]
        parts = {p: [slice(i * features + p * LANES, i * features + (p + 1) * LANES) for i in range(3)] for p, _ in heads}
        scores = []
        for pair, index in heads:
            key = projected_ref[:, parts[pair][1]]
            own = jnp.where(masks[index], key, jnp.zeros_like(key))
            scores.append(contract(own, projected_ref[:, parts[pair][0]], 1, 1))
        weights = []
        for (pair, index), score in zip(heads, scores):
            score = score * HEAD_DIM ** (-0.5) - slopes_ref[pair * per + index] * distance
            weight = jnp.exp(score - jnp.max(score, axis=0, keepdims=True))
            weight = weight * (1.0 / jnp.sum(weight, axis=0, keepdims=True))
            weights.append(weight.astype(BF16))
        for pair in range(first, first + group):
            value = projected_ref[:, parts[pair][2]]
            context = jnp.zeros((length, LANES), F32)
            for (other, index), weight in zip(heads, weights):
                if other == pair:
                    context = jnp.where(masks[index], contract(weight, value, 0, 0), context)
            context_ref[:, parts[pair][0]] = context.astype(BF16)


def attend_back_kernel(group, slopes_ref, projected_ref, context_grad_ref, grad_ref):
    length, features = context_grad_ref.shape
    masks = head_masks(length)
    distance = distances(length)
    per = len(masks)
    pairs = features // LANES
    for first in range(0, pairs, group):
        heads = [(pair, index) for pair in range(first, first + group) for index in range(per)]
        parts = {p: [slice(i * features + p * LANES, i * features + (p + 1) * LANES) for i in range(3)] for p, _ in heads}
        scores, weights_grads = [], []
        for pair, index in heads:
            key, value = projected_ref[:, parts[pair][1]], projected_ref[:, parts[pair][2]]
            own = jnp.where(masks[index], key, jnp.zeros_like(key))
            scores.append(contract(own, projected_ref[:, parts[pair][0]], 1, 1))
            own = jnp.where(masks[index], value, jnp.zeros_like(value))
            weights_grads.append(contract(own, context_grad_ref[:, parts[pair][0]], 1, 1))
        weights, score_grads = [], []
        for (pair, index), score, weights_grad in zip(heads, scores, weights_grads):
            score = score * HEAD_DIM ** (-0.5) - slopes_ref[pair * per + index] * distance
            weight = jnp.exp(score - jnp.max(score, axis=0, keepdims=True))
            weight = weight * (1.0 / jnp.sum(weight, axis=0, keepdims=True))
            mean_grad = jnp.sum(weight * weights_grad, axis=0, keepdims=True)
            score_grads.append((weight * (weights_grad - mean_grad)).astype(BF16))
            weights.append(weight.astype(BF16))
        for pair in range(first, first + group):
            query, key = projected_ref[:, parts[pair][0]], projected_ref[:, parts[pair][1]]
            context_grad = context_grad_ref[:, parts[pair][0]]
            grads = [jnp.zeros((length, LANES), F32)] * 3
            for (other, index), weight, score_grad in zip(heads, weights, score_grads):
                if other == pair:
                    new = [
                        contract(score_grad, key, 0, 0) * HEAD_DIM ** (-0.5),
                        contract(score_grad, query, 1, 0) * HEAD_DIM ** (-0.5),
                        contract(weight, context_grad, 1, 0),
                    ]
                    grads = [jnp.where(masks[index], n, g) for n, g in zip(new, grads)]
            for part, grad in zip(parts[pair], grads):
                grad_ref[:, part] = grad.astype(BF16)


def row_block(length, width):
    return pl.BlockSpec((length, width), lambda index: (index, 0))


def attend(projected, slopes, seqs):
    rows, width = projected.shape
    length, features = rows // seqs, width // 3
    return pl.pallas_call(
        functools.partial(attend_kernel, GROUP),
        grid=(seqs,),
        in_specs=[pl.BlockSpec(memory_space=pltpu.SMEM), row_block(length, width)],
        out_specs=row_block(length, features),
        out_shape=jax.ShapeDtypeStruct((rows, features), BF16),
        cost_estimate=pl.CostEstimate(
            flops=4 * rows * length * features, bytes_accessed=2 * rows * (width + features), transcendentals=rows * length * features // HEAD_DIM
        ),
        name="attend",
    )(slopes, projected)


def attend_back(projected, context_grad, slopes, seqs):
    rows, width = projected.shape
    length, features = rows // seqs, width // 3
    return pl.pallas_call(
        functools.partial(attend_back_kernel, GROUP_BACK),
        grid=(seqs,),
        in_specs=[
            pl.BlockSpec(memory_space=pltpu.SMEM),
            row_block(length, width),
            row_block(length, features),
        ],
        out_specs=row_block(length, width),
        out_shape=jax.ShapeDtypeStruct((rows, width), BF16),
        cost_estimate=pl.CostEstimate(
            flops=10 * rows * length * features, bytes_accessed=2 * rows * (2 * width + features), transcendentals=rows * length * features // HEAD_DIM
        ),
        name="attend_back",
    )(slopes, projected, context_grad)


def together(*trees):
    return lax.optimization_barrier(trees)


def near(chunk):
    return dict(chunk, near=exchange(chunk["own"][0], tensor_mask=1))


def far(chunk):
    return dict(chunk, far=exchange(jnp.stack([chunk["own"][0], chunk["near"]]), tensor_mask=2))


def first(chunk):
    remote = jnp.concatenate([chunk["near"][None], chunk["far"]])
    return dict(
        chunk,
        remote=remote,
        first=exchange(remote, dp_masks=FIRST),
        second=exchange(remote, dp_masks=SECOND),
    )


def second(chunk):
    return dict(chunk, third=exchange(chunk["first"], dp_masks=SECOND))


def assemble(chunk):
    rest = [chunk["remote"], chunk["first"], chunk["second"], chunk["third"]]
    return jnp.stack([jnp.concatenate([own[None], r]) for own, r in zip(chunk["own"], rest)])


def add_low(a, b):
    return (a.astype(F32) + b.astype(F32)).astype(BF16)


def halves(terms):
    return terms[: PLANE // 2], terms[PLANE // 2 :]


def reduce_second(terms):
    return terms[0], exchange(terms[1], dp_masks=SECOND)


def reduce_first(pair):
    terms = add_low(*pair)
    return terms[0], exchange(terms[1], dp_masks=FIRST)


def reduce_near(pair):
    terms = add_low(*pair)
    pairs = terms.reshape((2, 2) + terms.shape[1:])
    return pairs[:, 0], exchange(pairs[:, 1], tensor_mask=1)


def reduce_far(pair):
    terms = add_low(*pair)
    return terms[0], exchange(terms[1], tensor_mask=2)


def reduce_last(pair):
    one = add_low(*pair)
    mask = PLANE
    while mask < lax.axis_size("dp"):
        one = add_low(one, exchange(one, dp_masks=(mask, mask)))
        mask *= 2
    return one


def attn_forward(own_low, weights, norms, slopes, seqs):
    wqkv, wo = weights
    projected = dot(own_low, wqkv, 1, 1).astype(BF16)
    context = attend(projected, slopes, seqs)
    first_sum = own_low.astype(F32) + dot(context, wo, 1, 0)
    first_norm = norm_rows(first_sum, norms[0], norms[1])
    return projected, context, first_sum, first_norm


def both_rows(rows_low):
    return jnp.concatenate([rows_low, swap(rows_low)])


def join_rows(terms):
    rows = terms.shape[0] // 2
    return terms[:rows] + swap(terms[rows:].astype(BF16)).astype(F32)


def feed_forward(first_all, weights):
    gate_up, down = weights
    gated = dot(first_all, gate_up, 1, 1)
    gate_part, up_part = jnp.split(gated, 2, axis=-1)
    hidden = gelu_product(gate_part, up_part).astype(BF16)
    return gated, hidden, dot(hidden, down, 1, 0)


def feed_backward(mixed_all, first_all, weights, gated, hidden):
    gate_up, down = weights
    hidden_grad = dot(mixed_all, down, 1, 1)
    down_grad = dot(hidden, mixed_all, 0, 0).astype(BF16)
    gate_part, up_part = jnp.split(gated, 2, axis=-1)
    _, gelu_back = jax.vjp(gelu_product, gate_part, up_part)
    gate_grad, up_grad = gelu_back(hidden_grad)
    gated_grad = jnp.concatenate([gate_grad, up_grad], axis=-1).astype(BF16)
    gate_up_grad = dot(gated_grad, first_all, 0, 0).astype(BF16)
    return gate_up_grad, down_grad, dot(gated_grad, gate_up, 1, 0)


def norm_backward(total, gain, offset, grad):
    _, back = jax.vjp(norm_rows, total, gain, offset)
    return back(grad)


def attn_backward(own_low, sum_grad, weights, projected, context, slopes, seqs):
    wqkv, wo = weights
    attended_low = sum_grad.astype(BF16)
    context_grad = dot(attended_low, wo, 1, 1).astype(BF16)
    out_grad = dot(context, attended_low, 0, 0).astype(BF16)
    projected_grad = attend_back(projected, context_grad, slopes, seqs)
    qkv_grad = dot(projected_grad, own_low, 0, 0).astype(BF16)
    return projected_grad, qkv_grad, out_grad


def body(
    layer_input,
    out_grad,
    loss_mask,
    query_key_value_weight,
    attention_output_weight,
    gate_up_weight,
    down_weight,
    norm1_gain,
    norm1_bias,
    norm2_gain,
    norm2_bias,
):
    core = lax.axis_index("section")
    plane = lax.axis_index("dp")
    depth = lax.axis_index("tensor")
    is_first = core == 0
    micro, own_seqs, length, features = layer_input.shape
    local = query_key_value_weight.shape[-1]
    local_heads = local // HEAD_DIM
    units = down_weight.shape[1]
    part = HEAD_DIM // PLANE
    unit_part = units // 2 // PLANE // FEED_CHUNKS
    seqs = micro * own_seqs // 2
    rows = seqs * length

    orders = [jnp.array([0, 1, 2, 3]), jnp.array([0, 2, 1, 3])]
    steps = jnp.where(is_first, orders[0], orders[1])
    in_plane = jnp.bitwise_and(plane, PLANE - 1)

    def relative(slab):
        return [
            lax.dynamic_index_in_dim(slab, jnp.bitwise_xor(in_plane, steps[e]), 0, keepdims=False)
            for e in range(PLANE)
        ]

    qkv_rows = jnp.transpose(query_key_value_weight[0], (1, 2, 0))
    attn_rows = jnp.concatenate([qkv_rows, attention_output_weight], axis=0)
    attn_slab = attn_rows.reshape(2, 2, local_heads, PLANE, part, features)
    attn_slab = jnp.transpose(attn_slab, (0, 3, 1, 2, 4, 5)).reshape(2, PLANE, -1, features)
    gate_up_rows = jnp.transpose(gate_up_weight[0], (1, 2, 0))
    feed_rows = jnp.concatenate([gate_up_rows, down_weight], axis=0)
    feed_slab = feed_rows.reshape(3, 2, FEED_CHUNKS, PLANE, unit_part, features)
    feed_slab = jnp.transpose(feed_slab, (2, 1, 3, 0, 4, 5)).reshape(FEED_CHUNKS, 2, PLANE, -1, features)

    def share(slab):
        keep = lax.dynamic_index_in_dim(slab, core, 0, keepdims=False)
        got = swap(lax.dynamic_index_in_dim(slab, 1 - core, 0, keepdims=False))
        return jnp.where(is_first, keep, got), jnp.where(is_first, got, keep)

    attn_in = [{"own": relative(own)} for own in share(attn_slab)]
    feed_in = [[{"own": relative(own)} for own in share(feed_slab[k])] for k in range(FEED_CHUNKS)]
    a0, a1 = attn_in
    (p0, p1), (q0, q1) = feed_in


    norm_table = jnp.concatenate([norm1_gain, norm1_bias, norm2_gain, norm2_bias])
    norm_other = swap(norm_table)
    norm_first = jnp.where(is_first, norm_table, norm_other)
    norm_second = jnp.where(is_first, norm_other, norm_table)
    norms = [tuple(table[i] for i in range(4)) for table in (norm_first, norm_second)]

    slope_table = jnp.asarray(alibi_table(HEADS)).reshape(DEPTH, local_heads)
    slopes = jnp.concatenate(
        [lax.dynamic_index_in_dim(slope_table, jnp.bitwise_xor(depth, j), 0, keepdims=False) for j in range(DEPTH)]
    )

    def own_half(whole):
        flat = whole.reshape((2, rows) + whole.shape[3:])
        return lax.dynamic_index_in_dim(flat, core, 0, keepdims=False)

    start = own_half(layer_input)
    seed = own_half(out_grad).astype(F32) * own_half(loss_mask).astype(F32)[..., None]


    def attn_weights(chunk):
        full = assemble(chunk).reshape(PLANE, DEPTH, 2, local_heads, part, features)
        mine = jnp.transpose(full, (2, 1, 3, 0, 4, 5)).reshape(2, -1, features)
        other = swap(mine)
        qk = jnp.where(is_first, mine, other)
        vo = jnp.where(is_first, other, mine)
        wqkv = jnp.concatenate([qk.reshape(-1, features), vo[0]])
        return wqkv, vo[1]

    def feed_weights(chunk):
        full = assemble(chunk).reshape(PLANE * DEPTH, 3, unit_part, features)
        full = jnp.transpose(full, (1, 0, 2, 3)).reshape(3, -1, features)
        return full[:2].reshape(-1, features), full[2]

    a0 = near(a0)
    a0, p0 = together(a0, p0)
    a0, p0 = far(a0), near(p0)
    a0, p0, q0 = together(a0, p0, q0)
    a0, p0, q0 = first(a0), far(p0), near(q0)
    a0, p0, q0, a1 = together(a0, p0, q0, a1)
    a0, p0, q0, a1 = second(a0), first(p0), far(q0), near(a1)
    a0, p0, q0, a1, p1 = together(a0, p0, q0, a1, p1)
    p0, q0, a1, p1 = second(p0), first(q0), far(a1), near(p1)
    attn0 = attn_weights(a0)
    projected0, context0, sum0, norm0 = attn_forward(start, attn0, norms[0], slopes, seqs)
    low0, p0, q0, a1, p1, q1 = together(norm0.astype(BF16), p0, q0, a1, p1, q1)
    q0, a1, p1, q1 = second(q0), first(a1), far(p1), near(q1)
    all0 = both_rows(low0)
    feed_p0 = feed_weights(p0)
    gated_p0, hidden_p0, mixed = feed_forward(all0, feed_p0)
    mixed, q0, a1, p1, q1 = together(mixed, q0, a1, p1, q1)
    a1, p1, q1 = second(a1), first(p1), far(q1)
    feed_q0 = feed_weights(q0)
    gated_q0, hidden_q0, more = feed_forward(all0, feed_q0)
    mixed = mixed + more
    mixed, a1, p1, q1 = together(mixed, a1, p1, q1)
    p1, q1 = second(p1), first(q1)
    attn1 = attn_weights(a1)
    total0 = norm0 + join_rows(mixed)
    middle_low = norm_rows(total0, norms[0][2], norms[0][3]).astype(BF16)
    projected1, context1, sum1, norm1 = attn_forward(middle_low, attn1, norms[1], slopes, seqs)
    low1, p1, q1 = together(norm1.astype(BF16), p1, q1)
    q1 = second(q1)
    all1 = both_rows(low1)
    feed_p1 = feed_weights(p1)
    gated_p1, hidden_p1, mixed = feed_forward(all1, feed_p1)
    mixed, q1 = together(mixed, q1)
    feed_q1 = feed_weights(q1)
    gated_q1, hidden_q1, more = feed_forward(all1, feed_q1)
    total1 = norm1 + join_rows(mixed + more)
    final_low = norm_rows(total1, norms[1][2], norms[1][3]).astype(BF16)

    def give(early, late):
        mine = jnp.where(is_first, early, late)
        got = swap(jnp.where(is_first, late, early))
        both = jnp.concatenate([jnp.where(is_first, mine, got), jnp.where(is_first, got, mine)])
        return both.reshape((1, micro, own_seqs, length, features))

    def feed_terms(gate_up, down):
        full = jnp.concatenate([gate_up, down]).reshape(3, PLANE, DEPTH, unit_part, features)
        return halves(jnp.transpose(full, (1, 2, 0, 3, 4)).reshape(PLANE, DEPTH, -1, features))

    def attn_terms(qkv, out):
        full = jnp.concatenate([qkv, out]).reshape(2, -1, features)
        keep = lax.dynamic_index_in_dim(full, core, 0, keepdims=False)
        return keep, swap(lax.dynamic_index_in_dim(full, 1 - core, 0, keepdims=False))

    def attn_pieces(pair):
        full = add_low(*pair).reshape(2, DEPTH, local_heads, PLANE, part, features)
        return halves(jnp.transpose(full, (3, 1, 0, 2, 4, 5)).reshape(PLANE, DEPTH, -1, features))

    def hand_over(block, source):
        planes, depths = lax.axis_size("dp"), lax.axis_size("tensor")
        count = planes * depths
        pairs = [(source * count + i, (1 - source) * count + i) for i in range(count)]
        return lax.ppermute(block, AXES, pairs)

    second_grad, gain_two1, offset_two1 = norm_backward(total1, norms[1][2], norms[1][3], seed)
    mixed_all = both_rows(second_grad.astype(BF16))
    gate_up, down, terms = feed_backward(mixed_all, all1, feed_p1, gated_p1, hidden_p1)
    p1 = feed_terms(gate_up, down)
    p1, terms, mixed_all = together(p1, terms, mixed_all)
    p1 = reduce_second(p1)
    gate_up, down, more = feed_backward(mixed_all, all1, feed_q1, gated_q1, hidden_q1)
    q1 = feed_terms(gate_up, down)
    terms = terms + more
    terms, p1, q1 = together(terms, p1, q1)
    p1, q1 = reduce_first(p1), reduce_second(q1)
    first_grad = join_rows(terms) + second_grad
    sum_grad, gain_one1, offset_one1 = norm_backward(sum1, norms[1][0], norms[1][1], first_grad)
    projected_grad, qkv, out = attn_backward(middle_low, sum_grad, attn1, projected1, context1, slopes, seqs)
    layer_out = give(middle_low, final_low)
    projected_grad, qkv, out, p1, q1, layer_out = together(projected_grad, qkv, out, p1, q1, layer_out)
    projected_grad, a1 = together(projected_grad, attn_terms(qkv, out))
    a1, p1, q1 = reduce_second(attn_pieces(a1)), reduce_near(p1), reduce_first(q1)
    middle_grad = dot(projected_grad, attn1[0], 1, 0) + sum_grad
    second_grad, gain_two0, offset_two0 = norm_backward(total0, norms[0][2], norms[0][3], middle_grad)
    mixed_all = both_rows(second_grad.astype(BF16))
    gate_up, down, terms = feed_backward(mixed_all, all0, feed_p0, gated_p0, hidden_p0)
    p0 = feed_terms(gate_up, down)
    terms, mixed_all, a1, p1, q1, p0 = together(terms, mixed_all, a1, p1, q1, p0)
    a1, p1, q1, p0 = reduce_first(a1), reduce_far(p1), reduce_near(q1), reduce_second(p0)
    gate_up, down, more = feed_backward(mixed_all, all0, feed_q0, gated_q0, hidden_q0)
    q0 = feed_terms(gate_up, down)
    terms = terms + more
    terms, a1, p1, q1, p0, q0 = together(terms, a1, p1, q1, p0, q0)
    a1, q1, p0, q0 = reduce_near(a1), reduce_far(q1), reduce_first(p0), reduce_second(q0)
    first_grad = join_rows(terms) + second_grad
    sum_grad, gain_one0, offset_one0 = norm_backward(sum0, norms[0][0], norms[0][1], first_grad)
    vectors = jnp.stack(
        [gain_one0, offset_one0, gain_two0, offset_two0, gain_one1, offset_one1, gain_two1, offset_two1]
    )
    projected_grad, qkv, out = attn_backward(start, sum_grad, attn0, projected0, context0, slopes, seqs)
    projected_grad, qkv, out, a1, q1, p0, q0, vectors = together(projected_grad, qkv, out, a1, q1, p0, q0, vectors)
    a0, q0 = attn_terms(qkv, out), reduce_first(q0)
    shared = swap(vectors)
    start_grad = dot(projected_grad, attn0[0], 1, 0) + sum_grad
    start_grad, a0, q0, shared, vectors = together(start_grad, a0, q0, shared, vectors)
    a0, a1, p0, q0 = reduce_second(attn_pieces(a0)), reduce_far(a1), reduce_near(p0), reduce_near(q0)
    vectors = vectors + shared
    mask = 1
    while mask < lax.axis_size("dp"):
        vectors = vectors + exchange(vectors, dp_masks=(mask, mask))
        mask *= 2
    input_grad = give(start_grad, middle_grad)
    a0, a1, p0, q0, vectors, input_grad = together(a0, a1, p0, q0, vectors, input_grad)
    late = jnp.concatenate([reduce_last(p1), reduce_last(q1), reduce_last(a1)])
    a0, p0, q0, late_first = reduce_first(a0), reduce_far(p0), reduce_far(q0), exchange(late, dp_masks=FIRST)
    shared = exchange(vectors, tensor_mask=1)
    a0, p0, q0, late, late_first, vectors, shared = together(a0, p0, q0, late, late_first, vectors, shared)
    a0, late_second = reduce_near(a0), exchange(late, dp_masks=SECOND)
    vectors = vectors + shared
    shared = exchange(vectors, tensor_mask=2)
    a0, late_second, late_first, p0, q0, vectors, shared = together(
        a0, late_second, late_first, p0, q0, vectors, shared
    )
    a0, late_third = reduce_far(a0), exchange(late_first, dp_masks=SECOND)
    vectors = vectors + shared
    feed = jnp.concatenate([reduce_last(p0), reduce_last(q0)])
    feed_first = exchange(feed, dp_masks=FIRST)
    a0, late_third, feed, feed_first = together(a0, late_third, feed, feed_first)
    attn = reduce_last(a0)
    attn_first, attn_second = exchange(attn, dp_masks=FIRST), exchange(attn, dp_masks=SECOND)
    feed_second = exchange(feed, dp_masks=SECOND)
    late = jnp.stack([late, late_first, late_second, late_third])
    late_got = hand_over(late, 0)
    attn_first, attn_second, feed_second, feed_first, late_got = together(
        attn_first, attn_second, feed_second, feed_first, late_got
    )
    attn_third, feed_third = exchange(attn_first, dp_masks=SECOND), exchange(feed_first, dp_masks=SECOND)
    attn_early = jnp.stack([attn, attn_first, attn_second, attn_third])
    feed_early = jnp.stack([feed, feed_first, feed_second, feed_third])
    feed_got, attn_got = hand_over(feed_early, 1), hand_over(attn_early, 1)

    def settle(early, early_got, late, late_got):
        parts = [jnp.where(is_first, early, late_got), jnp.where(is_first, early_got, late)]
        return jnp.stack(
            [
                jnp.stack(
                    [
                        lax.dynamic_index_in_dim(half, order[jnp.bitwise_xor(in_plane, index)], 0, keepdims=False)
                        for half, order in zip(parts, orders)
                    ]
                )
                for index in range(PLANE)
            ]
        )

    feed_rows = FEED_CHUNKS * 3 * unit_part
    feed_both = settle(feed_early, feed_got, late[:, :feed_rows], late_got[:, :feed_rows])
    attn_both = settle(attn_early, attn_got, late[:, feed_rows:], late_got[:, feed_rows:])
    feed_total = feed_both.reshape(PLANE, 2, FEED_CHUNKS, 3, unit_part, features)
    feed_total = jnp.transpose(feed_total, (3, 1, 2, 0, 4, 5)).reshape(3, units, features).astype(F32)
    grad_in = jnp.transpose(feed_total[:2], (2, 0, 1))
    grad_down = feed_total[2]
    attn_total = attn_both.reshape(PLANE, 2, 2, local_heads, part, features)
    attn_total = jnp.transpose(attn_total, (1, 2, 3, 0, 4, 5)).reshape(4, local, features).astype(F32)
    grad_qkv = jnp.transpose(attn_total[:3], (2, 0, 1))
    grad_out = attn_total[3]

    vectors = lax.dynamic_index_in_dim(vectors.reshape(2, 4, features), core, 0, keepdims=False)
    vectors = lax.dynamic_slice_in_dim(vectors, depth * local, local, 1)

    return (
        layer_out,
        input_grad,
        grad_qkv[None],
        grad_out[None],
        grad_in[None],
        grad_down[None],
        vectors[0][None],
        vectors[1][None],
        vectors[2][None],
        vectors[3][None],
    )


def solution(mesh):
    placed = (
        P(None, ("dp", "tensor"), None, None),
        P(None, ("dp", "tensor"), None, None),
        P(None, ("dp", "tensor"), None),
        P("section", None, None, "tensor"),
        P("section", "tensor", None),
        P("section", None, None, "tensor"),
        P("section", "tensor", None),
        P("section", None),
        P("section", None),
        P("section", None),
        P("section", None),
    )
    return jax.shard_map(
        body,
        mesh=mesh,
        in_specs=placed,
        out_specs=(
            P("section", None, ("dp", "tensor"), None, None),
            P("section", None, ("dp", "tensor"), None, None),
            P("section", None, None, "tensor"),
            P("section", "tensor", None),
            P("section", None, None, "tensor"),
            P("section", "tensor", None),
            P("section", "tensor"),
            P("section", "tensor"),
            P("section", "tensor"),
            P("section", "tensor"),
        ),
        check_vma=False,
    )
```

```python
import functools
import math

import jax
import jax.numpy as jnp
import numpy as np
from jax import lax
from jax.experimental import pallas as pl
from jax.experimental.pallas import tpu as pltpu
from jax.sharding import PartitionSpec as P

HEADS = 12
HEAD_DIM = 64
NORM_EPSILON = 1e-05
AXES = ("section", "dp", "tensor")
FEED_CHUNKS = 2
NORM_ROWS = 16
LANES = 128
GROUP = 3
GROUP_BACK = 3

F32 = jnp.float32
BF16 = jnp.bfloat16


def power_slopes(total_heads):
    return [2.0 ** (-8.0 * (index + 1) / total_heads) for index in range(total_heads)]


def alibi_table(number_heads):
    closest = 2 ** int(math.floor(math.log2(number_heads)))
    slopes = power_slopes(closest)
    slopes = slopes + power_slopes(2 * closest)[0::2][: number_heads - closest]
    return np.array(slopes, dtype=np.float32)


def norm_rows(values, gain, offset):
    row_mean = jnp.mean(values, axis=-1, keepdims=True)
    centred = values - row_mean
    row_var = jnp.mean(centred * centred, axis=-1, keepdims=True)
    return centred * lax.rsqrt(row_var + NORM_EPSILON) * gain + offset


def gelu_product(gate_part, up_part):
    return jax.nn.gelu(gate_part, approximate=False) * up_part


def dot(a, b, ca, cb):
    return lax.dot_general(a, b, (((ca,), (cb,)), ((), ())), preferred_element_type=F32)


def exchange(block, section_mask=0, dp_masks=(0, 0), tensor_mask=0):
    dp = lax.axis_size("dp")
    tensor = lax.axis_size("tensor")
    pairs = []
    for s in range(lax.axis_size("section")):
        for d in range(dp):
            for t in range(tensor):
                target = ((s ^ section_mask) * dp + (d ^ dp_masks[s])) * tensor + (t ^ tensor_mask)
                pairs.append(((s * dp + d) * tensor + t, target))
    return lax.ppermute(block, AXES, pairs)


def swap(block):
    return exchange(block, section_mask=1)


FIRST = (1, 2)
SECOND = (2, 1)
PLANE = 4
DEPTH = 4


def contract(a, b, ca, cb):
    return lax.dot_general(a, b, (((ca,), (cb,)), ((), ())), preferred_element_type=F32)


def head_masks(length):
    lane = lax.broadcasted_iota(jnp.int32, (length, LANES), 1)
    return [lane // HEAD_DIM == index for index in range(LANES // HEAD_DIM)]


def distances(length):
    across = lax.broadcasted_iota(jnp.int32, (length, length), 0)
    along = lax.broadcasted_iota(jnp.int32, (length, length), 1)
    return jnp.abs(across - along).astype(F32)


def attend_kernel(group, slopes_ref, projected_ref, context_ref):
    length, features = context_ref.shape
    masks = head_masks(length)
    distance = distances(length)
    per = len(masks)
    pairs = features // LANES
    for first in range(0, pairs, group):
        heads = [(pair, index) for pair in range(first, first + group) for index in range(per)]
        parts = {p: [slice(i * features + p * LANES, i * features + (p + 1) * LANES) for i in range(3)] for p, _ in heads}
        scores = []
        for pair, index in heads:
            key = projected_ref[:, parts[pair][1]]
            own = jnp.where(masks[index], key, jnp.zeros_like(key))
            scores.append(contract(own, projected_ref[:, parts[pair][0]], 1, 1))
        weights = []
        for (pair, index), score in zip(heads, scores):
            score = score * HEAD_DIM ** (-0.5) - slopes_ref[pair * per + index] * distance
            weight = jnp.exp(score - jnp.max(score, axis=0, keepdims=True))
            weight = weight * (1.0 / jnp.sum(weight, axis=0, keepdims=True))
            weights.append(weight.astype(BF16))
        for pair in range(first, first + group):
            value = projected_ref[:, parts[pair][2]]
            context = jnp.zeros((length, LANES), F32)
            for (other, index), weight in zip(heads, weights):
                if other == pair:
                    context = jnp.where(masks[index], contract(weight, value, 0, 0), context)
            context_ref[:, parts[pair][0]] = context.astype(BF16)


def attend_back_kernel(group, slopes_ref, projected_ref, context_grad_ref, grad_ref):
    length, features = context_grad_ref.shape
    masks = head_masks(length)
    distance = distances(length)
    per = len(masks)
    pairs = features // LANES
    for first in range(0, pairs, group):
        heads = [(pair, index) for pair in range(first, first + group) for index in range(per)]
        parts = {p: [slice(i * features + p * LANES, i * features + (p + 1) * LANES) for i in range(3)] for p, _ in heads}
        scores, weights_grads = [], []
        for pair, index in heads:
            key, value = projected_ref[:, parts[pair][1]], projected_ref[:, parts[pair][2]]
            own = jnp.where(masks[index], key, jnp.zeros_like(key))
            scores.append(contract(own, projected_ref[:, parts[pair][0]], 1, 1))
            own = jnp.where(masks[index], value, jnp.zeros_like(value))
            weights_grads.append(contract(own, context_grad_ref[:, parts[pair][0]], 1, 1))
        weights, score_grads = [], []
        for (pair, index), score, weights_grad in zip(heads, scores, weights_grads):
            score = score * HEAD_DIM ** (-0.5) - slopes_ref[pair * per + index] * distance
            weight = jnp.exp(score - jnp.max(score, axis=0, keepdims=True))
            weight = weight * (1.0 / jnp.sum(weight, axis=0, keepdims=True))
            mean_grad = jnp.sum(weight * weights_grad, axis=0, keepdims=True)
            score_grads.append((weight * (weights_grad - mean_grad)).astype(BF16))
            weights.append(weight.astype(BF16))
        for pair in range(first, first + group):
            query, key = projected_ref[:, parts[pair][0]], projected_ref[:, parts[pair][1]]
            context_grad = context_grad_ref[:, parts[pair][0]]
            grads = [jnp.zeros((length, LANES), F32)] * 3
            for (other, index), weight, score_grad in zip(heads, weights, score_grads):
                if other == pair:
                    new = [
                        contract(score_grad, key, 0, 0) * HEAD_DIM ** (-0.5),
                        contract(score_grad, query, 1, 0) * HEAD_DIM ** (-0.5),
                        contract(weight, context_grad, 1, 0),
                    ]
                    grads = [jnp.where(masks[index], n, g) for n, g in zip(new, grads)]
            for part, grad in zip(parts[pair], grads):
                grad_ref[:, part] = grad.astype(BF16)


def row_block(length, width):
    return pl.BlockSpec((length, width), lambda index: (index, 0))


def attend(projected, slopes, seqs):
    rows, width = projected.shape
    length, features = rows // seqs, width // 3
    return pl.pallas_call(
        functools.partial(attend_kernel, GROUP),
        grid=(seqs,),
        in_specs=[pl.BlockSpec(memory_space=pltpu.SMEM), row_block(length, width)],
        out_specs=row_block(length, features),
        out_shape=jax.ShapeDtypeStruct((rows, features), BF16),
        cost_estimate=pl.CostEstimate(
            flops=4 * rows * length * features, bytes_accessed=2 * rows * (width + features), transcendentals=rows * length * features // HEAD_DIM
        ),
        name="attend",
    )(slopes, projected)


def attend_back(projected, context_grad, slopes, seqs):
    rows, width = projected.shape
    length, features = rows // seqs, width // 3
    return pl.pallas_call(
        functools.partial(attend_back_kernel, GROUP_BACK),
        grid=(seqs,),
        in_specs=[
            pl.BlockSpec(memory_space=pltpu.SMEM),
            row_block(length, width),
            row_block(length, features),
        ],
        out_specs=row_block(length, width),
        out_shape=jax.ShapeDtypeStruct((rows, width), BF16),
        cost_estimate=pl.CostEstimate(
            flops=10 * rows * length * features, bytes_accessed=2 * rows * (2 * width + features), transcendentals=rows * length * features // HEAD_DIM
        ),
        name="attend_back",
    )(slopes, projected, context_grad)


def settle_kernel(chunks, kinds, part, flags_ref, *refs):
    *pieces, gate_up_ref, down_ref, held = refs
    first = flags_ref[0] == 1
    count = len(pieces) // 4
    half_rows = chunks * count * part
    for half in range(2):
        for index in range(count):
            mine = pieces[half * count + index]
            other = pieces[(2 + half) * count + index]
            place = flags_ref[1 + half * count + index]
            for chunk in range(chunks):
                base = pl.multiple_of(half * half_rows + chunk * count * part + place * part, part)
                for kind in range(kinds):
                    start = (chunk * kinds + kind) * part
                    rows = jnp.where(first, mine[start : start + part, :], other[start : start + part, :]).astype(F32)
                    if kind < kinds - 1:
                        held[kind, pl.ds(base, part), :] = rows
                    else:
                        down_ref[pl.ds(base, part), :] = rows
    for kind in range(kinds - 1):
        gate_up_ref[:, kind, :] = jnp.transpose(held[kind])


def settle(pieces, flags, chunks, kinds, part):
    rows, features = pieces[0].shape
    units = 2 * (len(pieces) // 4) * chunks * part
    width = 2 * LANES
    return pl.pallas_call(
        functools.partial(settle_kernel, chunks, kinds, part),
        grid=(features // width,),
        in_specs=[pl.BlockSpec(memory_space=pltpu.SMEM)]
        + [pl.BlockSpec((rows, width), lambda index: (0, index))] * len(pieces),
        out_specs=[
            pl.BlockSpec((width, kinds - 1, units), lambda index: (index, 0, 0)),
            pl.BlockSpec((units, width), lambda index: (0, index)),
        ],
        out_shape=[
            jax.ShapeDtypeStruct((features, kinds - 1, units), F32),
            jax.ShapeDtypeStruct((units, features), F32),
        ],
        scratch_shapes=[pltpu.VMEM((kinds - 1, units, width), F32)],
        name="settle",
    )(flags, *pieces)


def together(*trees):
    return lax.optimization_barrier(trees)


def near(chunk):
    return dict(chunk, near=exchange(chunk["own"][0], tensor_mask=1))


def far(chunk):
    return dict(chunk, far=exchange(jnp.stack([chunk["own"][0], chunk["near"]]), tensor_mask=2))


def first(chunk):
    remote = jnp.concatenate([chunk["near"][None], chunk["far"]])
    return dict(
        chunk,
        remote=remote,
        first=exchange(remote, dp_masks=FIRST),
        second=exchange(remote, dp_masks=SECOND),
    )


def second(chunk):
    return dict(chunk, third=exchange(chunk["first"], dp_masks=SECOND))


def assemble(chunk):
    rest = [chunk["remote"], chunk["first"], chunk["second"], chunk["third"]]
    return jnp.stack([jnp.concatenate([own[None], r]) for own, r in zip(chunk["own"], rest)])


def add_low(a, b):
    return (a.astype(F32) + b.astype(F32)).astype(BF16)


def halves(terms):
    return terms[: PLANE // 2], terms[PLANE // 2 :]


def reduce_second(terms):
    return terms[0], exchange(terms[1], dp_masks=SECOND)


def reduce_first(pair):
    terms = add_low(*pair)
    return terms[0], exchange(terms[1], dp_masks=FIRST)


def reduce_near(pair):
    terms = add_low(*pair)
    pairs = terms.reshape((2, 2) + terms.shape[1:])
    return pairs[:, 0], exchange(pairs[:, 1], tensor_mask=1)


def reduce_far(pair):
    terms = add_low(*pair)
    return terms[0], exchange(terms[1], tensor_mask=2)


def reduce_last(pair):
    one = add_low(*pair)
    mask = PLANE
    while mask < lax.axis_size("dp"):
        one = add_low(one, exchange(one, dp_masks=(mask, mask)))
        mask *= 2
    return one


def attn_forward(own_low, weights, norms, slopes, seqs):
    wqkv, wo = weights
    projected = dot(own_low, wqkv, 1, 1).astype(BF16)
    context = attend(projected, slopes, seqs)
    first_sum = own_low.astype(F32) + dot(context, wo, 1, 0)
    first_norm = norm_rows(first_sum, norms[0], norms[1])
    return projected, context, first_sum, first_norm


def both_rows(rows_low):
    return jnp.concatenate([rows_low, swap(rows_low)])


def join_rows(terms):
    rows = terms.shape[0] // 2
    return terms[:rows] + swap(terms[rows:].astype(BF16)).astype(F32)


def feed_forward(first_all, weights):
    gate_up, down = weights
    gated = dot(first_all, gate_up, 1, 1)
    gate_part, up_part = jnp.split(gated, 2, axis=-1)
    hidden = gelu_product(gate_part, up_part).astype(BF16)
    return gated, hidden, dot(hidden, down, 1, 0)


def feed_backward(mixed_all, first_all, weights, gated, hidden):
    gate_up, down = weights
    hidden_grad = dot(mixed_all, down, 1, 1)
    down_grad = dot(hidden, mixed_all, 0, 0).astype(BF16)
    gate_part, up_part = jnp.split(gated, 2, axis=-1)
    _, gelu_back = jax.vjp(gelu_product, gate_part, up_part)
    gate_grad, up_grad = gelu_back(hidden_grad)
    gated_grad = jnp.concatenate([gate_grad, up_grad], axis=-1).astype(BF16)
    gate_up_grad = dot(gated_grad, first_all, 0, 0).astype(BF16)
    return gate_up_grad, down_grad, dot(gated_grad, gate_up, 1, 0)


def norm_backward(total, gain, offset, grad):
    _, back = jax.vjp(norm_rows, total, gain, offset)
    return back(grad)


def attn_backward(own_low, sum_grad, weights, projected, context, slopes, seqs):
    wqkv, wo = weights
    attended_low = sum_grad.astype(BF16)
    context_grad = dot(attended_low, wo, 1, 1).astype(BF16)
    out_grad = dot(context, attended_low, 0, 0).astype(BF16)
    projected_grad = attend_back(projected, context_grad, slopes, seqs)
    qkv_grad = dot(projected_grad, own_low, 0, 0).astype(BF16)
    return projected_grad, qkv_grad, out_grad


def body(
    layer_input,
    out_grad,
    loss_mask,
    query_key_value_weight,
    attention_output_weight,
    gate_up_weight,
    down_weight,
    norm1_gain,
    norm1_bias,
    norm2_gain,
    norm2_bias,
):
    core = lax.axis_index("section")
    plane = lax.axis_index("dp")
    depth = lax.axis_index("tensor")
    is_first = core == 0
    micro, own_seqs, length, features = layer_input.shape
    local = query_key_value_weight.shape[-1]
    local_heads = local // HEAD_DIM
    units = down_weight.shape[1]
    part = HEAD_DIM // PLANE
    unit_part = units // 2 // PLANE // FEED_CHUNKS
    seqs = micro * own_seqs // 2
    rows = seqs * length

    orders = [jnp.array([0, 1, 2, 3]), jnp.array([0, 2, 1, 3])]
    steps = jnp.where(is_first, orders[0], orders[1])
    in_plane = jnp.bitwise_and(plane, PLANE - 1)

    def relative(slab):
        return [
            lax.dynamic_index_in_dim(slab, jnp.bitwise_xor(in_plane, steps[e]), 0, keepdims=False)
            for e in range(PLANE)
        ]

    def share(slab):
        keep = lax.dynamic_index_in_dim(slab, core, 0, keepdims=False)
        got = swap(lax.dynamic_index_in_dim(slab, 1 - core, 0, keepdims=False))
        return jnp.where(is_first, keep, got), jnp.where(is_first, got, keep)

    qkv_rows = jnp.transpose(query_key_value_weight[0], (1, 2, 0))
    attn_rows = jnp.concatenate([qkv_rows, attention_output_weight], axis=0)
    attn_slab = attn_rows.reshape(2, 2, local_heads, PLANE, part, features)
    attn_slab = jnp.transpose(attn_slab, (0, 3, 1, 2, 4, 5)).reshape(2, PLANE, -1, features)
    attn_in = [{"own": relative(own)} for own in share(attn_slab)]
    attn_in[0] = near(attn_in[0])
    attn_in, gate_up_weight, down_weight = together(attn_in, gate_up_weight, down_weight)
    gate_up_rows = jnp.transpose(gate_up_weight[0], (1, 2, 0))
    feed_rows = jnp.concatenate([gate_up_rows, down_weight], axis=0)
    feed_slab = feed_rows.reshape(3, 2, FEED_CHUNKS, PLANE, unit_part, features)
    feed_slab = jnp.transpose(feed_slab, (2, 1, 3, 0, 4, 5)).reshape(FEED_CHUNKS, 2, PLANE, -1, features)

    feed_in = [[{"own": relative(own)} for own in share(feed_slab[k])] for k in range(FEED_CHUNKS)]
    a0, a1 = attn_in
    (p0, p1), (q0, q1) = feed_in


    norm_table = jnp.concatenate([norm1_gain, norm1_bias, norm2_gain, norm2_bias])
    norm_other = swap(norm_table)
    norm_first = jnp.where(is_first, norm_table, norm_other)
    norm_second = jnp.where(is_first, norm_other, norm_table)
    norms = [tuple(table[i] for i in range(4)) for table in (norm_first, norm_second)]

    slope_table = jnp.asarray(alibi_table(HEADS)).reshape(DEPTH, local_heads)
    slopes = jnp.concatenate(
        [lax.dynamic_index_in_dim(slope_table, jnp.bitwise_xor(depth, j), 0, keepdims=False) for j in range(DEPTH)]
    )

    def own_half(whole):
        flat = whole.reshape((2, rows) + whole.shape[3:])
        return lax.dynamic_index_in_dim(flat, core, 0, keepdims=False)

    start = own_half(layer_input)
    seed = own_half(out_grad).astype(F32) * own_half(loss_mask).astype(F32)[..., None]


    def attn_weights(chunk):
        full = assemble(chunk).reshape(PLANE, DEPTH, 2, local_heads, part, features)
        mine = jnp.transpose(full, (2, 1, 3, 0, 4, 5)).reshape(2, -1, features)
        other = swap(mine)
        qk = jnp.where(is_first, mine, other)
        vo = jnp.where(is_first, other, mine)
        wqkv = jnp.concatenate([qk.reshape(-1, features), vo[0]])
        return wqkv, vo[1]

    def feed_weights(chunk):
        full = assemble(chunk).reshape(PLANE * DEPTH, 3, unit_part, features)
        full = jnp.transpose(full, (1, 0, 2, 3)).reshape(3, -1, features)
        return full[:2].reshape(-1, features), full[2]

    a0, p0 = far(a0), near(p0)
    a0, p0, q0 = together(a0, p0, q0)
    a0, p0, q0 = first(a0), far(p0), near(q0)
    a0, p0, q0, a1 = together(a0, p0, q0, a1)
    a0, p0, q0, a1 = second(a0), first(p0), far(q0), near(a1)
    a0, p0, q0, a1, p1 = together(a0, p0, q0, a1, p1)
    p0, q0, a1, p1 = second(p0), first(q0), far(a1), near(p1)
    attn0 = attn_weights(a0)
    projected0, context0, sum0, norm0 = attn_forward(start, attn0, norms[0], slopes, seqs)
    low0, p0, q0, a1, p1, q1 = together(norm0.astype(BF16), p0, q0, a1, p1, q1)
    q0, a1, p1, q1 = second(q0), first(a1), far(p1), near(q1)
    all0 = both_rows(low0)
    feed_p0 = feed_weights(p0)
    gated_p0, hidden_p0, mixed = feed_forward(all0, feed_p0)
    mixed, q0, a1, p1, q1 = together(mixed, q0, a1, p1, q1)
    a1, p1, q1 = second(a1), first(p1), far(q1)
    feed_q0 = feed_weights(q0)
    gated_q0, hidden_q0, more = feed_forward(all0, feed_q0)
    mixed = mixed + more
    mixed, a1, p1, q1 = together(mixed, a1, p1, q1)
    p1, q1 = second(p1), first(q1)
    attn1 = attn_weights(a1)
    total0 = norm0 + join_rows(mixed)
    middle_low = norm_rows(total0, norms[0][2], norms[0][3]).astype(BF16)
    projected1, context1, sum1, norm1 = attn_forward(middle_low, attn1, norms[1], slopes, seqs)
    low1, p1, q1 = together(norm1.astype(BF16), p1, q1)
    q1 = second(q1)
    all1 = both_rows(low1)
    feed_p1 = feed_weights(p1)
    gated_p1, hidden_p1, mixed = feed_forward(all1, feed_p1)
    mixed, q1 = together(mixed, q1)
    feed_q1 = feed_weights(q1)
    gated_q1, hidden_q1, more = feed_forward(all1, feed_q1)
    total1 = norm1 + join_rows(mixed + more)
    final_low = norm_rows(total1, norms[1][2], norms[1][3]).astype(BF16)

    def give(early, late):
        mine = jnp.where(is_first, early, late)
        got = swap(jnp.where(is_first, late, early))
        both = jnp.concatenate([jnp.where(is_first, mine, got), jnp.where(is_first, got, mine)])
        return both.reshape((1, micro, own_seqs, length, features))

    def feed_terms(gate_up, down):
        full = jnp.concatenate([gate_up, down]).reshape(3, PLANE, DEPTH, unit_part, features)
        return halves(jnp.transpose(full, (1, 2, 0, 3, 4)).reshape(PLANE, DEPTH, -1, features))

    def attn_terms(qkv, out, vectors):
        spread = jnp.transpose(jnp.stack(vectors).reshape(4, DEPTH, local), (1, 0, 2)).reshape(DEPTH, features)
        spread = [lax.dynamic_index_in_dim(spread, jnp.bitwise_xor(depth, j), 0) for j in range(DEPTH)]
        spread = jnp.pad(jnp.concatenate(spread).astype(BF16), ((0, NORM_ROWS - DEPTH), (0, 0)))
        full = jnp.concatenate([qkv, out]).reshape(2, -1, features)
        full = jnp.concatenate([full, jnp.stack([spread, spread])], axis=1)
        keep = lax.dynamic_index_in_dim(full, core, 0, keepdims=False)
        return keep, swap(lax.dynamic_index_in_dim(full, 1 - core, 0, keepdims=False))

    def attn_pieces(pair):
        full = add_low(*pair)
        spread = full[-NORM_ROWS : DEPTH - NORM_ROWS]
        spread = jnp.broadcast_to(spread[None, :, None], (PLANE, DEPTH, NORM_ROWS, features))
        full = full[:-NORM_ROWS].reshape(2, DEPTH, local_heads, PLANE, part, features)
        full = jnp.transpose(full, (3, 1, 0, 2, 4, 5)).reshape(PLANE, DEPTH, -1, features)
        return halves(jnp.concatenate([full, spread], axis=2))

    def hand_over(block, source):
        planes, depths = lax.axis_size("dp"), lax.axis_size("tensor")
        count = planes * depths
        pairs = [(source * count + i, (1 - source) * count + i) for i in range(count)]
        return lax.ppermute(block, AXES, pairs)

    second_grad, gain_two1, offset_two1 = norm_backward(total1, norms[1][2], norms[1][3], seed)
    mixed_all = both_rows(second_grad.astype(BF16))
    gate_up, down, terms = feed_backward(mixed_all, all1, feed_p1, gated_p1, hidden_p1)
    p1 = feed_terms(gate_up, down)
    p1, terms, mixed_all = together(p1, terms, mixed_all)
    p1 = reduce_second(p1)
    gate_up, down, more = feed_backward(mixed_all, all1, feed_q1, gated_q1, hidden_q1)
    q1 = feed_terms(gate_up, down)
    terms = terms + more
    terms, p1, q1 = together(terms, p1, q1)
    p1, q1 = reduce_first(p1), reduce_second(q1)
    first_grad = join_rows(terms) + second_grad
    sum_grad, gain_one1, offset_one1 = norm_backward(sum1, norms[1][0], norms[1][1], first_grad)
    projected_grad, qkv, out = attn_backward(middle_low, sum_grad, attn1, projected1, context1, slopes, seqs)
    layer_out = give(middle_low, final_low)
    projected_grad, qkv, out, p1, q1, layer_out = together(projected_grad, qkv, out, p1, q1, layer_out)
    vectors = [gain_one1, offset_one1, gain_two1, offset_two1]
    projected_grad, a1 = together(projected_grad, attn_terms(qkv, out, vectors))
    a1, p1, q1 = reduce_second(attn_pieces(a1)), reduce_near(p1), reduce_first(q1)
    middle_grad = dot(projected_grad, attn1[0], 1, 0) + sum_grad
    second_grad, gain_two0, offset_two0 = norm_backward(total0, norms[0][2], norms[0][3], middle_grad)
    mixed_all = both_rows(second_grad.astype(BF16))
    gate_up, down, terms = feed_backward(mixed_all, all0, feed_p0, gated_p0, hidden_p0)
    p0 = feed_terms(gate_up, down)
    terms, mixed_all, a1, p1, q1, p0 = together(terms, mixed_all, a1, p1, q1, p0)
    a1, p1, q1, p0 = reduce_first(a1), reduce_far(p1), reduce_near(q1), reduce_second(p0)
    gate_up, down, more = feed_backward(mixed_all, all0, feed_q0, gated_q0, hidden_q0)
    q0 = feed_terms(gate_up, down)
    terms = terms + more
    terms, a1, p1, q1, p0, q0 = together(terms, a1, p1, q1, p0, q0)
    a1, q1, p0, q0 = reduce_near(a1), reduce_far(q1), reduce_first(p0), reduce_second(q0)
    first_grad = join_rows(terms) + second_grad
    sum_grad, gain_one0, offset_one0 = norm_backward(sum0, norms[0][0], norms[0][1], first_grad)
    projected_grad, qkv, out = attn_backward(start, sum_grad, attn0, projected0, context0, slopes, seqs)
    projected_grad, qkv, out, a1, q1, p0, q0 = together(projected_grad, qkv, out, a1, q1, p0, q0)
    a0 = attn_terms(qkv, out, [gain_one0, offset_one0, gain_two0, offset_two0])
    start_grad = dot(projected_grad, attn0[0], 1, 0) + sum_grad
    q0 = reduce_first(q0)
    start_grad, a0 = together(start_grad, a0)
    a0, a1, p0 = reduce_second(attn_pieces(a0)), reduce_far(a1), reduce_near(p0)
    input_grad = give(start_grad, middle_grad)
    a0, a1, p0, q0, input_grad = together(a0, a1, p0, q0, input_grad)
    attn_late = reduce_last(a1)
    late = jnp.concatenate([reduce_last(p1), reduce_last(q1), attn_late[:-NORM_ROWS]])
    a0, p0, q0, late_first = reduce_first(a0), reduce_far(p0), reduce_near(q0), exchange(late, dp_masks=FIRST)
    a0, p0, q0, late, late_first = together(a0, p0, q0, late, late_first)
    a0, q0, late_second = reduce_near(a0), reduce_far(q0), exchange(late, dp_masks=SECOND)
    late_got = [hand_over(late, 0), hand_over(late_first, 0)]
    a0, late_second, late_first, p0, q0 = together(a0, late_second, late_first, p0, q0)
    a0, late_third = reduce_far(a0), exchange(late_first, dp_masks=SECOND)
    feed = jnp.concatenate([reduce_last(p0), reduce_last(q0)])
    feed_first = exchange(feed, dp_masks=FIRST)
    late_got.append(hand_over(late_second, 0))
    a0, late_third, feed, feed_first, late_got = together(a0, late_third, feed, feed_first, late_got)
    attn_early = reduce_last(a0)
    attn = attn_early[:-NORM_ROWS]
    attn_first, attn_second = exchange(attn, dp_masks=FIRST), exchange(attn, dp_masks=SECOND)
    feed_second = exchange(feed, dp_masks=SECOND)
    late_got.append(hand_over(late_third, 0))
    feed_got = [hand_over(feed, 1), hand_over(feed_first, 1)]
    attn_first, attn_second, feed_second, feed_first, late_got, feed_got = together(
        attn_first, attn_second, feed_second, feed_first, late_got, feed_got
    )
    attn_third, feed_third = exchange(attn_first, dp_masks=SECOND), exchange(feed_first, dp_masks=SECOND)
    feed_early = [feed, feed_first, feed_second, feed_third]
    feed_got = feed_got + [hand_over(feed_second, 1), hand_over(feed_third, 1)]
    attn_early_all = jnp.stack([attn, attn_first, attn_second, attn_third])
    attn_got = hand_over(attn_early_all, 1)

    feed_rows = FEED_CHUNKS * 3 * unit_part
    late = [late, late_first, late_second, late_third]
    early_half = [feed_early, [piece[:feed_rows] for piece in late_got]]
    late_half = [feed_got, [piece[:feed_rows] for piece in late]]
    flags = jnp.concatenate(
        [is_first.astype(jnp.int32)[None]] + [jnp.bitwise_xor(in_plane, order) for order in orders]
    )
    grad_in, grad_down = settle(
        early_half[0] + late_half[0] + early_half[1] + late_half[1], flags, FEED_CHUNKS, 3, unit_part
    )
    attn_late_all = jnp.stack([piece[feed_rows:] for piece in late])
    attn_late_got = jnp.stack([piece[feed_rows:] for piece in late_got])
    parts = [jnp.where(is_first, attn_early_all, attn_late_got), jnp.where(is_first, attn_got, attn_late_all)]
    attn_total = jnp.stack(
        [
            jnp.stack(
                [
                    lax.dynamic_index_in_dim(half, order[jnp.bitwise_xor(in_plane, index)], 0, keepdims=False)
                    for half, order in zip(parts, orders)
                ]
            )
            for index in range(PLANE)
        ]
    )
    attn_total = attn_total.reshape(PLANE, 2, 2, local_heads, part, features)
    attn_total = jnp.transpose(attn_total, (1, 2, 3, 0, 4, 5)).reshape(4, local, features).astype(F32)
    grad_qkv = jnp.transpose(attn_total[:3], (2, 0, 1))
    grad_out = attn_total[3]

    vectors = jnp.where(is_first, attn_early[-1], attn_late[-1]).astype(F32).reshape(4, local)

    return (
        layer_out,
        input_grad,
        grad_qkv[None],
        grad_out[None],
        grad_in[None],
        grad_down[None],
        vectors[0][None],
        vectors[1][None],
        vectors[2][None],
        vectors[3][None],
    )


def solution(mesh):
    placed = (
        P(None, ("dp", "tensor"), None, None),
        P(None, ("dp", "tensor"), None, None),
        P(None, ("dp", "tensor"), None),
        P("section", None, None, "tensor"),
        P("section", "tensor", None),
        P("section", None, None, "tensor"),
        P("section", "tensor", None),
        P("section", None),
        P("section", None),
        P("section", None),
        P("section", None),
    )
    return jax.shard_map(
        body,
        mesh=mesh,
        in_specs=placed,
        out_specs=(
            P("section", None, ("dp", "tensor"), None, None),
            P("section", None, ("dp", "tensor"), None, None),
            P("section", None, None, "tensor"),
            P("section", "tensor", None),
            P("section", None, None, "tensor"),
            P("section", "tensor", None),
            P("section", "tensor"),
            P("section", "tensor"),
            P("section", "tensor"),
            P("section", "tensor"),
        ),
        check_vma=False,
    )
```

```python
import functools
import math

import jax
import jax.numpy as jnp
import numpy as np
from jax import lax
from jax.experimental import pallas as pl
from jax.experimental.pallas import tpu as pltpu
from jax.sharding import PartitionSpec as P

HEADS = 12
HEAD_DIM = 64
NORM_EPSILON = 1e-05
AXES = ("section", "dp", "tensor")
FEED_CHUNKS = 2
NORM_ROWS = 16
LANES = 128
GROUP = 3
GROUP_BACK = 3

F32 = jnp.float32
BF16 = jnp.bfloat16


def power_slopes(total_heads):
    return [2.0 ** (-8.0 * (index + 1) / total_heads) for index in range(total_heads)]


def alibi_table(number_heads):
    closest = 2 ** int(math.floor(math.log2(number_heads)))
    slopes = power_slopes(closest)
    slopes = slopes + power_slopes(2 * closest)[0::2][: number_heads - closest]
    return np.array(slopes, dtype=np.float32)


def norm_rows(values, gain, offset):
    row_mean = jnp.mean(values, axis=-1, keepdims=True)
    centred = values - row_mean
    row_var = jnp.mean(centred * centred, axis=-1, keepdims=True)
    return centred * lax.rsqrt(row_var + NORM_EPSILON) * gain + offset


def gelu_product(gate_part, up_part):
    return jax.nn.gelu(gate_part, approximate=False) * up_part


def dot(a, b, ca, cb):
    return lax.dot_general(a, b, (((ca,), (cb,)), ((), ())), preferred_element_type=F32)


def exchange(block, section_mask=0, dp_masks=(0, 0), tensor_mask=0):
    dp = lax.axis_size("dp")
    tensor = lax.axis_size("tensor")
    pairs = []
    for s in range(lax.axis_size("section")):
        for d in range(dp):
            for t in range(tensor):
                target = ((s ^ section_mask) * dp + (d ^ dp_masks[s])) * tensor + (t ^ tensor_mask)
                pairs.append(((s * dp + d) * tensor + t, target))
    return lax.ppermute(block, AXES, pairs)


def swap(block):
    return exchange(block, section_mask=1)


FIRST = (1, 2)
SECOND = (2, 1)
PLANE = 4
DEPTH = 4


def contract(a, b, ca, cb):
    return lax.dot_general(a, b, (((ca,), (cb,)), ((), ())), preferred_element_type=F32)


def head_masks(length):
    lane = lax.broadcasted_iota(jnp.int32, (length, LANES), 1)
    return [lane // HEAD_DIM == index for index in range(LANES // HEAD_DIM)]


def distances(length):
    across = lax.broadcasted_iota(jnp.int32, (length, length), 0)
    along = lax.broadcasted_iota(jnp.int32, (length, length), 1)
    return jnp.abs(across - along).astype(F32)


def attend_kernel(group, slopes_ref, projected_ref, context_ref):
    length, features = context_ref.shape
    masks = head_masks(length)
    distance = distances(length)
    per = len(masks)
    pairs = features // LANES
    for first in range(0, pairs, group):
        heads = [(pair, index) for pair in range(first, first + group) for index in range(per)]
        parts = {p: [slice(i * features + p * LANES, i * features + (p + 1) * LANES) for i in range(3)] for p, _ in heads}
        scores = []
        for pair, index in heads:
            key = projected_ref[:, parts[pair][1]]
            own = jnp.where(masks[index], key, jnp.zeros_like(key))
            scores.append(contract(own, projected_ref[:, parts[pair][0]], 1, 1))
        weights = []
        for (pair, index), score in zip(heads, scores):
            score = score * HEAD_DIM ** (-0.5) - slopes_ref[pair * per + index] * distance
            weight = jnp.exp(score - jnp.max(score, axis=0, keepdims=True))
            weight = weight * (1.0 / jnp.sum(weight, axis=0, keepdims=True))
            weights.append(weight.astype(BF16))
        for pair in range(first, first + group):
            value = projected_ref[:, parts[pair][2]]
            context = jnp.zeros((length, LANES), F32)
            for (other, index), weight in zip(heads, weights):
                if other == pair:
                    context = jnp.where(masks[index], contract(weight, value, 0, 0), context)
            context_ref[:, parts[pair][0]] = context.astype(BF16)


def attend_back_kernel(group, slopes_ref, projected_ref, context_grad_ref, grad_ref):
    length, features = context_grad_ref.shape
    masks = head_masks(length)
    distance = distances(length)
    per = len(masks)
    pairs = features // LANES
    for first in range(0, pairs, group):
        heads = [(pair, index) for pair in range(first, first + group) for index in range(per)]
        parts = {p: [slice(i * features + p * LANES, i * features + (p + 1) * LANES) for i in range(3)] for p, _ in heads}
        scores, weights_grads = [], []
        for pair, index in heads:
            key, value = projected_ref[:, parts[pair][1]], projected_ref[:, parts[pair][2]]
            own = jnp.where(masks[index], key, jnp.zeros_like(key))
            scores.append(contract(own, projected_ref[:, parts[pair][0]], 1, 1))
            own = jnp.where(masks[index], value, jnp.zeros_like(value))
            weights_grads.append(contract(own, context_grad_ref[:, parts[pair][0]], 1, 1))
        weights, score_grads = [], []
        for (pair, index), score, weights_grad in zip(heads, scores, weights_grads):
            score = score * HEAD_DIM ** (-0.5) - slopes_ref[pair * per + index] * distance
            weight = jnp.exp(score - jnp.max(score, axis=0, keepdims=True))
            weight = weight * (1.0 / jnp.sum(weight, axis=0, keepdims=True))
            mean_grad = jnp.sum(weight * weights_grad, axis=0, keepdims=True)
            score_grads.append((weight * (weights_grad - mean_grad)).astype(BF16))
            weights.append(weight.astype(BF16))
        for pair in range(first, first + group):
            query, key = projected_ref[:, parts[pair][0]], projected_ref[:, parts[pair][1]]
            context_grad = context_grad_ref[:, parts[pair][0]]
            grads = [jnp.zeros((length, LANES), F32)] * 3
            for (other, index), weight, score_grad in zip(heads, weights, score_grads):
                if other == pair:
                    new = [
                        contract(score_grad, key, 0, 0) * HEAD_DIM ** (-0.5),
                        contract(score_grad, query, 1, 0) * HEAD_DIM ** (-0.5),
                        contract(weight, context_grad, 1, 0),
                    ]
                    grads = [jnp.where(masks[index], n, g) for n, g in zip(new, grads)]
            for part, grad in zip(parts[pair], grads):
                grad_ref[:, part] = grad.astype(BF16)


def row_block(length, width):
    return pl.BlockSpec((length, width), lambda index: (index, 0))


def attend(projected, slopes, seqs):
    rows, width = projected.shape
    length, features = rows // seqs, width // 3
    return pl.pallas_call(
        functools.partial(attend_kernel, GROUP),
        grid=(seqs,),
        in_specs=[pl.BlockSpec(memory_space=pltpu.SMEM), row_block(length, width)],
        out_specs=row_block(length, features),
        out_shape=jax.ShapeDtypeStruct((rows, features), BF16),
        cost_estimate=pl.CostEstimate(
            flops=4 * rows * length * features, bytes_accessed=2 * rows * (width + features), transcendentals=rows * length * features // HEAD_DIM
        ),
        name="attend",
    )(slopes, projected)


def attend_back(projected, context_grad, slopes, seqs):
    rows, width = projected.shape
    length, features = rows // seqs, width // 3
    return pl.pallas_call(
        functools.partial(attend_back_kernel, GROUP_BACK),
        grid=(seqs,),
        in_specs=[
            pl.BlockSpec(memory_space=pltpu.SMEM),
            row_block(length, width),
            row_block(length, features),
        ],
        out_specs=row_block(length, width),
        out_shape=jax.ShapeDtypeStruct((rows, width), BF16),
        cost_estimate=pl.CostEstimate(
            flops=10 * rows * length * features, bytes_accessed=2 * rows * (2 * width + features), transcendentals=rows * length * features // HEAD_DIM
        ),
        name="attend_back",
    )(slopes, projected, context_grad)


def settle_kernel(chunks, kinds, part, flags_ref, *refs):
    *pieces, gate_up_ref, down_ref, held = refs
    first = flags_ref[0] == 1
    count = len(pieces) // 4
    half_rows = chunks * count * part
    for half in range(2):
        for index in range(count):
            mine = pieces[half * count + index]
            other = pieces[(2 + half) * count + index]
            place = flags_ref[1 + half * count + index]
            for chunk in range(chunks):
                base = pl.multiple_of(half * half_rows + chunk * count * part + place * part, part)
                for kind in range(kinds):
                    start = (chunk * kinds + kind) * part
                    rows = jnp.where(first, mine[start : start + part, :], other[start : start + part, :]).astype(F32)
                    if kind < kinds - 1:
                        held[kind, pl.ds(base, part), :] = rows
                    else:
                        down_ref[pl.ds(base, part), :] = rows
    for kind in range(kinds - 1):
        gate_up_ref[:, kind, :] = jnp.transpose(held[kind])


def settle(pieces, flags, chunks, kinds, part):
    rows, features = pieces[0].shape
    units = 2 * (len(pieces) // 4) * chunks * part
    width = 2 * LANES
    return pl.pallas_call(
        functools.partial(settle_kernel, chunks, kinds, part),
        grid=(features // width,),
        in_specs=[pl.BlockSpec(memory_space=pltpu.SMEM)]
        + [pl.BlockSpec((rows, width), lambda index: (0, index))] * len(pieces),
        out_specs=[
            pl.BlockSpec((width, kinds - 1, units), lambda index: (index, 0, 0)),
            pl.BlockSpec((units, width), lambda index: (0, index)),
        ],
        out_shape=[
            jax.ShapeDtypeStruct((features, kinds - 1, units), F32),
            jax.ShapeDtypeStruct((units, features), F32),
        ],
        scratch_shapes=[pltpu.VMEM((kinds - 1, units, width), F32)],
        name="settle",
    )(flags, *pieces)


def together(*trees):
    return lax.optimization_barrier(trees)


def near(chunk):
    return dict(chunk, near=exchange(chunk["own"][0], tensor_mask=1))


def far(chunk):
    return dict(chunk, far=exchange(jnp.stack([chunk["own"][0], chunk["near"]]), tensor_mask=2))


def first(chunk):
    remote = jnp.concatenate([chunk["near"][None], chunk["far"]])
    return dict(
        chunk,
        remote=remote,
        first=exchange(remote, dp_masks=FIRST),
        second=exchange(remote, dp_masks=SECOND),
    )


def second(chunk):
    return dict(chunk, third=exchange(chunk["first"], dp_masks=SECOND))


def assemble(chunk):
    rest = [chunk["remote"], chunk["first"], chunk["second"], chunk["third"]]
    return jnp.stack([jnp.concatenate([own[None], r]) for own, r in zip(chunk["own"], rest)])


def add_low(a, b):
    return (a.astype(F32) + b.astype(F32)).astype(BF16)


def total_low(*parts):
    return sum(part.astype(F32) for part in parts).astype(BF16)


def reduce_open(terms):
    return (
        terms[0],
        terms[1],
        exchange(terms[3], dp_masks=SECOND),
        exchange(terms[2], dp_masks=SECOND),
    )


def reduce_turn(parts):
    return parts[0], exchange(total_low(parts[1], parts[2]), dp_masks=FIRST)


def reduce_near(own, turned, opened):
    pairs = total_low(own, turned, opened)
    pairs = pairs.reshape((2, 2) + pairs.shape[1:])
    return pairs[:, 0], exchange(pairs[:, 1], tensor_mask=1)


def reduce_far(pair):
    terms = total_low(*pair)
    return terms[0], exchange(terms[1], tensor_mask=2)


def reduce_last(pair):
    one = total_low(*pair)
    mask = PLANE
    while mask < lax.axis_size("dp"):
        one = total_low(one, exchange(one, dp_masks=(mask, mask)))
        mask *= 2
    return one


def attn_forward(own_low, weights, norms, slopes, seqs):
    wqkv, wo = weights
    projected = dot(own_low, wqkv, 1, 1).astype(BF16)
    context = attend(projected, slopes, seqs)
    first_sum = own_low.astype(F32) + dot(context, wo, 1, 0)
    first_norm = norm_rows(first_sum, norms[0], norms[1])
    return projected, context, first_sum, first_norm


def both_rows(rows_low):
    return jnp.concatenate([rows_low, swap(rows_low)])


def join_rows(terms):
    rows = terms.shape[0] // 2
    return terms[:rows] + swap(terms[rows:].astype(BF16)).astype(F32)


def feed_forward(first_all, weights):
    gate_up, down = weights
    gated = dot(first_all, gate_up, 1, 1)
    gate_part, up_part = jnp.split(gated, 2, axis=-1)
    hidden = gelu_product(gate_part, up_part).astype(BF16)
    return gated, hidden, dot(hidden, down, 1, 0)


def feed_backward(mixed_all, weights, gated):
    hidden_grad = dot(mixed_all, weights[1], 1, 1)
    gate_part, up_part = jnp.split(gated, 2, axis=-1)
    _, gelu_back = jax.vjp(gelu_product, gate_part, up_part)
    gate_grad, up_grad = gelu_back(hidden_grad)
    return jnp.concatenate([gate_grad, up_grad], axis=-1).astype(BF16)


def feed_weight_grads(mixed_all, first_all, gated_grad, hidden):
    return dot(gated_grad, first_all, 0, 0).astype(BF16), dot(hidden, mixed_all, 0, 0).astype(BF16)


def norm_backward(total, gain, offset, grad):
    _, back = jax.vjp(norm_rows, total, gain, offset)
    return back(grad)


def context_backward(sum_grad, weights, context):
    attended_low = sum_grad.astype(BF16)
    context_grad = dot(attended_low, weights[1], 1, 1).astype(BF16)
    return context_grad, dot(context, attended_low, 0, 0).astype(BF16)


def body(
    layer_input,
    out_grad,
    loss_mask,
    query_key_value_weight,
    attention_output_weight,
    gate_up_weight,
    down_weight,
    norm1_gain,
    norm1_bias,
    norm2_gain,
    norm2_bias,
):
    core = lax.axis_index("section")
    plane = lax.axis_index("dp")
    depth = lax.axis_index("tensor")
    is_first = core == 0
    micro, own_seqs, length, features = layer_input.shape
    local = query_key_value_weight.shape[-1]
    local_heads = local // HEAD_DIM
    units = down_weight.shape[1]
    part = HEAD_DIM // PLANE
    unit_part = units // 2 // PLANE // FEED_CHUNKS
    seqs = micro * own_seqs // 2
    rows = seqs * length

    orders = [jnp.array([0, 1, 2, 3]), jnp.array([0, 2, 1, 3])]
    steps = jnp.where(is_first, orders[0], orders[1])
    in_plane = jnp.bitwise_and(plane, PLANE - 1)

    def relative(slab):
        return [
            lax.dynamic_index_in_dim(slab, jnp.bitwise_xor(in_plane, steps[e]), 0, keepdims=False)
            for e in range(PLANE)
        ]

    def share(slab):
        keep = lax.dynamic_index_in_dim(slab, core, 0, keepdims=False)
        got = swap(lax.dynamic_index_in_dim(slab, 1 - core, 0, keepdims=False))
        return jnp.where(is_first, keep, got), jnp.where(is_first, got, keep)

    qkv_rows = jnp.transpose(query_key_value_weight[0], (1, 2, 0))
    attn_rows = jnp.concatenate([qkv_rows, attention_output_weight], axis=0)
    attn_slab = attn_rows.reshape(2, 2, local_heads, PLANE, part, features)
    attn_slab = jnp.transpose(attn_slab, (0, 3, 1, 2, 4, 5)).reshape(2, PLANE, -1, features)
    attn_in = [{"own": relative(own)} for own in share(attn_slab)]
    attn_in[0] = near(attn_in[0])
    attn_in, gate_up_weight, down_weight = together(attn_in, gate_up_weight, down_weight)
    gate_up_rows = jnp.transpose(gate_up_weight[0], (1, 2, 0))
    feed_rows = jnp.concatenate([gate_up_rows, down_weight], axis=0)
    feed_slab = feed_rows.reshape(3, 2, FEED_CHUNKS, PLANE, unit_part, features)
    feed_slab = jnp.transpose(feed_slab, (2, 1, 3, 0, 4, 5)).reshape(FEED_CHUNKS, 2, PLANE, -1, features)

    feed_in = [[{"own": relative(own)} for own in share(feed_slab[k])] for k in range(FEED_CHUNKS)]
    a0, a1 = attn_in
    (p0, p1), (q0, q1) = feed_in


    norm_table = jnp.concatenate([norm1_gain, norm1_bias, norm2_gain, norm2_bias])
    norm_other = swap(norm_table)
    norm_first = jnp.where(is_first, norm_table, norm_other)
    norm_second = jnp.where(is_first, norm_other, norm_table)
    norms = [tuple(table[i] for i in range(4)) for table in (norm_first, norm_second)]

    slope_table = jnp.asarray(alibi_table(HEADS)).reshape(DEPTH, local_heads)
    slopes = jnp.concatenate(
        [lax.dynamic_index_in_dim(slope_table, jnp.bitwise_xor(depth, j), 0, keepdims=False) for j in range(DEPTH)]
    )

    def own_half(whole):
        flat = whole.reshape((2, rows) + whole.shape[3:])
        return lax.dynamic_index_in_dim(flat, core, 0, keepdims=False)

    start = own_half(layer_input)
    seed = own_half(out_grad).astype(F32) * own_half(loss_mask).astype(F32)[..., None]


    def attn_weights(chunk):
        full = assemble(chunk).reshape(PLANE, DEPTH, 2, local_heads, part, features)
        mine = jnp.transpose(full, (2, 1, 3, 0, 4, 5)).reshape(2, -1, features)
        other = swap(mine)
        qk = jnp.where(is_first, mine, other)
        vo = jnp.where(is_first, other, mine)
        wqkv = jnp.concatenate([qk.reshape(-1, features), vo[0]])
        return wqkv, vo[1]

    def feed_weights(chunk):
        full = assemble(chunk).reshape(PLANE * DEPTH, 3, unit_part, features)
        full = jnp.transpose(full, (1, 0, 2, 3)).reshape(3, -1, features)
        return full[:2].reshape(-1, features), full[2]

    a0, p0 = far(a0), near(p0)
    a0, p0, q0 = together(a0, p0, q0)
    a0, p0, q0 = first(a0), far(p0), near(q0)
    a0, p0, q0, a1 = together(a0, p0, q0, a1)
    a0, p0, q0, a1 = second(a0), first(p0), far(q0), near(a1)
    a0, p0, q0, a1, p1 = together(a0, p0, q0, a1, p1)
    p0, q0, a1, p1 = second(p0), first(q0), far(a1), near(p1)
    attn0 = attn_weights(a0)
    projected0, context0, sum0, norm0 = attn_forward(start, attn0, norms[0], slopes, seqs)
    low0, p0, q0, a1, p1, q1 = together(norm0.astype(BF16), p0, q0, a1, p1, q1)
    q0, a1, p1, q1 = second(q0), first(a1), far(p1), near(q1)
    all0 = both_rows(low0)
    feed_p0 = feed_weights(p0)
    gated_p0, hidden_p0, mixed = feed_forward(all0, feed_p0)
    mixed, q0, a1, p1, q1 = together(mixed, q0, a1, p1, q1)
    a1, p1, q1 = second(a1), first(p1), far(q1)
    feed_q0 = feed_weights(q0)
    gated_q0, hidden_q0, more = feed_forward(all0, feed_q0)
    mixed = mixed + more
    mixed, a1, p1, q1 = together(mixed, a1, p1, q1)
    p1, q1 = second(p1), first(q1)
    attn1 = attn_weights(a1)
    total0 = norm0 + join_rows(mixed)
    middle_low = norm_rows(total0, norms[0][2], norms[0][3]).astype(BF16)
    projected1, context1, sum1, norm1 = attn_forward(middle_low, attn1, norms[1], slopes, seqs)
    low1, p1, q1 = together(norm1.astype(BF16), p1, q1)
    q1 = second(q1)
    all1 = both_rows(low1)
    feed_p1 = feed_weights(p1)
    gated_p1, hidden_p1, mixed = feed_forward(all1, feed_p1)
    mixed, q1 = together(mixed, q1)
    feed_q1 = feed_weights(q1)
    gated_q1, hidden_q1, more = feed_forward(all1, feed_q1)
    total1 = norm1 + join_rows(mixed + more)
    final_low = norm_rows(total1, norms[1][2], norms[1][3]).astype(BF16)

    def give(early, late):
        mine = jnp.where(is_first, early, late)
        got = swap(jnp.where(is_first, late, early))
        both = jnp.concatenate([jnp.where(is_first, mine, got), jnp.where(is_first, got, mine)])
        return both.reshape((1, micro, own_seqs, length, features))

    def feed_terms(gate_up, down):
        full = jnp.concatenate([gate_up, down]).reshape(3, PLANE, DEPTH, unit_part, features)
        full = jnp.transpose(full, (1, 2, 0, 3, 4)).reshape(PLANE, DEPTH, -1, features)
        return [full[e] for e in range(PLANE)]

    def attn_terms(qkv, out, vectors):
        spread = jnp.transpose(jnp.stack(vectors).reshape(4, DEPTH, local), (1, 0, 2)).reshape(DEPTH, features)
        spread = [lax.dynamic_index_in_dim(spread, jnp.bitwise_xor(depth, j), 0) for j in range(DEPTH)]
        spread = jnp.pad(jnp.concatenate(spread).astype(BF16), ((0, NORM_ROWS - DEPTH), (0, 0)))
        full = jnp.concatenate([qkv, out]).reshape(2, -1, features)
        full = jnp.concatenate([full, jnp.stack([spread, spread])], axis=1)
        keep = lax.dynamic_index_in_dim(full, core, 0, keepdims=False)
        return keep, swap(lax.dynamic_index_in_dim(full, 1 - core, 0, keepdims=False))

    def attn_pieces(pair):
        full = add_low(*pair)
        spread = full[-NORM_ROWS : DEPTH - NORM_ROWS]
        spread = jnp.broadcast_to(spread[None, :, None], (PLANE, DEPTH, NORM_ROWS, features))
        full = full[:-NORM_ROWS].reshape(2, DEPTH, local_heads, PLANE, part, features)
        full = jnp.transpose(full, (3, 1, 0, 2, 4, 5)).reshape(PLANE, DEPTH, -1, features)
        full = jnp.concatenate([full, spread], axis=2)
        return [full[e] for e in range(PLANE)]

    def hand_over(block, source):
        planes, depths = lax.axis_size("dp"), lax.axis_size("tensor")
        count = planes * depths
        pairs = [(source * count + i, (1 - source) * count + i) for i in range(count)]
        return lax.ppermute(block, AXES, pairs)

    second_grad, gain_two1, offset_two1 = norm_backward(total1, norms[1][2], norms[1][3], seed)
    mixed_all = both_rows(second_grad.astype(BF16))
    grad_p = feed_backward(mixed_all, feed_p1, gated_p1)
    p1 = feed_terms(*feed_weight_grads(mixed_all, all1, grad_p, hidden_p1))
    mixed_all, grad_p, p1 = together(mixed_all, grad_p, p1)

    p1_own, p1_half, p1_a, p1_b = reduce_open(p1)
    terms = dot(grad_p, feed_p1[0], 1, 0)
    grad_q = feed_backward(mixed_all, feed_q1, gated_q1)
    terms = terms + dot(grad_q, feed_q1[0], 1, 0)
    q1 = feed_terms(*feed_weight_grads(mixed_all, all1, grad_q, hidden_q1))
    layer_out = give(middle_low, final_low)
    terms, q1, p1_a, layer_out = together(terms, q1, p1_a, layer_out)

    p1_own, p1_c = reduce_turn((p1_own, p1_half, p1_a))
    first_grad = join_rows(terms) + second_grad
    sum_grad, gain_one1, offset_one1 = norm_backward(sum1, norms[1][0], norms[1][1], first_grad)
    context_grad, out = context_backward(sum_grad, attn1, context1)
    context_grad, out, q1, p1_b = together(context_grad, out, q1, p1_b)

    q1_own, q1_half, q1_a, q1_b = reduce_open(q1)
    projected_grad = attend_back(projected1, context_grad, slopes, seqs)
    qkv = dot(projected_grad, middle_low, 0, 0).astype(BF16)
    projected_grad, qkv, q1_a, p1_c = together(projected_grad, qkv, q1_a, p1_c)

    a1 = attn_terms(qkv, out, [gain_one1, offset_one1, gain_two1, offset_two1])
    q1_own, q1_c = reduce_turn((q1_own, q1_half, q1_a))
    p1 = reduce_near(p1_own, p1_c, p1_b)
    middle_grad = dot(projected_grad, attn1[0], 1, 0) + sum_grad
    second_grad, gain_two0, offset_two0 = norm_backward(total0, norms[0][2], norms[0][3], middle_grad)
    mixed_low = second_grad.astype(BF16)
    mixed_low, a1, q1_b, p1 = together(mixed_low, a1, q1_b, p1)

    mixed_all = both_rows(mixed_low)
    a1_own, a1_half, a1_a, a1_b = reduce_open(attn_pieces(a1))
    p1 = reduce_far(p1)
    grad_p = feed_backward(mixed_all, feed_p0, gated_p0)
    mixed_all, grad_p, a1_a, q1_c, p1 = together(mixed_all, grad_p, a1_a, q1_c, p1)

    a1_own, a1_c = reduce_turn((a1_own, a1_half, a1_a))
    q1 = reduce_near(q1_own, q1_c, q1_b)
    p0 = feed_terms(*feed_weight_grads(mixed_all, all0, grad_p, hidden_p0))
    terms = dot(grad_p, feed_p0[0], 1, 0)
    mixed_all, terms, p0, a1_b, q1 = together(mixed_all, terms, p0, a1_b, q1)

    p0_own, p0_half, p0_a, p0_b = reduce_open(p0)
    q1 = reduce_far(q1)
    grad_q = feed_backward(mixed_all, feed_q0, gated_q0)
    terms = terms + dot(grad_q, feed_q0[0], 1, 0)
    terms, grad_q, p0_a, a1_c, q1 = together(terms, grad_q, p0_a, a1_c, q1)

    p0_own, p0_c = reduce_turn((p0_own, p0_half, p0_a))
    a1 = reduce_near(a1_own, a1_c, a1_b)
    q0 = feed_terms(*feed_weight_grads(mixed_all, all0, grad_q, hidden_q0))
    first_grad = join_rows(terms) + second_grad
    sum_grad, gain_one0, offset_one0 = norm_backward(sum0, norms[0][0], norms[0][1], first_grad)
    sum_grad, q0, p0_b, a1 = together(sum_grad, q0, p0_b, a1)

    q0_own, q0_half, q0_a, q0_b = reduce_open(q0)
    a1 = reduce_far(a1)
    context_grad, out = context_backward(sum_grad, attn0, context0)
    projected_grad = attend_back(projected0, context_grad, slopes, seqs)
    qkv = dot(projected_grad, start, 0, 0).astype(BF16)
    projected_grad, qkv, out, q0_a, p0_c, a1 = together(projected_grad, qkv, out, q0_a, p0_c, a1)

    a0 = attn_terms(qkv, out, [gain_one0, offset_one0, gain_two0, offset_two0])
    q0_own, q0_c = reduce_turn((q0_own, q0_half, q0_a))
    p0 = reduce_near(p0_own, p0_c, p0_b)
    attn_late = reduce_last(a1)
    late = jnp.concatenate([reduce_last(p1), reduce_last(q1), attn_late[:-NORM_ROWS]])
    start_grad = dot(projected_grad, attn0[0], 1, 0) + sum_grad
    start_grad, late, a0, q0_b, p0 = together(start_grad, late, a0, q0_b, p0)

    a0_own, a0_half, a0_a, a0_b = reduce_open(attn_pieces(a0))
    p0 = reduce_far(p0)
    late_first = exchange(late, dp_masks=FIRST)
    late_got = [hand_over(late, 0)]
    a0_a, q0_c, p0, late_got = together(a0_a, q0_c, p0, late_got)

    a0_own, a0_c = reduce_turn((a0_own, a0_half, a0_a))
    q0 = reduce_near(q0_own, q0_c, q0_b)
    late_second = exchange(late, dp_masks=SECOND)
    input_grad = give(start_grad, middle_grad)
    a0_b, q0, late_first, input_grad = together(a0_b, q0, late_first, input_grad)

    q0 = reduce_far(q0)
    late_got.append(hand_over(late_first, 0))
    a0_c, q0, late_got = together(a0_c, q0, late_got)

    a0 = reduce_near(a0_own, a0_c, a0_b)
    late_third = exchange(late_first, dp_masks=SECOND)
    feed = jnp.concatenate([reduce_last(p0), reduce_last(q0)])
    feed_first = exchange(feed, dp_masks=FIRST)
    a0, late_second, feed = together(a0, late_second, feed)

    a0 = reduce_far(a0)
    feed_second = exchange(feed, dp_masks=SECOND)
    late_got.append(hand_over(late_second, 0))
    feed_got = [hand_over(feed, 1)]
    a0, feed_first, late_third, late_got, feed_got = together(a0, feed_first, late_third, late_got, feed_got)

    attn_early = reduce_last(a0)
    attn = attn_early[:-NORM_ROWS]
    attn_first, attn_second = exchange(attn, dp_masks=FIRST), exchange(attn, dp_masks=SECOND)
    feed_third = exchange(feed_first, dp_masks=SECOND)
    late_got.append(hand_over(late_third, 0))
    feed_got.append(hand_over(feed_first, 1))
    attn_first, feed_second, late_got, feed_got = together(attn_first, feed_second, late_got, feed_got)

    attn_third = exchange(attn_first, dp_masks=SECOND)
    feed_early = [feed, feed_first, feed_second, feed_third]
    feed_got = feed_got + [hand_over(feed_second, 1), hand_over(feed_third, 1)]
    attn_early_all = jnp.stack([attn, attn_first, attn_second, attn_third])
    attn_got = hand_over(attn_early_all, 1)

    feed_rows = FEED_CHUNKS * 3 * unit_part
    late = [late, late_first, late_second, late_third]
    early_half = [feed_early, [piece[:feed_rows] for piece in late_got]]
    late_half = [feed_got, [piece[:feed_rows] for piece in late]]
    flags = jnp.concatenate(
        [is_first.astype(jnp.int32)[None]] + [jnp.bitwise_xor(in_plane, order) for order in orders]
    )
    grad_in, grad_down = settle(
        early_half[0] + late_half[0] + early_half[1] + late_half[1], flags, FEED_CHUNKS, 3, unit_part
    )
    attn_late_all = jnp.stack([piece[feed_rows:] for piece in late])
    attn_late_got = jnp.stack([piece[feed_rows:] for piece in late_got])
    parts = [jnp.where(is_first, attn_early_all, attn_late_got), jnp.where(is_first, attn_got, attn_late_all)]
    attn_total = jnp.stack(
        [
            jnp.stack(
                [
                    lax.dynamic_index_in_dim(half, order[jnp.bitwise_xor(in_plane, index)], 0, keepdims=False)
                    for half, order in zip(parts, orders)
                ]
            )
            for index in range(PLANE)
        ]
    )
    attn_total = attn_total.reshape(PLANE, 2, 2, local_heads, part, features)
    attn_total = jnp.transpose(attn_total, (1, 2, 3, 0, 4, 5)).reshape(4, local, features).astype(F32)
    grad_qkv = jnp.transpose(attn_total[:3], (2, 0, 1))
    grad_out = attn_total[3]

    vectors = jnp.where(is_first, attn_early[-1], attn_late[-1]).astype(F32).reshape(4, local)

    return (
        layer_out,
        input_grad,
        grad_qkv[None],
        grad_out[None],
        grad_in[None],
        grad_down[None],
        vectors[0][None],
        vectors[1][None],
        vectors[2][None],
        vectors[3][None],
    )


def solution(mesh):
    placed = (
        P(None, ("dp", "tensor"), None, None),
        P(None, ("dp", "tensor"), None, None),
        P(None, ("dp", "tensor"), None),
        P("section", None, None, "tensor"),
        P("section", "tensor", None),
        P("section", None, None, "tensor"),
        P("section", "tensor", None),
        P("section", None),
        P("section", None),
        P("section", None),
        P("section", None),
    )
    return jax.shard_map(
        body,
        mesh=mesh,
        in_specs=placed,
        out_specs=(
            P("section", None, ("dp", "tensor"), None, None),
            P("section", None, ("dp", "tensor"), None, None),
            P("section", None, None, "tensor"),
            P("section", "tensor", None),
            P("section", None, None, "tensor"),
            P("section", "tensor", None),
            P("section", "tensor"),
            P("section", "tensor"),
            P("section", "tensor"),
            P("section", "tensor"),
        ),
        check_vma=False,
    )
```

```python
import functools
import math

import jax
import jax.numpy as jnp
import numpy as np
from jax import lax
from jax.experimental import pallas as pl
from jax.experimental.pallas import tpu as pltpu
from jax.sharding import PartitionSpec as P

HEADS = 12
HEAD_DIM = 64
NORM_EPSILON = 1e-05
AXES = ("section", "dp", "tensor")
FEED_CHUNKS = 2
NORM_ROWS = 16
LANES = 128
GROUP = 3
GROUP_BACK = 3

F32 = jnp.float32
BF16 = jnp.bfloat16


def power_slopes(total_heads):
    return [2.0 ** (-8.0 * (index + 1) / total_heads) for index in range(total_heads)]


def alibi_table(number_heads):
    closest = 2 ** int(math.floor(math.log2(number_heads)))
    slopes = power_slopes(closest)
    slopes = slopes + power_slopes(2 * closest)[0::2][: number_heads - closest]
    return np.array(slopes, dtype=np.float32)


def norm_rows(values, gain, offset):
    row_mean = jnp.mean(values, axis=-1, keepdims=True)
    centred = values - row_mean
    row_var = jnp.mean(centred * centred, axis=-1, keepdims=True)
    return centred * lax.rsqrt(row_var + NORM_EPSILON) * gain + offset


def gelu_product(gate_part, up_part):
    return jax.nn.gelu(gate_part, approximate=False) * up_part


def dot(a, b, ca, cb):
    return lax.dot_general(a, b, (((ca,), (cb,)), ((), ())), preferred_element_type=F32)


def exchange(block, section_mask=0, dp_masks=(0, 0), tensor_mask=0):
    dp = lax.axis_size("dp")
    tensor = lax.axis_size("tensor")
    pairs = []
    for s in range(lax.axis_size("section")):
        for d in range(dp):
            for t in range(tensor):
                target = ((s ^ section_mask) * dp + (d ^ dp_masks[s])) * tensor + (t ^ tensor_mask)
                pairs.append(((s * dp + d) * tensor + t, target))
    return lax.ppermute(block, AXES, pairs)


def swap(block):
    return exchange(block, section_mask=1)


FIRST = (1, 2)
SECOND = (2, 1)
PLANE = 4
DEPTH = 4


def contract(a, b, ca, cb):
    return lax.dot_general(a, b, (((ca,), (cb,)), ((), ())), preferred_element_type=F32)


def head_masks(length):
    lane = lax.broadcasted_iota(jnp.int32, (length, LANES), 1)
    return [lane // HEAD_DIM == index for index in range(LANES // HEAD_DIM)]


def distances(length):
    across = lax.broadcasted_iota(jnp.int32, (length, length), 0)
    along = lax.broadcasted_iota(jnp.int32, (length, length), 1)
    return jnp.abs(across - along).astype(F32)


def attend_kernel(group, slopes_ref, projected_ref, context_ref):
    length, features = context_ref.shape
    masks = head_masks(length)
    distance = distances(length)
    per = len(masks)
    pairs = features // LANES
    for first in range(0, pairs, group):
        heads = [(pair, index) for pair in range(first, first + group) for index in range(per)]
        parts = {p: [slice(i * features + p * LANES, i * features + (p + 1) * LANES) for i in range(3)] for p, _ in heads}
        scores = []
        for pair, index in heads:
            key = projected_ref[:, parts[pair][1]]
            own = jnp.where(masks[index], key, jnp.zeros_like(key))
            scores.append(contract(own, projected_ref[:, parts[pair][0]], 1, 1))
        weights = []
        for (pair, index), score in zip(heads, scores):
            score = score * HEAD_DIM ** (-0.5) - slopes_ref[pair * per + index] * distance
            weight = jnp.exp(score - jnp.max(score, axis=0, keepdims=True))
            weight = weight * (1.0 / jnp.sum(weight, axis=0, keepdims=True))
            weights.append(weight.astype(BF16))
        for pair in range(first, first + group):
            value = projected_ref[:, parts[pair][2]]
            context = jnp.zeros((length, LANES), F32)
            for (other, index), weight in zip(heads, weights):
                if other == pair:
                    context = jnp.where(masks[index], contract(weight, value, 0, 0), context)
            context_ref[:, parts[pair][0]] = context.astype(BF16)


def attend_back_kernel(group, slopes_ref, projected_ref, context_grad_ref, grad_ref):
    length, features = context_grad_ref.shape
    masks = head_masks(length)
    distance = distances(length)
    per = len(masks)
    pairs = features // LANES
    for first in range(0, pairs, group):
        heads = [(pair, index) for pair in range(first, first + group) for index in range(per)]
        parts = {p: [slice(i * features + p * LANES, i * features + (p + 1) * LANES) for i in range(3)] for p, _ in heads}
        scores, weights_grads = [], []
        for pair, index in heads:
            key, value = projected_ref[:, parts[pair][1]], projected_ref[:, parts[pair][2]]
            own = jnp.where(masks[index], key, jnp.zeros_like(key))
            scores.append(contract(own, projected_ref[:, parts[pair][0]], 1, 1))
            own = jnp.where(masks[index], value, jnp.zeros_like(value))
            weights_grads.append(contract(own, context_grad_ref[:, parts[pair][0]], 1, 1))
        weights, score_grads = [], []
        for (pair, index), score, weights_grad in zip(heads, scores, weights_grads):
            score = score * HEAD_DIM ** (-0.5) - slopes_ref[pair * per + index] * distance
            weight = jnp.exp(score - jnp.max(score, axis=0, keepdims=True))
            weight = weight * (1.0 / jnp.sum(weight, axis=0, keepdims=True))
            mean_grad = jnp.sum(weight * weights_grad, axis=0, keepdims=True)
            score_grads.append((weight * (weights_grad - mean_grad)).astype(BF16))
            weights.append(weight.astype(BF16))
        for pair in range(first, first + group):
            query, key = projected_ref[:, parts[pair][0]], projected_ref[:, parts[pair][1]]
            context_grad = context_grad_ref[:, parts[pair][0]]
            grads = [jnp.zeros((length, LANES), F32)] * 3
            for (other, index), weight, score_grad in zip(heads, weights, score_grads):
                if other == pair:
                    new = [
                        contract(score_grad, key, 0, 0) * HEAD_DIM ** (-0.5),
                        contract(score_grad, query, 1, 0) * HEAD_DIM ** (-0.5),
                        contract(weight, context_grad, 1, 0),
                    ]
                    grads = [jnp.where(masks[index], n, g) for n, g in zip(new, grads)]
            for part, grad in zip(parts[pair], grads):
                grad_ref[:, part] = grad.astype(BF16)


def row_block(length, width):
    return pl.BlockSpec((length, width), lambda index: (index, 0))


def attend(projected, slopes, seqs):
    rows, width = projected.shape
    length, features = rows // seqs, width // 3
    return pl.pallas_call(
        functools.partial(attend_kernel, GROUP),
        grid=(seqs,),
        in_specs=[pl.BlockSpec(memory_space=pltpu.SMEM), row_block(length, width)],
        out_specs=row_block(length, features),
        out_shape=jax.ShapeDtypeStruct((rows, features), BF16),
        cost_estimate=pl.CostEstimate(
            flops=4 * rows * length * features, bytes_accessed=2 * rows * (width + features), transcendentals=rows * length * features // HEAD_DIM
        ),
        name="attend",
    )(slopes, projected)


def attend_back(projected, context_grad, slopes, seqs):
    rows, width = projected.shape
    length, features = rows // seqs, width // 3
    return pl.pallas_call(
        functools.partial(attend_back_kernel, GROUP_BACK),
        grid=(seqs,),
        in_specs=[
            pl.BlockSpec(memory_space=pltpu.SMEM),
            row_block(length, width),
            row_block(length, features),
        ],
        out_specs=row_block(length, width),
        out_shape=jax.ShapeDtypeStruct((rows, width), BF16),
        cost_estimate=pl.CostEstimate(
            flops=10 * rows * length * features, bytes_accessed=2 * rows * (2 * width + features), transcendentals=rows * length * features // HEAD_DIM
        ),
        name="attend_back",
    )(slopes, projected, context_grad)


def settle_kernel(chunks, kinds, part, flags_ref, *refs):
    *pieces, gate_up_ref, down_ref, held = refs
    first = flags_ref[0] == 1
    count = len(pieces) // 4
    half_rows = chunks * count * part
    for half in range(2):
        for index in range(count):
            mine = pieces[half * count + index]
            other = pieces[(2 + half) * count + index]
            place = flags_ref[1 + half * count + index]
            for chunk in range(chunks):
                base = pl.multiple_of(half * half_rows + chunk * count * part + place * part, part)
                for kind in range(kinds):
                    start = (chunk * kinds + kind) * part
                    rows = jnp.where(first, mine[start : start + part, :], other[start : start + part, :]).astype(F32)
                    if kind < kinds - 1:
                        held[kind, pl.ds(base, part), :] = rows
                    else:
                        down_ref[pl.ds(base, part), :] = rows
    for kind in range(kinds - 1):
        gate_up_ref[:, kind, :] = jnp.transpose(held[kind])


def settle(pieces, flags, chunks, kinds, part):
    rows, features = pieces[0].shape
    units = 2 * (len(pieces) // 4) * chunks * part
    width = 2 * LANES
    return pl.pallas_call(
        functools.partial(settle_kernel, chunks, kinds, part),
        grid=(features // width,),
        in_specs=[pl.BlockSpec(memory_space=pltpu.SMEM)]
        + [pl.BlockSpec((rows, width), lambda index: (0, index))] * len(pieces),
        out_specs=[
            pl.BlockSpec((width, kinds - 1, units), lambda index: (index, 0, 0)),
            pl.BlockSpec((units, width), lambda index: (0, index)),
        ],
        out_shape=[
            jax.ShapeDtypeStruct((features, kinds - 1, units), F32),
            jax.ShapeDtypeStruct((units, features), F32),
        ],
        scratch_shapes=[pltpu.VMEM((kinds - 1, units, width), F32)],
        name="settle",
    )(flags, *pieces)


def together(*trees):
    return lax.optimization_barrier(trees)


def first(chunk):
    depth, every = lax.axis_index("tensor"), chunk["every"]
    remote = jnp.stack([jnp.where(j < depth, every[j], every[j + 1]) for j in range(DEPTH - 1)])
    return dict(
        chunk,
        first=exchange(remote, dp_masks=FIRST),
        second=exchange(remote, dp_masks=SECOND),
    )


def by_depth(rest):
    depth = lax.axis_index("tensor")
    for mask in (1, 2):
        crossed = jnp.bitwise_and(depth, mask) != 0
        rest = [jnp.where(crossed, rest[j ^ mask], rest[j]) for j in range(DEPTH)]
    return jnp.stack(rest)


def second(chunk):
    return dict(chunk, third=exchange(chunk["first"], dp_masks=SECOND))


def with_own(own, rest):
    depth = lax.axis_index("tensor")
    before = [rest[min(j, DEPTH - 2)] for j in range(DEPTH)]
    after = [rest[max(j - 1, 0)] for j in range(DEPTH)]
    return jnp.stack(
        [jnp.where(j == depth, own, jnp.where(j < depth, b, a)) for j, b, a in zip(range(DEPTH), before, after)]
    )


def assemble(chunk):
    rest = [chunk["first"], chunk["second"], chunk["third"]]
    return jnp.stack([chunk["every"]] + [with_own(own, r) for own, r in zip(chunk["own"][1:], rest)])


def add_low(a, b):
    return (a.astype(F32) + b.astype(F32)).astype(BF16)


def total_low(*parts):
    return sum(part.astype(F32) for part in parts).astype(BF16)


def reduce_open(terms):
    return (
        terms[0],
        terms[1],
        exchange(terms[3], dp_masks=SECOND),
        exchange(terms[2], dp_masks=SECOND),
    )


def reduce_turn(parts):
    return parts[0], exchange(total_low(parts[1], parts[2]), dp_masks=FIRST)


def reduce_along(own, turned, opened):
    return lax.psum_scatter(total_low(own, turned, opened), "tensor", scatter_dimension=0)


def reduce_near(own, turned, opened):
    pairs = total_low(own, turned, opened)
    pairs = pairs.reshape((2, 2) + pairs.shape[1:])
    odd = lax.axis_index("tensor") % 2 == 1
    keep = jnp.where(odd, pairs[:, 1], pairs[:, 0])
    return keep, exchange(jnp.where(odd, pairs[:, 0], pairs[:, 1]), tensor_mask=1)


def reduce_far(pair):
    terms = total_low(*pair)
    upper = lax.axis_index("tensor") // 2 == 1
    keep = jnp.where(upper, terms[1], terms[0])
    return keep, exchange(jnp.where(upper, terms[0], terms[1]), tensor_mask=2)


def reduce_last(*parts):
    one = total_low(*parts)
    mask = PLANE
    while mask < lax.axis_size("dp"):
        one = total_low(one, exchange(one, dp_masks=(mask, mask)))
        mask *= 2
    return one


def attn_forward(own_low, weights, norms, slopes, seqs):
    wqkv, wo = weights
    projected = dot(own_low, wqkv, 1, 1).astype(BF16)
    context = attend(projected, slopes, seqs)
    first_sum = own_low.astype(F32) + dot(context, wo, 1, 0)
    first_norm = norm_rows(first_sum, norms[0], norms[1])
    return projected, context, first_sum, first_norm


def both_rows(rows_low):
    return jnp.concatenate([rows_low, swap(rows_low)])


def join_rows(terms):
    rows = terms.shape[0] // 2
    return terms[:rows] + swap(terms[rows:].astype(BF16)).astype(F32)


def feed_forward(first_all, weights):
    gate_up, down = weights
    gated = dot(first_all, gate_up, 1, 1)
    gate_part, up_part = jnp.split(gated, 2, axis=-1)
    hidden = gelu_product(gate_part, up_part).astype(BF16)
    return gated, hidden, dot(hidden, down, 1, 0)


def feed_backward(mixed_all, weights, gated):
    hidden_grad = dot(mixed_all, weights[1], 1, 1)
    gate_part, up_part = jnp.split(gated, 2, axis=-1)
    _, gelu_back = jax.vjp(gelu_product, gate_part, up_part)
    gate_grad, up_grad = gelu_back(hidden_grad)
    return jnp.concatenate([gate_grad, up_grad], axis=-1).astype(BF16)


def feed_weight_grads(mixed_all, first_all, gated_grad, hidden):
    return dot(gated_grad, first_all, 0, 0).astype(BF16), dot(hidden, mixed_all, 0, 0).astype(BF16)


def norm_backward(total, gain, offset, grad):
    _, back = jax.vjp(norm_rows, total, gain, offset)
    return back(grad)


def context_backward(sum_grad, weights, context):
    attended_low = sum_grad.astype(BF16)
    context_grad = dot(attended_low, weights[1], 1, 1).astype(BF16)
    return context_grad, dot(context, attended_low, 0, 0).astype(BF16)


def body(
    layer_input,
    out_grad,
    loss_mask,
    query_key_value_weight,
    attention_output_weight,
    gate_up_weight,
    down_weight,
    norm1_gain,
    norm1_bias,
    norm2_gain,
    norm2_bias,
):
    core = lax.axis_index("section")
    plane = lax.axis_index("dp")
    depth = lax.axis_index("tensor")
    is_first = core == 0
    micro, own_seqs, length, features = layer_input.shape
    local = query_key_value_weight.shape[-1]
    local_heads = local // HEAD_DIM
    units = down_weight.shape[1]
    part = HEAD_DIM // PLANE
    unit_part = units // 2 // PLANE // FEED_CHUNKS
    seqs = micro * own_seqs // 2
    rows = seqs * length

    orders = [jnp.array([0, 1, 2, 3]), jnp.array([0, 2, 1, 3])]
    steps = jnp.where(is_first, orders[0], orders[1])
    in_plane = jnp.bitwise_and(plane, PLANE - 1)

    def relative(slab):
        return [
            lax.dynamic_index_in_dim(slab, jnp.bitwise_xor(in_plane, steps[e]), 0, keepdims=False)
            for e in range(PLANE)
        ]

    def share(slab):
        keep = lax.dynamic_index_in_dim(slab, core, 0, keepdims=False)
        got = swap(lax.dynamic_index_in_dim(slab, 1 - core, 0, keepdims=False))
        return jnp.where(is_first, keep, got), jnp.where(is_first, got, keep)

    def along(slab):
        return lax.all_gather(slab, "tensor")

    qkv_rows = jnp.transpose(query_key_value_weight[0], (1, 2, 0))
    attn_rows = jnp.concatenate([qkv_rows, attention_output_weight], axis=0)
    attn_slab = attn_rows.reshape(2, 2, local_heads, PLANE, part, features)
    attn_slab = jnp.transpose(attn_slab, (0, 3, 1, 2, 4, 5)).reshape(2, PLANE, -1, features)
    attn_in = [{"own": relative(own)} for own in share(attn_slab)]
    a0, a1 = attn_in
    mine = a0["own"][0]
    beside = exchange(mine, tensor_mask=1)
    mine, beside, gate_up_weight, down_weight = together(mine, beside, gate_up_weight, down_weight)
    gate_up_rows = jnp.transpose(gate_up_weight[0], (1, 2, 0))
    feed_rows = jnp.concatenate([gate_up_rows, down_weight], axis=0)
    feed_slab = feed_rows.reshape(3, 2, FEED_CHUNKS, PLANE, unit_part, features)
    feed_slab = jnp.transpose(feed_slab, (2, 1, 3, 0, 4, 5)).reshape(FEED_CHUNKS, 2, PLANE, -1, features)

    feed_in = [[{"own": relative(own)} for own in share(feed_slab[k])] for k in range(FEED_CHUNKS)]
    (p0, p1), (q0, q1) = feed_in

    norm_table = jnp.concatenate([norm1_gain, norm1_bias, norm2_gain, norm2_bias])
    norm_other = swap(norm_table)
    norm_first = jnp.where(is_first, norm_table, norm_other)
    norm_second = jnp.where(is_first, norm_other, norm_table)
    norms = [tuple(table[i] for i in range(4)) for table in (norm_first, norm_second)]

    slopes = jnp.asarray(alibi_table(HEADS))

    def own_half(whole):
        flat = whole.reshape((2, rows) + whole.shape[3:])
        return lax.dynamic_index_in_dim(flat, core, 0, keepdims=False)

    start = own_half(layer_input)
    seed = own_half(out_grad).astype(F32) * own_half(loss_mask).astype(F32)[..., None]


    def attn_weights(chunk):
        full = assemble(chunk).reshape(PLANE, DEPTH, 2, local_heads, part, features)
        mine = jnp.transpose(full, (2, 1, 3, 0, 4, 5)).reshape(2, -1, features)
        other = swap(mine)
        qk = jnp.where(is_first, mine, other)
        vo = jnp.where(is_first, other, mine)
        wqkv = jnp.concatenate([qk.reshape(-1, features), vo[0]])
        return wqkv, vo[1]

    def feed_weights(chunk):
        full = assemble(chunk).reshape(PLANE * DEPTH, 3, unit_part, features)
        full = jnp.transpose(full, (1, 0, 2, 3)).reshape(3, -1, features)
        return full[:2].reshape(-1, features), full[2]

    def along_all(*chunks):
        return along(jnp.concatenate([chunk["own"][0] for chunk in chunks]))

    def cut(every, *chunks):
        done = []
        for chunk in chunks:
            rows_here = chunk["own"][0].shape[0]
            done.append(dict(chunk, every=every[:, :rows_here]))
            every = every[:, rows_here:]
        return done

    beyond = exchange(jnp.stack([mine, beside]), tensor_mask=2)
    p0, q0, a1, beyond, mine, beside = together(p0, q0, a1, beyond, mine, beside)
    every0 = along_all(p0, q0, a1)
    a0["every"] = by_depth([mine, beside, beyond[0], beyond[1]])
    a0 = first(a0)
    (a0,) = together(a0)
    a0 = second(a0)
    a0, every0, p1, q1 = together(a0, every0, p1, q1)
    p0, q0, a1 = cut(every0, p0, q0, a1)
    p0 = first(p0)
    every1 = along_all(p1, q1)
    attn0 = attn_weights(a0)
    projected0, context0, sum0, norm0 = attn_forward(start, attn0, norms[0], slopes, seqs)
    low0, p0 = together(norm0.astype(BF16), p0)
    p0, q0 = second(p0), first(q0)
    all0 = both_rows(low0)
    all0, p0 = together(all0, p0)
    feed_p0 = feed_weights(p0)
    gated_p0, hidden_p0, mixed = feed_forward(all0, feed_p0)
    mixed, q0 = together(mixed, q0)
    q0, a1 = second(q0), first(a1)
    feed_q0 = feed_weights(q0)
    gated_q0, hidden_q0, more = feed_forward(all0, feed_q0)
    mixed = mixed + more
    mixed, a1, every1 = together(mixed, a1, every1)
    p1, q1 = cut(every1, p1, q1)
    a1, p1, q1 = second(a1), first(p1), first(q1)
    attn1 = attn_weights(a1)
    total0 = norm0 + join_rows(mixed)
    middle_low = norm_rows(total0, norms[0][2], norms[0][3]).astype(BF16)
    projected1, context1, sum1, norm1 = attn_forward(middle_low, attn1, norms[1], slopes, seqs)
    low1, p1, q1 = together(norm1.astype(BF16), p1, q1)
    p1, q1 = second(p1), second(q1)
    all1 = both_rows(low1)
    all1, p1 = together(all1, p1)
    feed_p1 = feed_weights(p1)
    gated_p1, hidden_p1, mixed = feed_forward(all1, feed_p1)
    mixed, q1 = together(mixed, q1)
    feed_q1 = feed_weights(q1)
    gated_q1, hidden_q1, more = feed_forward(all1, feed_q1)
    total1 = norm1 + join_rows(mixed + more)
    final_low = norm_rows(total1, norms[1][2], norms[1][3]).astype(BF16)

    def give(early, late):
        mine = jnp.where(is_first, early, late)
        got = swap(jnp.where(is_first, late, early))
        both = jnp.concatenate([jnp.where(is_first, mine, got), jnp.where(is_first, got, mine)])
        return both.reshape((1, micro, own_seqs, length, features))

    def feed_terms(gate_up, down):
        full = jnp.concatenate([gate_up, down]).reshape(3, PLANE, DEPTH, unit_part, features)
        full = jnp.transpose(full, (1, 2, 0, 3, 4)).reshape(PLANE, DEPTH, -1, features)
        return [full[e] for e in range(PLANE)]

    def attn_terms(qkv, out, vectors):
        spread = jnp.pad(jnp.stack(vectors).astype(BF16), ((0, NORM_ROWS - len(vectors)), (0, 0)))
        full = jnp.concatenate([qkv, out]).reshape(2, -1, features)
        full = jnp.concatenate([full, jnp.stack([spread, spread])], axis=1)
        keep = lax.dynamic_index_in_dim(full, core, 0, keepdims=False)
        return keep, swap(lax.dynamic_index_in_dim(full, 1 - core, 0, keepdims=False))

    def attn_pieces(pair):
        full = add_low(*pair)
        spread = jnp.broadcast_to(full[-NORM_ROWS:], (PLANE, DEPTH, NORM_ROWS, features))
        full = full[:-NORM_ROWS].reshape(2, DEPTH, local_heads, PLANE, part, features)
        full = jnp.transpose(full, (3, 1, 0, 2, 4, 5)).reshape(PLANE, DEPTH, -1, features)
        full = jnp.concatenate([full, spread], axis=2)
        return [full[e] for e in range(PLANE)]

    def hand_over(block, source):
        planes, depths = lax.axis_size("dp"), lax.axis_size("tensor")
        count = planes * depths
        pairs = [(source * count + i, (1 - source) * count + i) for i in range(count)]
        return lax.ppermute(block, AXES, pairs)

    second_grad, gain_two1, offset_two1 = norm_backward(total1, norms[1][2], norms[1][3], seed)
    mixed_all = both_rows(second_grad.astype(BF16))
    grad_p = feed_backward(mixed_all, feed_p1, gated_p1)
    p1 = feed_terms(*feed_weight_grads(mixed_all, all1, grad_p, hidden_p1))
    mixed_all, grad_p, p1 = together(mixed_all, grad_p, p1)

    p1_own, p1_half, p1_a, p1_b = reduce_open(p1)
    terms = dot(grad_p, feed_p1[0], 1, 0)
    grad_q = feed_backward(mixed_all, feed_q1, gated_q1)
    terms = terms + dot(grad_q, feed_q1[0], 1, 0)
    q1 = feed_terms(*feed_weight_grads(mixed_all, all1, grad_q, hidden_q1))
    layer_out = give(middle_low, final_low)
    terms, q1, p1_a, layer_out = together(terms, q1, p1_a, layer_out)

    p1_own, p1_c = reduce_turn((p1_own, p1_half, p1_a))
    first_grad = join_rows(terms) + second_grad
    sum_grad, gain_one1, offset_one1 = norm_backward(sum1, norms[1][0], norms[1][1], first_grad)
    context_grad, out = context_backward(sum_grad, attn1, context1)
    context_grad, out, q1, p1_b = together(context_grad, out, q1, p1_b)

    q1_own, q1_half, q1_a, q1_b = reduce_open(q1)
    projected_grad = attend_back(projected1, context_grad, slopes, seqs)
    qkv = dot(projected_grad, middle_low, 0, 0).astype(BF16)
    projected_grad, qkv, q1_a, p1_c = together(projected_grad, qkv, q1_a, p1_c)

    a1 = attn_terms(qkv, out, [gain_one1, offset_one1, gain_two1, offset_two1])
    q1_own, q1_c = reduce_turn((q1_own, q1_half, q1_a))
    p1 = reduce_along(p1_own, p1_c, p1_b)
    middle_grad = dot(projected_grad, attn1[0], 1, 0) + sum_grad
    second_grad, gain_two0, offset_two0 = norm_backward(total0, norms[0][2], norms[0][3], middle_grad)
    mixed_low = second_grad.astype(BF16)
    mixed_low, a1, q1_b = together(mixed_low, a1, q1_b)

    mixed_all = both_rows(mixed_low)
    a1_own, a1_half, a1_a, a1_b = reduce_open(attn_pieces(a1))
    grad_p = feed_backward(mixed_all, feed_p0, gated_p0)
    mixed_all, grad_p, a1_a, q1_c = together(mixed_all, grad_p, a1_a, q1_c)

    a1_own, a1_c = reduce_turn((a1_own, a1_half, a1_a))
    q1 = reduce_along(q1_own, q1_c, q1_b)
    p0 = feed_terms(*feed_weight_grads(mixed_all, all0, grad_p, hidden_p0))
    terms = dot(grad_p, feed_p0[0], 1, 0)
    mixed_all, terms, p0, a1_b = together(mixed_all, terms, p0, a1_b)

    p0_own, p0_half, p0_a, p0_b = reduce_open(p0)
    grad_q = feed_backward(mixed_all, feed_q0, gated_q0)
    terms = terms + dot(grad_q, feed_q0[0], 1, 0)
    terms, grad_q, p0_a, a1_c, p1 = together(terms, grad_q, p0_a, a1_c, p1)

    p0_own, p0_c = reduce_turn((p0_own, p0_half, p0_a))
    a1 = reduce_along(a1_own, a1_c, a1_b)
    q0 = feed_terms(*feed_weight_grads(mixed_all, all0, grad_q, hidden_q0))
    first_grad = join_rows(terms) + second_grad
    sum_grad, gain_one0, offset_one0 = norm_backward(sum0, norms[0][0], norms[0][1], first_grad)
    sum_grad, q0, p0_b = together(sum_grad, q0, p0_b)

    q0_own, q0_half, q0_a, q0_b = reduce_open(q0)
    context_grad, out = context_backward(sum_grad, attn0, context0)
    projected_grad = attend_back(projected0, context_grad, slopes, seqs)
    qkv = dot(projected_grad, start, 0, 0).astype(BF16)
    projected_grad, qkv, out, q0_a, p0_c, q1 = together(projected_grad, qkv, out, q0_a, p0_c, q1)

    a0 = attn_terms(qkv, out, [gain_one0, offset_one0, gain_two0, offset_two0])
    q0_own, q0_c = reduce_turn((q0_own, q0_half, q0_a))
    p0 = reduce_along(p0_own, p0_c, p0_b)
    start_grad = dot(projected_grad, attn0[0], 1, 0) + sum_grad
    start_grad, a1, a0, q0_b = together(start_grad, a1, a0, q0_b)

    a0_own, a0_half, a0_a, a0_b = reduce_open(attn_pieces(a0))
    attn_late = reduce_last(a1)
    late = jnp.concatenate([reduce_last(p1), reduce_last(q1), attn_late[:-NORM_ROWS]])
    late_first = exchange(late, dp_masks=FIRST)
    late_got = [hand_over(late, 0)]
    a0_a, q0_c, late_got = together(a0_a, q0_c, late_got)

    a0_own, a0_c = reduce_turn((a0_own, a0_half, a0_a))
    q0 = reduce_along(q0_own, q0_c, q0_b)
    late_second = exchange(late, dp_masks=SECOND)
    input_grad = give(start_grad, middle_grad)
    a0_b, late_first, input_grad = together(a0_b, late_first, input_grad)

    late_got.append(hand_over(late_first, 0))
    a0_c, late_got, p0 = together(a0_c, late_got, p0)

    a0 = reduce_near(a0_own, a0_c, a0_b)
    late_third = exchange(late_first, dp_masks=SECOND)
    a0, late_second, q0 = together(a0, late_second, q0)

    a0 = reduce_far(a0)
    feed = jnp.concatenate([reduce_last(p0), reduce_last(q0)])
    feed_first = exchange(feed, dp_masks=FIRST)
    feed_second = exchange(feed, dp_masks=SECOND)
    late_got.append(hand_over(late_second, 0))
    feed_got = [hand_over(feed, 1)]
    a0, feed_first, late_third, late_got, feed_got = together(a0, feed_first, late_third, late_got, feed_got)

    attn_early = reduce_last(*a0)
    attn = attn_early[:-NORM_ROWS]
    attn_first, attn_second = exchange(attn, dp_masks=FIRST), exchange(attn, dp_masks=SECOND)
    feed_third = exchange(feed_first, dp_masks=SECOND)
    late_got.append(hand_over(late_third, 0))
    feed_got.append(hand_over(feed_first, 1))
    attn_first, attn_second, feed_second, late_got, feed_got = together(
        attn_first, attn_second, feed_second, late_got, feed_got
    )

    attn_third = exchange(attn_first, dp_masks=SECOND)
    feed_early = [feed, feed_first, feed_second, feed_third]
    feed_got = feed_got + [hand_over(feed_second, 1), hand_over(feed_third, 1)]
    attn_early_all = jnp.stack([attn, attn_first, attn_second, attn_third])
    attn_got = hand_over(attn_early_all, 1)

    feed_rows = FEED_CHUNKS * 3 * unit_part
    late = [late, late_first, late_second, late_third]
    early_half = [feed_early, [piece[:feed_rows] for piece in late_got]]
    late_half = [feed_got, [piece[:feed_rows] for piece in late]]
    flags = jnp.concatenate(
        [is_first.astype(jnp.int32)[None]] + [jnp.bitwise_xor(in_plane, order) for order in orders]
    )
    grad_in, grad_down = settle(
        early_half[0] + late_half[0] + early_half[1] + late_half[1], flags, FEED_CHUNKS, 3, unit_part
    )
    attn_late_all = jnp.stack([piece[feed_rows:] for piece in late])
    attn_late_got = jnp.stack([piece[feed_rows:] for piece in late_got])
    parts = [jnp.where(is_first, attn_early_all, attn_late_got), jnp.where(is_first, attn_got, attn_late_all)]
    attn_total = jnp.stack(
        [
            jnp.stack(
                [
                    lax.dynamic_index_in_dim(half, order[jnp.bitwise_xor(in_plane, index)], 0, keepdims=False)
                    for half, order in zip(parts, orders)
                ]
            )
            for index in range(PLANE)
        ]
    )
    attn_total = attn_total.reshape(PLANE, 2, 2, local_heads, part, features)
    attn_total = jnp.transpose(attn_total, (1, 2, 3, 0, 4, 5)).reshape(4, local, features).astype(F32)
    grad_qkv = jnp.transpose(attn_total[:3], (2, 0, 1))
    grad_out = attn_total[3]

    vectors = jnp.where(is_first, attn_early[-NORM_ROWS:], attn_late[-NORM_ROWS:]).astype(F32)
    vectors = lax.dynamic_slice_in_dim(vectors, depth * local, local, 1)

    return (
        layer_out,
        input_grad,
        grad_qkv[None],
        grad_out[None],
        grad_in[None],
        grad_down[None],
        vectors[0][None],
        vectors[1][None],
        vectors[2][None],
        vectors[3][None],
    )


def solution(mesh):
    placed = (
        P(None, ("dp", "tensor"), None, None),
        P(None, ("dp", "tensor"), None, None),
        P(None, ("dp", "tensor"), None),
        P("section", None, None, "tensor"),
        P("section", "tensor", None),
        P("section", None, None, "tensor"),
        P("section", "tensor", None),
        P("section", None),
        P("section", None),
        P("section", None),
        P("section", None),
    )
    return jax.shard_map(
        body,
        mesh=mesh,
        in_specs=placed,
        out_specs=(
            P("section", None, ("dp", "tensor"), None, None),
            P("section", None, ("dp", "tensor"), None, None),
            P("section", None, None, "tensor"),
            P("section", "tensor", None),
            P("section", None, None, "tensor"),
            P("section", "tensor", None),
            P("section", "tensor"),
            P("section", "tensor"),
            P("section", "tensor"),
            P("section", "tensor"),
        ),
        check_vma=False,
    )
```

```python
import functools
import math

import jax
import jax.numpy as jnp
import numpy as np
from jax import lax
from jax.experimental import pallas as pl
from jax.experimental.pallas import tpu as pltpu
from jax.sharding import PartitionSpec as P

HEADS = 12
HEAD_DIM = 64
NORM_EPSILON = 1e-05
AXES = ("section", "dp", "tensor")
FEED_CHUNKS = 2
NORM_ROWS = 16
LANES = 128
GROUP = 3
GROUP_BACK = 3

F32 = jnp.float32
BF16 = jnp.bfloat16


def power_slopes(total_heads):
    return [2.0 ** (-8.0 * (index + 1) / total_heads) for index in range(total_heads)]


def alibi_table(number_heads):
    closest = 2 ** int(math.floor(math.log2(number_heads)))
    slopes = power_slopes(closest)
    slopes = slopes + power_slopes(2 * closest)[0::2][: number_heads - closest]
    return np.array(slopes, dtype=np.float32)


def norm_rows(values, gain, offset):
    row_mean = jnp.mean(values, axis=-1, keepdims=True)
    centred = values - row_mean
    row_var = jnp.mean(centred * centred, axis=-1, keepdims=True)
    return centred * lax.rsqrt(row_var + NORM_EPSILON) * gain + offset


def gelu_product(gate_part, up_part):
    return jax.nn.gelu(gate_part, approximate=False) * up_part


def dot(a, b, ca, cb):
    return lax.dot_general(a, b, (((ca,), (cb,)), ((), ())), preferred_element_type=F32)


def exchange(block, section_mask=0, dp_masks=(0, 0), tensor_mask=0):
    dp = lax.axis_size("dp")
    tensor = lax.axis_size("tensor")
    pairs = []
    for s in range(lax.axis_size("section")):
        for d in range(dp):
            for t in range(tensor):
                target = ((s ^ section_mask) * dp + (d ^ dp_masks[s])) * tensor + (t ^ tensor_mask)
                pairs.append(((s * dp + d) * tensor + t, target))
    return lax.ppermute(block, AXES, pairs)


def swap(block):
    return exchange(block, section_mask=1)


FIRST = (1, 2)
SECOND = (2, 1)
PLANE = 4
DEPTH = 4


def contract(a, b, ca, cb):
    return lax.dot_general(a, b, (((ca,), (cb,)), ((), ())), preferred_element_type=F32)


def head_masks(length):
    lane = lax.broadcasted_iota(jnp.int32, (length, LANES), 1)
    return [lane // HEAD_DIM == index for index in range(LANES // HEAD_DIM)]


def distances(length):
    across = lax.broadcasted_iota(jnp.int32, (length, length), 0)
    along = lax.broadcasted_iota(jnp.int32, (length, length), 1)
    return jnp.abs(across - along).astype(F32)


def attend_kernel(group, slopes_ref, projected_ref, context_ref):
    length, features = context_ref.shape
    masks = head_masks(length)
    distance = distances(length)
    per = len(masks)
    pairs = features // LANES
    for first in range(0, pairs, group):
        heads = [(pair, index) for pair in range(first, first + group) for index in range(per)]
        parts = {p: [slice(i * features + p * LANES, i * features + (p + 1) * LANES) for i in range(3)] for p, _ in heads}
        scores = []
        for pair, index in heads:
            key = projected_ref[:, parts[pair][1]]
            own = jnp.where(masks[index], key, jnp.zeros_like(key))
            scores.append(contract(own, projected_ref[:, parts[pair][0]], 1, 1))
        weights = []
        for (pair, index), score in zip(heads, scores):
            score = score * HEAD_DIM ** (-0.5) - slopes_ref[pair * per + index] * distance
            weight = jnp.exp(score - jnp.max(score, axis=0, keepdims=True))
            weight = weight * (1.0 / jnp.sum(weight, axis=0, keepdims=True))
            weights.append(weight.astype(BF16))
        for pair in range(first, first + group):
            value = projected_ref[:, parts[pair][2]]
            context = jnp.zeros((length, LANES), F32)
            for (other, index), weight in zip(heads, weights):
                if other == pair:
                    context = jnp.where(masks[index], contract(weight, value, 0, 0), context)
            context_ref[:, parts[pair][0]] = context.astype(BF16)


def attend_back_kernel(group, slopes_ref, projected_ref, context_grad_ref, grad_ref):
    length, features = context_grad_ref.shape
    masks = head_masks(length)
    distance = distances(length)
    per = len(masks)
    pairs = features // LANES
    for first in range(0, pairs, group):
        heads = [(pair, index) for pair in range(first, first + group) for index in range(per)]
        parts = {p: [slice(i * features + p * LANES, i * features + (p + 1) * LANES) for i in range(3)] for p, _ in heads}
        scores, weights_grads = [], []
        for pair, index in heads:
            key, value = projected_ref[:, parts[pair][1]], projected_ref[:, parts[pair][2]]
            own = jnp.where(masks[index], key, jnp.zeros_like(key))
            scores.append(contract(own, projected_ref[:, parts[pair][0]], 1, 1))
            own = jnp.where(masks[index], value, jnp.zeros_like(value))
            weights_grads.append(contract(own, context_grad_ref[:, parts[pair][0]], 1, 1))
        weights, score_grads = [], []
        for (pair, index), score, weights_grad in zip(heads, scores, weights_grads):
            score = score * HEAD_DIM ** (-0.5) - slopes_ref[pair * per + index] * distance
            weight = jnp.exp(score - jnp.max(score, axis=0, keepdims=True))
            weight = weight * (1.0 / jnp.sum(weight, axis=0, keepdims=True))
            mean_grad = jnp.sum(weight * weights_grad, axis=0, keepdims=True)
            score_grads.append((weight * (weights_grad - mean_grad)).astype(BF16))
            weights.append(weight.astype(BF16))
        for pair in range(first, first + group):
            query, key = projected_ref[:, parts[pair][0]], projected_ref[:, parts[pair][1]]
            context_grad = context_grad_ref[:, parts[pair][0]]
            grads = [jnp.zeros((length, LANES), F32)] * 3
            for (other, index), weight, score_grad in zip(heads, weights, score_grads):
                if other == pair:
                    new = [
                        contract(score_grad, key, 0, 0) * HEAD_DIM ** (-0.5),
                        contract(score_grad, query, 1, 0) * HEAD_DIM ** (-0.5),
                        contract(weight, context_grad, 1, 0),
                    ]
                    grads = [jnp.where(masks[index], n, g) for n, g in zip(new, grads)]
            for part, grad in zip(parts[pair], grads):
                grad_ref[:, part] = grad.astype(BF16)


def row_block(length, width):
    return pl.BlockSpec((length, width), lambda index: (index, 0))


def attend(projected, slopes, seqs):
    rows, width = projected.shape
    length, features = rows // seqs, width // 3
    return pl.pallas_call(
        functools.partial(attend_kernel, GROUP),
        grid=(seqs,),
        in_specs=[pl.BlockSpec(memory_space=pltpu.SMEM), row_block(length, width)],
        out_specs=row_block(length, features),
        out_shape=jax.ShapeDtypeStruct((rows, features), BF16),
        cost_estimate=pl.CostEstimate(
            flops=4 * rows * length * features, bytes_accessed=2 * rows * (width + features), transcendentals=rows * length * features // HEAD_DIM
        ),
        name="attend",
    )(slopes, projected)


def attend_back(projected, context_grad, slopes, seqs):
    rows, width = projected.shape
    length, features = rows // seqs, width // 3
    return pl.pallas_call(
        functools.partial(attend_back_kernel, GROUP_BACK),
        grid=(seqs,),
        in_specs=[
            pl.BlockSpec(memory_space=pltpu.SMEM),
            row_block(length, width),
            row_block(length, features),
        ],
        out_specs=row_block(length, width),
        out_shape=jax.ShapeDtypeStruct((rows, width), BF16),
        cost_estimate=pl.CostEstimate(
            flops=10 * rows * length * features, bytes_accessed=2 * rows * (2 * width + features), transcendentals=rows * length * features // HEAD_DIM
        ),
        name="attend_back",
    )(slopes, projected, context_grad)


def settle_kernel(chunks, kinds, part, flags_ref, *refs):
    *pieces, gate_up_ref, down_ref, held = refs
    first = flags_ref[0] == 1
    count = len(pieces) // 4
    half_rows = chunks * count * part
    for half in range(2):
        for index in range(count):
            mine = pieces[half * count + index]
            other = pieces[(2 + half) * count + index]
            place = flags_ref[1 + half * count + index]
            for chunk in range(chunks):
                base = pl.multiple_of(half * half_rows + chunk * count * part + place * part, part)
                for kind in range(kinds):
                    start = (chunk * kinds + kind) * part
                    rows = jnp.where(first, mine[start : start + part, :], other[start : start + part, :]).astype(F32)
                    if kind < kinds - 1:
                        held[kind, pl.ds(base, part), :] = rows
                    else:
                        down_ref[pl.ds(base, part), :] = rows
    for kind in range(kinds - 1):
        gate_up_ref[:, kind, :] = jnp.transpose(held[kind])


def settle(pieces, flags, chunks, kinds, part):
    rows, features = pieces[0].shape
    units = 2 * (len(pieces) // 4) * chunks * part
    width = 2 * LANES
    return pl.pallas_call(
        functools.partial(settle_kernel, chunks, kinds, part),
        grid=(features // width,),
        in_specs=[pl.BlockSpec(memory_space=pltpu.SMEM)]
        + [pl.BlockSpec((rows, width), lambda index: (0, index))] * len(pieces),
        out_specs=[
            pl.BlockSpec((width, kinds - 1, units), lambda index: (index, 0, 0)),
            pl.BlockSpec((units, width), lambda index: (0, index)),
        ],
        out_shape=[
            jax.ShapeDtypeStruct((features, kinds - 1, units), F32),
            jax.ShapeDtypeStruct((units, features), F32),
        ],
        scratch_shapes=[pltpu.VMEM((kinds - 1, units, width), F32)],
        name="settle",
    )(flags, *pieces)


def together(*trees):
    return lax.optimization_barrier(trees)


def near(chunk):
    return dict(chunk, near=exchange(chunk["own"][0], tensor_mask=1))


def far(chunk):
    return dict(chunk, far=exchange(jnp.stack([chunk["own"][0], chunk["near"]]), tensor_mask=2))


def first(chunk):
    remote = jnp.concatenate([chunk["near"][None], chunk["far"]])
    return dict(
        chunk,
        remote=remote,
        first=exchange(remote, dp_masks=FIRST),
        second=exchange(remote, dp_masks=SECOND),
    )


def second(chunk):
    return dict(chunk, third=exchange(chunk["first"], dp_masks=SECOND))


def assemble(chunk):
    rest = [chunk["remote"], chunk["first"], chunk["second"], chunk["third"]]
    return jnp.stack([jnp.concatenate([own[None], r]) for own, r in zip(chunk["own"], rest)])


def add_low(a, b):
    return (a.astype(F32) + b.astype(F32)).astype(BF16)


def total_low(*parts):
    return sum(part.astype(F32) for part in parts).astype(BF16)


def reduce_open(terms):
    return (
        terms[0],
        terms[1],
        exchange(terms[3], dp_masks=SECOND),
        exchange(terms[2], dp_masks=SECOND),
    )


def reduce_turn(parts):
    return parts[0], exchange(total_low(parts[1], parts[2]), dp_masks=FIRST)


def reduce_near(own, turned, opened):
    pairs = total_low(own, turned, opened)
    pairs = pairs.reshape((2, 2) + pairs.shape[1:])
    return pairs[:, 0], exchange(pairs[:, 1], tensor_mask=1)


def reduce_far(pair):
    terms = total_low(*pair)
    return terms[0], exchange(terms[1], tensor_mask=2)


def reduce_last(pair):
    one = total_low(*pair)
    mask = PLANE
    while mask < lax.axis_size("dp"):
        one = total_low(one, exchange(one, dp_masks=(mask, mask)))
        mask *= 2
    return one


def attn_forward(own_low, weights, norms, slopes, seqs):
    wqkv, wo = weights
    projected = dot(own_low, wqkv, 1, 1).astype(BF16)
    context = attend(projected, slopes, seqs)
    first_sum = own_low.astype(F32) + dot(context, wo, 1, 0)
    first_norm = norm_rows(first_sum, norms[0], norms[1])
    return projected, context, first_sum, first_norm


def both_rows(rows_low):
    return jnp.concatenate([rows_low, swap(rows_low)])


def join_rows(terms):
    rows = terms.shape[0] // 2
    return terms[:rows] + swap(terms[rows:].astype(BF16)).astype(F32)


def feed_forward(first_all, weights):
    gate_up, down = weights
    gated = dot(first_all, gate_up, 1, 1)
    gate_part, up_part = jnp.split(gated, 2, axis=-1)
    hidden = gelu_product(gate_part, up_part).astype(BF16)
    return gated, hidden, dot(hidden, down, 1, 0)


def feed_backward(mixed_all, weights, gated):
    hidden_grad = dot(mixed_all, weights[1], 1, 1)
    gate_part, up_part = jnp.split(gated, 2, axis=-1)
    _, gelu_back = jax.vjp(gelu_product, gate_part, up_part)
    gate_grad, up_grad = gelu_back(hidden_grad)
    return jnp.concatenate([gate_grad, up_grad], axis=-1).astype(BF16)


def feed_weight_grads(mixed_all, first_all, gated_grad, hidden):
    return dot(gated_grad, first_all, 0, 0).astype(BF16), dot(hidden, mixed_all, 0, 0).astype(BF16)


def norm_backward(total, gain, offset, grad):
    _, back = jax.vjp(norm_rows, total, gain, offset)
    return back(grad)


def context_backward(sum_grad, weights, context):
    attended_low = sum_grad.astype(BF16)
    context_grad = dot(attended_low, weights[1], 1, 1).astype(BF16)
    return context_grad, dot(context, attended_low, 0, 0).astype(BF16)


def body(
    layer_input,
    out_grad,
    loss_mask,
    query_key_value_weight,
    attention_output_weight,
    gate_up_weight,
    down_weight,
    norm1_gain,
    norm1_bias,
    norm2_gain,
    norm2_bias,
):
    core = lax.axis_index("section")
    plane = lax.axis_index("dp")
    depth = lax.axis_index("tensor")
    is_first = core == 0
    micro, own_seqs, length, features = layer_input.shape
    local = query_key_value_weight.shape[-1]
    local_heads = local // HEAD_DIM
    units = down_weight.shape[1]
    part = HEAD_DIM // PLANE
    unit_part = units // 2 // PLANE // FEED_CHUNKS
    seqs = micro * own_seqs // 2
    rows = seqs * length

    orders = [jnp.array([0, 1, 2, 3]), jnp.array([0, 2, 1, 3])]
    steps = jnp.where(is_first, orders[0], orders[1])
    in_plane = jnp.bitwise_and(plane, PLANE - 1)

    def relative(slab):
        return [
            lax.dynamic_index_in_dim(slab, jnp.bitwise_xor(in_plane, steps[e]), 0, keepdims=False)
            for e in range(PLANE)
        ]

    def share(slab):
        keep = lax.dynamic_index_in_dim(slab, core, 0, keepdims=False)
        got = swap(lax.dynamic_index_in_dim(slab, 1 - core, 0, keepdims=False))
        return jnp.where(is_first, keep, got), jnp.where(is_first, got, keep)

    qkv_rows = jnp.transpose(query_key_value_weight[0], (1, 2, 0))
    attn_rows = jnp.concatenate([qkv_rows, attention_output_weight], axis=0)
    attn_slab = attn_rows.reshape(2, 2, local_heads, PLANE, part, features)
    attn_slab = jnp.transpose(attn_slab, (0, 3, 1, 2, 4, 5)).reshape(2, PLANE, -1, features)
    attn_in = [{"own": relative(own)} for own in share(attn_slab)]
    attn_in[0] = near(attn_in[0])
    attn_in, gate_up_weight, down_weight = together(attn_in, gate_up_weight, down_weight)
    gate_up_rows = jnp.transpose(gate_up_weight[0], (1, 2, 0))
    feed_rows = jnp.concatenate([gate_up_rows, down_weight], axis=0)
    feed_slab = feed_rows.reshape(3, 2, FEED_CHUNKS, PLANE, unit_part, features)
    feed_slab = jnp.transpose(feed_slab, (2, 1, 3, 0, 4, 5)).reshape(FEED_CHUNKS, 2, PLANE, -1, features)

    feed_in = [[{"own": relative(own)} for own in share(feed_slab[k])] for k in range(FEED_CHUNKS)]
    a0, a1 = attn_in
    (p0, p1), (q0, q1) = feed_in


    norm_table = jnp.concatenate([norm1_gain, norm1_bias, norm2_gain, norm2_bias])
    norm_other = swap(norm_table)
    norm_first = jnp.where(is_first, norm_table, norm_other)
    norm_second = jnp.where(is_first, norm_other, norm_table)
    norms = [tuple(table[i] for i in range(4)) for table in (norm_first, norm_second)]

    slope_table = jnp.asarray(alibi_table(HEADS)).reshape(DEPTH, local_heads)
    slopes = jnp.concatenate(
        [lax.dynamic_index_in_dim(slope_table, jnp.bitwise_xor(depth, j), 0, keepdims=False) for j in range(DEPTH)]
    )

    def own_half(whole):
        flat = whole.reshape((2, rows) + whole.shape[3:])
        return lax.dynamic_index_in_dim(flat, core, 0, keepdims=False)

    start = own_half(layer_input)
    seed = own_half(out_grad).astype(F32) * own_half(loss_mask).astype(F32)[..., None]


    def attn_weights(chunk):
        full = assemble(chunk).reshape(PLANE, DEPTH, 2, local_heads, part, features)
        mine = jnp.transpose(full, (2, 1, 3, 0, 4, 5)).reshape(2, -1, features)
        other = swap(mine)
        qk = jnp.where(is_first, mine, other)
        vo = jnp.where(is_first, other, mine)
        wqkv = jnp.concatenate([qk.reshape(-1, features), vo[0]])
        return wqkv, vo[1]

    def feed_weights(chunk):
        full = assemble(chunk).reshape(PLANE * DEPTH, 3, unit_part, features)
        full = jnp.transpose(full, (1, 0, 2, 3)).reshape(3, -1, features)
        return full[:2].reshape(-1, features), full[2]

    a0, p0 = far(a0), near(p0)
    a0, p0, q0 = together(a0, p0, q0)
    a0, p0, q0 = first(a0), far(p0), near(q0)
    a0, p0, q0, a1 = together(a0, p0, q0, a1)
    a0, p0, q0, a1 = second(a0), first(p0), far(q0), near(a1)
    a0, p0, q0, a1, p1 = together(a0, p0, q0, a1, p1)
    p0, q0, a1, p1 = second(p0), first(q0), far(a1), near(p1)
    attn0 = attn_weights(a0)
    projected0, context0, sum0, norm0 = attn_forward(start, attn0, norms[0], slopes, seqs)
    low0, p0, q0, a1, p1, q1 = together(norm0.astype(BF16), p0, q0, a1, p1, q1)
    q0, a1, p1, q1 = second(q0), first(a1), far(p1), near(q1)
    all0 = both_rows(low0)
    feed_p0 = feed_weights(p0)
    gated_p0, hidden_p0, mixed = feed_forward(all0, feed_p0)
    mixed, q0, a1, p1, q1 = together(mixed, q0, a1, p1, q1)
    a1, p1, q1 = second(a1), first(p1), far(q1)
    feed_q0 = feed_weights(q0)
    gated_q0, hidden_q0, more = feed_forward(all0, feed_q0)
    mixed = mixed + more
    mixed, a1, p1, q1 = together(mixed, a1, p1, q1)
    p1, q1 = second(p1), first(q1)
    attn1 = attn_weights(a1)
    total0 = norm0 + join_rows(mixed)
    middle_low = norm_rows(total0, norms[0][2], norms[0][3]).astype(BF16)
    projected1, context1, sum1, norm1 = attn_forward(middle_low, attn1, norms[1], slopes, seqs)
    low1, p1, q1 = together(norm1.astype(BF16), p1, q1)
    q1 = second(q1)
    all1 = both_rows(low1)
    feed_p1 = feed_weights(p1)
    gated_p1, hidden_p1, mixed = feed_forward(all1, feed_p1)
    mixed, q1 = together(mixed, q1)
    feed_q1 = feed_weights(q1)
    gated_q1, hidden_q1, more = feed_forward(all1, feed_q1)
    total1 = norm1 + join_rows(mixed + more)
    final_low = norm_rows(total1, norms[1][2], norms[1][3]).astype(BF16)

    def give(early, late):
        mine = jnp.where(is_first, early, late)
        got = swap(jnp.where(is_first, late, early))
        both = jnp.concatenate([jnp.where(is_first, mine, got), jnp.where(is_first, got, mine)])
        return both.reshape((1, micro, own_seqs, length, features))

    def feed_terms(gate_up, down):
        full = jnp.concatenate([gate_up, down]).reshape(3, PLANE, DEPTH, unit_part, features)
        full = jnp.transpose(full, (1, 2, 0, 3, 4)).reshape(PLANE, DEPTH, -1, features)
        return [full[e] for e in range(PLANE)]

    def attn_terms(qkv, out, vectors):
        spread = jnp.pad(jnp.stack(vectors).astype(BF16), ((0, NORM_ROWS - len(vectors)), (0, 0)))
        spread = jnp.broadcast_to(spread, (2, PLANE, DEPTH, NORM_ROWS, features))
        full = jnp.concatenate([qkv, out]).reshape(2, 2, DEPTH, local_heads, PLANE, part, features)
        full = jnp.transpose(full, (0, 4, 2, 1, 3, 5, 6)).reshape(2, PLANE, DEPTH, -1, features)
        return jnp.concatenate([full, spread], axis=3)

    def attn_swap(full):
        keep = lax.dynamic_index_in_dim(full, core, 0, keepdims=False)
        return keep, swap(lax.dynamic_index_in_dim(full, 1 - core, 0, keepdims=False))

    def attn_pieces(pair):
        full = total_low(*pair)
        return [full[e] for e in range(PLANE)]

    def hand_over(block, source):
        planes, depths = lax.axis_size("dp"), lax.axis_size("tensor")
        count = planes * depths
        pairs = [(source * count + i, (1 - source) * count + i) for i in range(count)]
        return lax.ppermute(block, AXES, pairs)

    second_grad, gain_two1, offset_two1 = norm_backward(total1, norms[1][2], norms[1][3], seed)
    mixed_all = both_rows(second_grad.astype(BF16))
    grad_p = feed_backward(mixed_all, feed_p1, gated_p1)
    p1 = feed_terms(*feed_weight_grads(mixed_all, all1, grad_p, hidden_p1))
    mixed_all, grad_p, p1 = together(mixed_all, grad_p, p1)

    p1_own, p1_half, p1_a, p1_b = reduce_open(p1)
    terms = dot(grad_p, feed_p1[0], 1, 0)
    grad_q = feed_backward(mixed_all, feed_q1, gated_q1)
    terms = terms + dot(grad_q, feed_q1[0], 1, 0)
    q1 = feed_terms(*feed_weight_grads(mixed_all, all1, grad_q, hidden_q1))
    layer_out = give(middle_low, final_low)
    terms, q1, p1_a, layer_out = together(terms, q1, p1_a, layer_out)

    p1_own, p1_c = reduce_turn((p1_own, p1_half, p1_a))
    first_grad = join_rows(terms) + second_grad
    sum_grad, gain_one1, offset_one1 = norm_backward(sum1, norms[1][0], norms[1][1], first_grad)
    context_grad, out = context_backward(sum_grad, attn1, context1)
    context_grad, out, q1, p1_b = together(context_grad, out, q1, p1_b)

    q1_own, q1_half, q1_a, q1_b = reduce_open(q1)
    projected_grad = attend_back(projected1, context_grad, slopes, seqs)
    qkv = dot(projected_grad, middle_low, 0, 0).astype(BF16)
    a1 = attn_terms(qkv, out, [gain_one1, offset_one1, gain_two1, offset_two1])
    projected_grad, a1, q1_a, p1_c = together(projected_grad, a1, q1_a, p1_c)

    a1 = attn_swap(a1)
    q1_own, q1_c = reduce_turn((q1_own, q1_half, q1_a))
    p1 = reduce_near(p1_own, p1_c, p1_b)
    middle_grad = dot(projected_grad, attn1[0], 1, 0) + sum_grad
    second_grad, gain_two0, offset_two0 = norm_backward(total0, norms[0][2], norms[0][3], middle_grad)
    mixed_low = second_grad.astype(BF16)
    mixed_low, a1, q1_b, p1 = together(mixed_low, a1, q1_b, p1)

    mixed_all = both_rows(mixed_low)
    a1_own, a1_half, a1_a, a1_b = reduce_open(attn_pieces(a1))
    p1 = reduce_far(p1)
    grad_p = feed_backward(mixed_all, feed_p0, gated_p0)
    mixed_all, grad_p, a1_a, q1_c, p1 = together(mixed_all, grad_p, a1_a, q1_c, p1)

    a1_own, a1_c = reduce_turn((a1_own, a1_half, a1_a))
    q1 = reduce_near(q1_own, q1_c, q1_b)
    p0 = feed_terms(*feed_weight_grads(mixed_all, all0, grad_p, hidden_p0))
    terms = dot(grad_p, feed_p0[0], 1, 0)
    mixed_all, terms, p0, a1_b, q1 = together(mixed_all, terms, p0, a1_b, q1)

    p0_own, p0_half, p0_a, p0_b = reduce_open(p0)
    q1 = reduce_far(q1)
    grad_q = feed_backward(mixed_all, feed_q0, gated_q0)
    terms = terms + dot(grad_q, feed_q0[0], 1, 0)
    terms, grad_q, p0_a, a1_c, q1 = together(terms, grad_q, p0_a, a1_c, q1)

    p0_own, p0_c = reduce_turn((p0_own, p0_half, p0_a))
    a1 = reduce_near(a1_own, a1_c, a1_b)
    late = jnp.concatenate([reduce_last(p1), reduce_last(q1)])
    late_first = exchange(late, dp_masks=FIRST)
    q0 = feed_terms(*feed_weight_grads(mixed_all, all0, grad_q, hidden_q0))
    first_grad = join_rows(terms) + second_grad
    sum_grad, gain_one0, offset_one0 = norm_backward(sum0, norms[0][0], norms[0][1], first_grad)
    sum_grad, q0, p0_b, a1, late, late_first = together(sum_grad, q0, p0_b, a1, late, late_first)

    q0_own, q0_half, q0_a, q0_b = reduce_open(q0)
    a1 = reduce_far(a1)
    context_grad, out = context_backward(sum_grad, attn0, context0)
    projected_grad = attend_back(projected0, context_grad, slopes, seqs)
    qkv = dot(projected_grad, start, 0, 0).astype(BF16)
    a0 = attn_terms(qkv, out, [gain_one0, offset_one0, gain_two0, offset_two0])
    late_second = exchange(late, dp_masks=SECOND)
    projected_grad, a0, q0_a, p0_c, a1, late_second = together(projected_grad, a0, q0_a, p0_c, a1, late_second)

    a0 = attn_swap(a0)
    q0_own, q0_c = reduce_turn((q0_own, q0_half, q0_a))
    start_grad = dot(projected_grad, attn0[0], 1, 0) + sum_grad
    start_grad, a0, q0_b = together(start_grad, a0, q0_b)

    a0 = attn_pieces(a0)
    a0_got = exchange(jnp.stack(a0[2:]), dp_masks=SECOND)
    p0 = reduce_near(p0_own, p0_c, p0_b)
    input_grad = give(start_grad, middle_grad)
    a0_got, q0_c, p0, input_grad = together(a0_got, q0_c, p0, input_grad)

    a0_c = exchange(total_low(a0[1], a0_got[1]), dp_masks=FIRST)
    q0 = reduce_near(q0_own, q0_c, q0_b)
    p0 = reduce_far(p0)
    late_third = exchange(late_first, dp_masks=SECOND)
    late_got = [hand_over(late, 0), hand_over(late_first, 0)]
    a0_c, q0, p0, late_third, late_got = together(a0_c, q0, p0, late_third, late_got)

    a0 = reduce_near(a0[0], a0_got[0], a0_c)
    q0 = reduce_far(q0)
    attn_late = reduce_last(a1)
    attn = attn_late[:-NORM_ROWS]
    late_attn = [attn, exchange(attn, dp_masks=FIRST), exchange(attn, dp_masks=SECOND)]
    late_got += [hand_over(late_second, 0), hand_over(late_third, 0)]
    a0, q0, late_attn, late_got = together(a0, q0, late_attn, late_got)

    a0 = reduce_far(a0)
    late_attn.append(exchange(late_attn[1], dp_masks=SECOND))
    feed = jnp.concatenate([reduce_last(p0), reduce_last(q0)])
    feed_first = exchange(feed, dp_masks=FIRST)
    feed_got = [hand_over(feed, 1)]
    a0, late_attn, feed, feed_first, feed_got = together(a0, late_attn, feed, feed_first, feed_got)

    attn_early = reduce_last(a0)
    attn = attn_early[:-NORM_ROWS]
    attn_first, attn_second = exchange(attn, dp_masks=FIRST), exchange(attn, dp_masks=SECOND)
    feed_second = exchange(feed, dp_masks=SECOND)
    attn_late_all = jnp.stack(late_attn)
    attn_late_got = hand_over(attn_late_all, 0)
    feed_got.append(hand_over(feed_first, 1))
    attn_first, attn_second, feed_second, attn_late_got, feed_got = together(
        attn_first, attn_second, feed_second, attn_late_got, feed_got
    )

    attn_third, feed_third = exchange(attn_first, dp_masks=SECOND), exchange(feed_first, dp_masks=SECOND)
    feed_got.append(hand_over(feed_second, 1))
    attn_early_all = jnp.stack([attn, attn_first, attn_second, attn_third])
    attn_got = hand_over(attn_early_all, 1)
    feed_got.append(hand_over(feed_third, 1))

    feed_early = [feed, feed_first, feed_second, feed_third]
    feed_late = [late, late_first, late_second, late_third]
    flags = jnp.concatenate(
        [is_first.astype(jnp.int32)[None]] + [jnp.bitwise_xor(in_plane, order) for order in orders]
    )
    grad_in, grad_down = settle(
        feed_early + feed_got + late_got + feed_late, flags, FEED_CHUNKS, 3, unit_part
    )
    parts = [jnp.where(is_first, attn_early_all, attn_late_got), jnp.where(is_first, attn_got, attn_late_all)]
    attn_total = jnp.stack(
        [
            jnp.stack(
                [
                    lax.dynamic_index_in_dim(half, order[jnp.bitwise_xor(in_plane, index)], 0, keepdims=False)
                    for half, order in zip(parts, orders)
                ]
            )
            for index in range(PLANE)
        ]
    )
    attn_total = attn_total.reshape(PLANE, 2, 2, local_heads, part, features)
    attn_total = jnp.transpose(attn_total, (1, 2, 3, 0, 4, 5)).reshape(4, local, features).astype(F32)
    grad_qkv = jnp.transpose(attn_total[:3], (2, 0, 1))
    grad_out = attn_total[3]

    vectors = jnp.where(is_first, attn_early[-NORM_ROWS:], attn_late[-NORM_ROWS:]).astype(F32)
    vectors = lax.dynamic_slice_in_dim(vectors, depth * local, local, 1)

    return (
        layer_out,
        input_grad,
        grad_qkv[None],
        grad_out[None],
        grad_in[None],
        grad_down[None],
        vectors[0][None],
        vectors[1][None],
        vectors[2][None],
        vectors[3][None],
    )


def solution(mesh):
    placed = (
        P(None, ("dp", "tensor"), None, None),
        P(None, ("dp", "tensor"), None, None),
        P(None, ("dp", "tensor"), None),
        P("section", None, None, "tensor"),
        P("section", "tensor", None),
        P("section", None, None, "tensor"),
        P("section", "tensor", None),
        P("section", None),
        P("section", None),
        P("section", None),
        P("section", None),
    )
    return jax.shard_map(
        body,
        mesh=mesh,
        in_specs=placed,
        out_specs=(
            P("section", None, ("dp", "tensor"), None, None),
            P("section", None, ("dp", "tensor"), None, None),
            P("section", None, None, "tensor"),
            P("section", "tensor", None),
            P("section", None, None, "tensor"),
            P("section", "tensor", None),
            P("section", "tensor"),
            P("section", "tensor"),
            P("section", "tensor"),
            P("section", "tensor"),
        ),
        check_vma=False,
    )
```

```python
import functools
import math

import jax
import jax.numpy as jnp
import numpy as np
from jax import lax
from jax.experimental import pallas as pl
from jax.experimental.pallas import tpu as pltpu
from jax.sharding import PartitionSpec as P

HEADS = 12
HEAD_DIM = 64
NORM_EPSILON = 1e-05
AXES = ("section", "dp", "tensor")
FEED_CHUNKS = 2
NORM_ROWS = 16
LANES = 128
GROUP = 3
GROUP_BACK = 3

F32 = jnp.float32
BF16 = jnp.bfloat16


def power_slopes(total_heads):
    return [2.0 ** (-8.0 * (index + 1) / total_heads) for index in range(total_heads)]


def alibi_table(number_heads):
    closest = 2 ** int(math.floor(math.log2(number_heads)))
    slopes = power_slopes(closest)
    slopes = slopes + power_slopes(2 * closest)[0::2][: number_heads - closest]
    return np.array(slopes, dtype=np.float32)


def norm_rows(values, gain, offset):
    row_mean = jnp.mean(values, axis=-1, keepdims=True)
    centred = values - row_mean
    row_var = jnp.mean(centred * centred, axis=-1, keepdims=True)
    return centred * lax.rsqrt(row_var + NORM_EPSILON) * gain + offset


def gelu_product(gate_part, up_part):
    return jax.nn.gelu(gate_part, approximate=False) * up_part


def dot(a, b, ca, cb):
    return lax.dot_general(a, b, (((ca,), (cb,)), ((), ())), preferred_element_type=F32)


def exchange(block, section_mask=0, dp_masks=(0, 0), tensor_mask=0):
    dp = lax.axis_size("dp")
    tensor = lax.axis_size("tensor")
    pairs = []
    for s in range(lax.axis_size("section")):
        for d in range(dp):
            for t in range(tensor):
                target = ((s ^ section_mask) * dp + (d ^ dp_masks[s])) * tensor + (t ^ tensor_mask)
                pairs.append(((s * dp + d) * tensor + t, target))
    return lax.ppermute(block, AXES, pairs)


def swap(block):
    return exchange(block, section_mask=1)


FIRST = (1, 2)
SECOND = (2, 1)
PLANE = 4
DEPTH = 4


def contract(a, b, ca, cb):
    return lax.dot_general(a, b, (((ca,), (cb,)), ((), ())), preferred_element_type=F32)


def head_masks(length):
    lane = lax.broadcasted_iota(jnp.int32, (length, LANES), 1)
    return [lane // HEAD_DIM == index for index in range(LANES // HEAD_DIM)]


def distances(length):
    across = lax.broadcasted_iota(jnp.int32, (length, length), 0)
    along = lax.broadcasted_iota(jnp.int32, (length, length), 1)
    return jnp.abs(across - along).astype(F32)


def attend_kernel(group, slopes_ref, projected_ref, context_ref):
    length, features = context_ref.shape
    masks = head_masks(length)
    distance = distances(length)
    per = len(masks)
    pairs = features // LANES
    for first in range(0, pairs, group):
        heads = [(pair, index) for pair in range(first, first + group) for index in range(per)]
        parts = {p: [slice(i * features + p * LANES, i * features + (p + 1) * LANES) for i in range(3)] for p, _ in heads}
        scores = []
        for pair, index in heads:
            key = projected_ref[:, parts[pair][1]]
            own = jnp.where(masks[index], key, jnp.zeros_like(key))
            scores.append(contract(own, projected_ref[:, parts[pair][0]], 1, 1))
        weights = []
        for (pair, index), score in zip(heads, scores):
            score = score * HEAD_DIM ** (-0.5) - slopes_ref[pair * per + index] * distance
            weight = jnp.exp(score - jnp.max(score, axis=0, keepdims=True))
            weight = weight * (1.0 / jnp.sum(weight, axis=0, keepdims=True))
            weights.append(weight.astype(BF16))
        for pair in range(first, first + group):
            value = projected_ref[:, parts[pair][2]]
            context = jnp.zeros((length, LANES), F32)
            for (other, index), weight in zip(heads, weights):
                if other == pair:
                    context = jnp.where(masks[index], contract(weight, value, 0, 0), context)
            context_ref[:, parts[pair][0]] = context.astype(BF16)


def attend_back_kernel(group, slopes_ref, projected_ref, context_grad_ref, grad_ref):
    length, features = context_grad_ref.shape
    masks = head_masks(length)
    distance = distances(length)
    per = len(masks)
    pairs = features // LANES
    for first in range(0, pairs, group):
        heads = [(pair, index) for pair in range(first, first + group) for index in range(per)]
        parts = {p: [slice(i * features + p * LANES, i * features + (p + 1) * LANES) for i in range(3)] for p, _ in heads}
        scores, weights_grads = [], []
        for pair, index in heads:
            key, value = projected_ref[:, parts[pair][1]], projected_ref[:, parts[pair][2]]
            own = jnp.where(masks[index], key, jnp.zeros_like(key))
            scores.append(contract(own, projected_ref[:, parts[pair][0]], 1, 1))
            own = jnp.where(masks[index], value, jnp.zeros_like(value))
            weights_grads.append(contract(own, context_grad_ref[:, parts[pair][0]], 1, 1))
        weights, score_grads = [], []
        for (pair, index), score, weights_grad in zip(heads, scores, weights_grads):
            score = score * HEAD_DIM ** (-0.5) - slopes_ref[pair * per + index] * distance
            weight = jnp.exp(score - jnp.max(score, axis=0, keepdims=True))
            weight = weight * (1.0 / jnp.sum(weight, axis=0, keepdims=True))
            mean_grad = jnp.sum(weight * weights_grad, axis=0, keepdims=True)
            score_grads.append((weight * (weights_grad - mean_grad)).astype(BF16))
            weights.append(weight.astype(BF16))
        for pair in range(first, first + group):
            query, key = projected_ref[:, parts[pair][0]], projected_ref[:, parts[pair][1]]
            context_grad = context_grad_ref[:, parts[pair][0]]
            grads = [jnp.zeros((length, LANES), F32)] * 3
            for (other, index), weight, score_grad in zip(heads, weights, score_grads):
                if other == pair:
                    new = [
                        contract(score_grad, key, 0, 0) * HEAD_DIM ** (-0.5),
                        contract(score_grad, query, 1, 0) * HEAD_DIM ** (-0.5),
                        contract(weight, context_grad, 1, 0),
                    ]
                    grads = [jnp.where(masks[index], n, g) for n, g in zip(new, grads)]
            for part, grad in zip(parts[pair], grads):
                grad_ref[:, part] = grad.astype(BF16)


def row_block(length, width):
    return pl.BlockSpec((length, width), lambda index: (index, 0))


def attend(projected, slopes, seqs):
    rows, width = projected.shape
    length, features = rows // seqs, width // 3
    return pl.pallas_call(
        functools.partial(attend_kernel, GROUP),
        grid=(seqs,),
        in_specs=[pl.BlockSpec(memory_space=pltpu.SMEM), row_block(length, width)],
        out_specs=row_block(length, features),
        out_shape=jax.ShapeDtypeStruct((rows, features), BF16),
        cost_estimate=pl.CostEstimate(
            flops=4 * rows * length * features, bytes_accessed=2 * rows * (width + features), transcendentals=rows * length * features // HEAD_DIM
        ),
        name="attend",
    )(slopes, projected)


def attend_back(projected, context_grad, slopes, seqs):
    rows, width = projected.shape
    length, features = rows // seqs, width // 3
    return pl.pallas_call(
        functools.partial(attend_back_kernel, GROUP_BACK),
        grid=(seqs,),
        in_specs=[
            pl.BlockSpec(memory_space=pltpu.SMEM),
            row_block(length, width),
            row_block(length, features),
        ],
        out_specs=row_block(length, width),
        out_shape=jax.ShapeDtypeStruct((rows, width), BF16),
        cost_estimate=pl.CostEstimate(
            flops=10 * rows * length * features, bytes_accessed=2 * rows * (2 * width + features), transcendentals=rows * length * features // HEAD_DIM
        ),
        name="attend_back",
    )(slopes, projected, context_grad)


def settle_kernel(chunks, kinds, part, flags_ref, *refs):
    *pieces, gate_up_ref, down_ref, held = refs
    first = flags_ref[0] == 1
    count = len(pieces) // 4
    half_rows = chunks * count * part
    for half in range(2):
        for index in range(count):
            mine = pieces[half * count + index]
            other = pieces[(2 + half) * count + index]
            place = flags_ref[1 + half * count + index]
            for chunk in range(chunks):
                base = pl.multiple_of(half * half_rows + chunk * count * part + place * part, part)
                for kind in range(kinds):
                    start = (chunk * kinds + kind) * part
                    rows = jnp.where(first, mine[start : start + part, :], other[start : start + part, :]).astype(F32)
                    if kind < kinds - 1:
                        held[kind, pl.ds(base, part), :] = rows
                    else:
                        down_ref[pl.ds(base, part), :] = rows
    for kind in range(kinds - 1):
        gate_up_ref[:, kind, :] = jnp.transpose(held[kind])


def settle(pieces, flags, chunks, kinds, part):
    rows, features = pieces[0].shape
    units = 2 * (len(pieces) // 4) * chunks * part
    width = 2 * LANES
    return pl.pallas_call(
        functools.partial(settle_kernel, chunks, kinds, part),
        grid=(features // width,),
        in_specs=[pl.BlockSpec(memory_space=pltpu.SMEM)]
        + [pl.BlockSpec((rows, width), lambda index: (0, index))] * len(pieces),
        out_specs=[
            pl.BlockSpec((width, kinds - 1, units), lambda index: (index, 0, 0)),
            pl.BlockSpec((units, width), lambda index: (0, index)),
        ],
        out_shape=[
            jax.ShapeDtypeStruct((features, kinds - 1, units), F32),
            jax.ShapeDtypeStruct((units, features), F32),
        ],
        scratch_shapes=[pltpu.VMEM((kinds - 1, units, width), F32)],
        name="settle",
    )(flags, *pieces)


def together(*trees):
    return lax.optimization_barrier(trees)


def near(chunk):
    return dict(chunk, near=exchange(chunk["own"][0], tensor_mask=1))


def far(chunk):
    return dict(chunk, far=exchange(jnp.stack([chunk["own"][0], chunk["near"]]), tensor_mask=2))


def first(chunk):
    remote = jnp.concatenate([chunk["near"][None], chunk["far"]])
    return dict(
        chunk,
        remote=remote,
        first=exchange(remote, dp_masks=FIRST),
        second=exchange(remote, dp_masks=SECOND),
    )


def second(chunk):
    return dict(chunk, third=exchange(chunk["first"], dp_masks=SECOND))


def assemble(chunk):
    rest = [chunk["remote"], chunk["first"], chunk["second"], chunk["third"]]
    return jnp.stack([jnp.concatenate([own[None], r]) for own, r in zip(chunk["own"], rest)])


def add_low(a, b):
    return (a.astype(F32) + b.astype(F32)).astype(BF16)


def total_low(*parts):
    return sum(part.astype(F32) for part in parts).astype(BF16)


def reduce_open(terms):
    return (
        terms[0],
        terms[1],
        exchange(terms[3], dp_masks=SECOND),
        exchange(terms[2], dp_masks=SECOND),
    )


def reduce_turn(parts):
    return parts[0], exchange(total_low(parts[1], parts[2]), dp_masks=FIRST)


def reduce_near(own, turned, opened):
    pairs = total_low(own, turned, opened)
    pairs = pairs.reshape((2, 2) + pairs.shape[1:])
    return pairs[:, 0], exchange(pairs[:, 1], tensor_mask=1)


def reduce_far(pair):
    terms = total_low(*pair)
    return terms[0], exchange(terms[1], tensor_mask=2)


def reduce_last(pair):
    one = total_low(*pair)
    mask = PLANE
    while mask < lax.axis_size("dp"):
        one = total_low(one, exchange(one, dp_masks=(mask, mask)))
        mask *= 2
    return one


def attn_forward(own_low, weights, norms, slopes, seqs):
    wqkv, wo = weights
    projected = dot(own_low, wqkv, 1, 1).astype(BF16)
    context = attend(projected, slopes, seqs)
    first_sum = own_low.astype(F32) + dot(context, wo, 1, 0)
    first_norm = norm_rows(first_sum, norms[0], norms[1])
    return projected, context, first_sum, first_norm


def both_rows(rows_low):
    return jnp.concatenate([rows_low, swap(rows_low)])


def join_rows(terms):
    rows = terms.shape[0] // 2
    return terms[:rows] + swap(terms[rows:].astype(BF16)).astype(F32)


def feed_forward(first_all, weights):
    gate_up, down = weights
    gated = dot(first_all, gate_up, 1, 1)
    gate_part, up_part = jnp.split(gated, 2, axis=-1)
    hidden = gelu_product(gate_part, up_part).astype(BF16)
    return gated, hidden, dot(hidden, down, 1, 0)


def feed_backward(mixed_all, weights, gated):
    hidden_grad = dot(mixed_all, weights[1], 1, 1)
    gate_part, up_part = jnp.split(gated, 2, axis=-1)
    _, gelu_back = jax.vjp(gelu_product, gate_part, up_part)
    gate_grad, up_grad = gelu_back(hidden_grad)
    return jnp.concatenate([gate_grad, up_grad], axis=-1).astype(BF16)


def feed_weight_grads(mixed_all, first_all, gated_grad, hidden):
    return dot(gated_grad, first_all, 0, 0).astype(BF16), dot(hidden, mixed_all, 0, 0).astype(BF16)


def norm_backward(total, gain, offset, grad):
    _, back = jax.vjp(norm_rows, total, gain, offset)
    return back(grad)


def context_backward(sum_grad, weights, context):
    attended_low = sum_grad.astype(BF16)
    context_grad = dot(attended_low, weights[1], 1, 1).astype(BF16)
    return context_grad, dot(context, attended_low, 0, 0).astype(BF16)


def body(
    layer_input,
    out_grad,
    loss_mask,
    query_key_value_weight,
    attention_output_weight,
    gate_up_weight,
    down_weight,
    norm1_gain,
    norm1_bias,
    norm2_gain,
    norm2_bias,
):
    core = lax.axis_index("section")
    plane = lax.axis_index("dp")
    depth = lax.axis_index("tensor")
    is_first = core == 0
    micro, own_seqs, length, features = layer_input.shape
    local = query_key_value_weight.shape[-1]
    local_heads = local // HEAD_DIM
    units = down_weight.shape[1]
    part = HEAD_DIM // PLANE
    unit_part = units // 2 // PLANE // FEED_CHUNKS
    seqs = micro * own_seqs // 2
    rows = seqs * length

    orders = [jnp.array([0, 1, 2, 3]), jnp.array([0, 2, 1, 3])]
    steps = jnp.where(is_first, orders[0], orders[1])
    in_plane = jnp.bitwise_and(plane, PLANE - 1)

    def relative(slab):
        return [
            lax.dynamic_index_in_dim(slab, jnp.bitwise_xor(in_plane, steps[e]), 0, keepdims=False)
            for e in range(PLANE)
        ]

    def share(slab):
        keep = lax.dynamic_index_in_dim(slab, core, 0, keepdims=False)
        got = swap(lax.dynamic_index_in_dim(slab, 1 - core, 0, keepdims=False))
        return jnp.where(is_first, keep, got), jnp.where(is_first, got, keep)

    qkv_rows = jnp.transpose(query_key_value_weight[0], (1, 2, 0))
    attn_rows = jnp.concatenate([qkv_rows, attention_output_weight], axis=0)
    attn_slab = attn_rows.reshape(2, 2, local_heads, PLANE, part, features)
    attn_slab = jnp.transpose(attn_slab, (0, 3, 1, 2, 4, 5)).reshape(2, PLANE, -1, features)
    attn_in = [{"own": relative(own)} for own in share(attn_slab)]
    attn_in[0] = near(attn_in[0])
    attn_in, gate_up_weight, down_weight = together(attn_in, gate_up_weight, down_weight)
    gate_up_rows = jnp.transpose(gate_up_weight[0], (1, 2, 0))
    feed_rows = jnp.concatenate([gate_up_rows, down_weight], axis=0)
    feed_slab = feed_rows.reshape(3, 2, FEED_CHUNKS, PLANE, unit_part, features)
    feed_slab = jnp.transpose(feed_slab, (2, 1, 3, 0, 4, 5)).reshape(FEED_CHUNKS, 2, PLANE, -1, features)

    feed_in = [[{"own": relative(own)} for own in share(feed_slab[k])] for k in range(FEED_CHUNKS)]
    a0, a1 = attn_in
    (p0, p1), (q0, q1) = feed_in


    norm_table = jnp.concatenate([norm1_gain, norm1_bias, norm2_gain, norm2_bias])
    norm_other = swap(norm_table)
    norm_first = jnp.where(is_first, norm_table, norm_other)
    norm_second = jnp.where(is_first, norm_other, norm_table)
    norms = [tuple(table[i] for i in range(4)) for table in (norm_first, norm_second)]

    slope_table = jnp.asarray(alibi_table(HEADS)).reshape(DEPTH, local_heads)
    slopes = jnp.concatenate(
        [lax.dynamic_index_in_dim(slope_table, jnp.bitwise_xor(depth, j), 0, keepdims=False) for j in range(DEPTH)]
    )

    def own_half(whole):
        flat = whole.reshape((2, rows) + whole.shape[3:])
        return lax.dynamic_index_in_dim(flat, core, 0, keepdims=False)

    start = own_half(layer_input)
    seed = own_half(out_grad).astype(F32) * own_half(loss_mask).astype(F32)[..., None]


    def attn_weights(chunk):
        full = assemble(chunk).reshape(PLANE, DEPTH, 2, local_heads, part, features)
        mine = jnp.transpose(full, (2, 1, 3, 0, 4, 5)).reshape(2, -1, features)
        other = swap(mine)
        qk = jnp.where(is_first, mine, other)
        vo = jnp.where(is_first, other, mine)
        wqkv = jnp.concatenate([qk.reshape(-1, features), vo[0]])
        return wqkv, vo[1]

    def feed_weights(chunk):
        full = assemble(chunk).reshape(PLANE * DEPTH, 3, unit_part, features)
        full = jnp.transpose(full, (1, 0, 2, 3)).reshape(3, -1, features)
        return full[:2].reshape(-1, features), full[2]

    a0, p0 = far(a0), near(p0)
    a0, p0, q0, norms, seed = together(a0, p0, q0, norms, seed)
    a0, p0, q0 = first(a0), far(p0), near(q0)
    a0, p0, q0, a1 = together(a0, p0, q0, a1)
    a0, p0, q0, a1 = second(a0), first(p0), far(q0), near(a1)
    a0, p0, q0, a1, p1 = together(a0, p0, q0, a1, p1)
    p0, q0, a1, p1 = second(p0), first(q0), far(a1), near(p1)
    attn0 = attn_weights(a0)
    projected0, context0, sum0, norm0 = attn_forward(start, attn0, norms[0], slopes, seqs)
    low0, p0, q0, a1, p1, q1 = together(norm0.astype(BF16), p0, q0, a1, p1, q1)
    q0, a1, p1, q1 = second(q0), first(a1), far(p1), near(q1)
    all0 = both_rows(low0)
    feed_p0 = feed_weights(p0)
    gated_p0, hidden_p0, mixed = feed_forward(all0, feed_p0)
    mixed, q0, a1, p1, q1 = together(mixed, q0, a1, p1, q1)
    a1, p1, q1 = second(a1), first(p1), far(q1)
    feed_q0 = feed_weights(q0)
    gated_q0, hidden_q0, more = feed_forward(all0, feed_q0)
    mixed = mixed + more
    mixed, a1, p1, q1 = together(mixed, a1, p1, q1)
    p1, q1 = second(p1), first(q1)
    attn1 = attn_weights(a1)
    total0 = norm0 + join_rows(mixed)
    middle_low = norm_rows(total0, norms[0][2], norms[0][3]).astype(BF16)
    projected1, context1, sum1, norm1 = attn_forward(middle_low, attn1, norms[1], slopes, seqs)
    low1, p1, q1 = together(norm1.astype(BF16), p1, q1)
    q1 = second(q1)
    all1 = both_rows(low1)
    feed_p1 = feed_weights(p1)
    gated_p1, hidden_p1, mixed = feed_forward(all1, feed_p1)
    mixed, q1 = together(mixed, q1)
    feed_q1 = feed_weights(q1)
    gated_q1, hidden_q1, more = feed_forward(all1, feed_q1)
    total1 = norm1 + join_rows(mixed + more)
    final_low = norm_rows(total1, norms[1][2], norms[1][3]).astype(BF16)

    def give(early, late):
        mine = jnp.where(is_first, early, late)
        got = swap(jnp.where(is_first, late, early))
        both = jnp.concatenate([jnp.where(is_first, mine, got), jnp.where(is_first, got, mine)])
        return both.reshape((1, micro, own_seqs, length, features))

    def feed_terms(gate_up, down):
        full = jnp.concatenate([gate_up, down]).reshape(3, PLANE, DEPTH, unit_part, features)
        full = jnp.transpose(full, (1, 2, 0, 3, 4)).reshape(PLANE, DEPTH, -1, features)
        return [full[e] for e in range(PLANE)]

    def attn_terms(qkv, out, vectors):
        spread = jnp.pad(jnp.stack(vectors).astype(BF16), ((0, NORM_ROWS - len(vectors)), (0, 0)))
        spread = jnp.broadcast_to(spread, (2, PLANE, DEPTH, NORM_ROWS, features))
        full = jnp.concatenate([qkv, out]).reshape(2, 2, DEPTH, local_heads, PLANE, part, features)
        full = jnp.transpose(full, (0, 4, 2, 1, 3, 5, 6)).reshape(2, PLANE, DEPTH, -1, features)
        return jnp.concatenate([full, spread], axis=3)

    def attn_swap(full):
        keep = lax.dynamic_index_in_dim(full, core, 0, keepdims=False)
        return keep, swap(lax.dynamic_index_in_dim(full, 1 - core, 0, keepdims=False))

    def attn_pieces(pair):
        full = total_low(*pair)
        return [full[e] for e in range(PLANE)]

    def hand_over(block, source):
        planes, depths = lax.axis_size("dp"), lax.axis_size("tensor")
        count = planes * depths
        pairs = [(source * count + i, (1 - source) * count + i) for i in range(count)]
        return lax.ppermute(block, AXES, pairs)

    second_grad, gain_two1, offset_two1 = norm_backward(total1, norms[1][2], norms[1][3], seed)
    mixed_all = both_rows(second_grad.astype(BF16))
    grad_p = feed_backward(mixed_all, feed_p1, gated_p1)
    p1 = feed_terms(*feed_weight_grads(mixed_all, all1, grad_p, hidden_p1))
    mixed_all, grad_p, p1 = together(mixed_all, grad_p, p1)

    p1_own, p1_half, p1_a, p1_b = reduce_open(p1)
    grad_q = feed_backward(mixed_all, feed_q1, gated_q1)
    mixed_all, grad_p, grad_q, p1_a = together(mixed_all, grad_p, grad_q, p1_a)

    p1_own, p1_c = reduce_turn((p1_own, p1_half, p1_a))
    q1 = feed_terms(*feed_weight_grads(mixed_all, all1, grad_q, hidden_q1))
    terms = dot(grad_p, feed_p1[0], 1, 0) + dot(grad_q, feed_q1[0], 1, 0)
    layer_out = give(middle_low, final_low)
    terms, q1, p1_b, layer_out = together(terms, q1, p1_b, layer_out)

    q1_own, q1_half, q1_a, q1_b = reduce_open(q1)
    first_grad = join_rows(terms) + second_grad
    sum_grad, gain_one1, offset_one1 = norm_backward(sum1, norms[1][0], norms[1][1], first_grad)
    context_grad, out = context_backward(sum_grad, attn1, context1)
    context_grad, out, p1_c, q1_a = together(context_grad, out, p1_c, q1_a)

    q1_own, q1_c = reduce_turn((q1_own, q1_half, q1_a))
    projected_grad = attend_back(projected1, context_grad, slopes, seqs)
    qkv = dot(projected_grad, middle_low, 0, 0).astype(BF16)
    a1 = attn_terms(qkv, out, [gain_one1, offset_one1, gain_two1, offset_two1])
    projected_grad, a1, q1_b = together(projected_grad, a1, q1_b)

    a1 = attn_swap(a1)
    p1 = reduce_near(p1_own, p1_c, p1_b)
    middle_grad = dot(projected_grad, attn1[0], 1, 0) + sum_grad
    second_grad, gain_two0, offset_two0 = norm_backward(total0, norms[0][2], norms[0][3], middle_grad)
    mixed_low, a1, q1_c, p1 = together(second_grad.astype(BF16), a1, q1_c, p1)

    mixed_all = both_rows(mixed_low)
    a1_own, a1_half, a1_a, a1_b = reduce_open(attn_pieces(a1))
    p1 = reduce_far(p1)
    q1 = reduce_near(q1_own, q1_c, q1_b)
    grad_p = feed_backward(mixed_all, feed_p0, gated_p0)
    mixed_all, grad_p, a1_a, p1, q1 = together(mixed_all, grad_p, a1_a, p1, q1)

    a1_own, a1_c = reduce_turn((a1_own, a1_half, a1_a))
    q1 = reduce_far(q1)
    p0 = feed_terms(*feed_weight_grads(mixed_all, all0, grad_p, hidden_p0))
    terms = dot(grad_p, feed_p0[0], 1, 0)
    mixed_all, terms, p0, a1_b, q1 = together(mixed_all, terms, p0, a1_b, q1)

    p0_own, p0_half, p0_a, p0_b = reduce_open(p0)
    grad_q = feed_backward(mixed_all, feed_q0, gated_q0)
    terms = terms + dot(grad_q, feed_q0[0], 1, 0)
    terms, grad_q, p0_a, a1_c = together(terms, grad_q, p0_a, a1_c)

    p0_own, p0_c = reduce_turn((p0_own, p0_half, p0_a))
    a1 = reduce_near(a1_own, a1_c, a1_b)
    late = jnp.concatenate([reduce_last(p1), reduce_last(q1)])
    late_first = exchange(late, dp_masks=FIRST)
    q0 = feed_terms(*feed_weight_grads(mixed_all, all0, grad_q, hidden_q0))
    first_grad = join_rows(terms) + second_grad
    sum_grad, gain_one0, offset_one0 = norm_backward(sum0, norms[0][0], norms[0][1], first_grad)
    sum_grad, q0, p0_b, a1, late, late_first = together(sum_grad, q0, p0_b, a1, late, late_first)

    q0_own, q0_half, q0_a, q0_b = reduce_open(q0)
    a1 = reduce_far(a1)
    context_grad, out = context_backward(sum_grad, attn0, context0)
    projected_grad = attend_back(projected0, context_grad, slopes, seqs)
    qkv = dot(projected_grad, start, 0, 0).astype(BF16)
    a0 = attn_terms(qkv, out, [gain_one0, offset_one0, gain_two0, offset_two0])
    late_second = exchange(late, dp_masks=SECOND)
    projected_grad, a0, q0_a, p0_c, a1, late_second = together(projected_grad, a0, q0_a, p0_c, a1, late_second)

    a0 = attn_swap(a0)
    q0_own, q0_c = reduce_turn((q0_own, q0_half, q0_a))
    start_grad = dot(projected_grad, attn0[0], 1, 0) + sum_grad
    start_grad, a0, q0_b, q0_c = together(start_grad, a0, q0_b, q0_c)

    a0 = attn_pieces(a0)
    a0_got = exchange(jnp.stack(a0[2:]), dp_masks=SECOND)
    p0 = reduce_near(p0_own, p0_c, p0_b)
    input_grad = give(start_grad, middle_grad)
    a0_got, p0, input_grad = together(a0_got, p0, input_grad)

    a0_c = exchange(total_low(a0[1], a0_got[1]), dp_masks=FIRST)
    q0 = reduce_near(q0_own, q0_c, q0_b)
    p0 = reduce_far(p0)
    late_third = exchange(late_first, dp_masks=SECOND)
    a0_c, q0, p0, late_third = together(a0_c, q0, p0, late_third)

    a0 = reduce_near(a0[0], a0_got[0], a0_c)
    q0 = reduce_far(q0)
    attn_late = reduce_last(a1)
    attn = attn_late[:-NORM_ROWS]
    late_attn = [attn, exchange(attn, dp_masks=FIRST), exchange(attn, dp_masks=SECOND)]
    late_got = hand_over(jnp.stack([late, late_first, late_second, late_third]), 0)
    a0, q0, late_attn = together(a0, q0, late_attn)

    a0 = reduce_far(a0)
    late_attn.append(exchange(late_attn[1], dp_masks=SECOND))
    feed = jnp.concatenate([reduce_last(p0), reduce_last(q0)])
    feed_first = exchange(feed, dp_masks=FIRST)
    feed_got = [hand_over(feed, 1)]
    a0, late_attn, feed, feed_first, feed_got, late_got = together(
        a0, late_attn, feed, feed_first, feed_got, late_got
    )

    attn_early = reduce_last(a0)
    attn = attn_early[:-NORM_ROWS]
    attn_first, attn_second = exchange(attn, dp_masks=FIRST), exchange(attn, dp_masks=SECOND)
    feed_second = exchange(feed, dp_masks=SECOND)
    attn_late_all = jnp.stack(late_attn)
    attn_late_got = hand_over(attn_late_all, 0)
    feed_got.append(hand_over(feed_first, 1))
    attn_first, attn_second, feed_second, attn_late_got, feed_got = together(
        attn_first, attn_second, feed_second, attn_late_got, feed_got
    )

    attn_third, feed_third = exchange(attn_first, dp_masks=SECOND), exchange(feed_first, dp_masks=SECOND)
    feed_got.append(hand_over(feed_second, 1))
    attn_early_all = jnp.stack([attn, attn_first, attn_second, attn_third])
    attn_got = hand_over(attn_early_all, 1)
    feed_got.append(hand_over(feed_third, 1))

    feed_early = [feed, feed_first, feed_second, feed_third]
    feed_late = [late, late_first, late_second, late_third]
    flags = jnp.concatenate(
        [is_first.astype(jnp.int32)[None]] + [jnp.bitwise_xor(in_plane, order) for order in orders]
    )
    grad_in, grad_down = settle(
        feed_early + feed_got + [late_got[e] for e in range(PLANE)] + feed_late, flags, FEED_CHUNKS, 3, unit_part
    )
    parts = [jnp.where(is_first, attn_early_all, attn_late_got), jnp.where(is_first, attn_got, attn_late_all)]
    attn_total = jnp.stack(
        [
            jnp.stack(
                [
                    lax.dynamic_index_in_dim(half, order[jnp.bitwise_xor(in_plane, index)], 0, keepdims=False)
                    for half, order in zip(parts, orders)
                ]
            )
            for index in range(PLANE)
        ]
    )
    attn_total = attn_total.reshape(PLANE, 2, 2, local_heads, part, features)
    attn_total = jnp.transpose(attn_total, (1, 2, 3, 0, 4, 5)).reshape(4, local, features).astype(F32)
    grad_qkv = jnp.transpose(attn_total[:3], (2, 0, 1))
    grad_out = attn_total[3]

    vectors = jnp.where(is_first, attn_early[-NORM_ROWS:], attn_late[-NORM_ROWS:]).astype(F32)
    vectors = lax.dynamic_slice_in_dim(vectors, depth * local, local, 1)

    return (
        layer_out,
        input_grad,
        grad_qkv[None],
        grad_out[None],
        grad_in[None],
        grad_down[None],
        vectors[0][None],
        vectors[1][None],
        vectors[2][None],
        vectors[3][None],
    )


def solution(mesh):
    placed = (
        P(None, ("dp", "tensor"), None, None),
        P(None, ("dp", "tensor"), None, None),
        P(None, ("dp", "tensor"), None),
        P("section", None, None, "tensor"),
        P("section", "tensor", None),
        P("section", None, None, "tensor"),
        P("section", "tensor", None),
        P("section", None),
        P("section", None),
        P("section", None),
        P("section", None),
    )
    return jax.shard_map(
        body,
        mesh=mesh,
        in_specs=placed,
        out_specs=(
            P("section", None, ("dp", "tensor"), None, None),
            P("section", None, ("dp", "tensor"), None, None),
            P("section", None, None, "tensor"),
            P("section", "tensor", None),
            P("section", None, None, "tensor"),
            P("section", "tensor", None),
            P("section", "tensor"),
            P("section", "tensor"),
            P("section", "tensor"),
            P("section", "tensor"),
        ),
        check_vma=False,
    )
```

```python
import functools
import math

import jax
import jax.numpy as jnp
import numpy as np
from jax import lax
from jax.experimental import pallas as pl
from jax.experimental.pallas import tpu as pltpu
from jax.sharding import PartitionSpec as P

HEADS = 12
HEAD_DIM = 64
NORM_EPSILON = 1e-05
AXES = ("section", "dp", "tensor")
FEED_CHUNKS = 2
NORM_ROWS = 16
LANES = 128
GROUP = 3
GROUP_BACK = 3

F32 = jnp.float32
BF16 = jnp.bfloat16


def power_slopes(total_heads):
    return [2.0 ** (-8.0 * (index + 1) / total_heads) for index in range(total_heads)]


def alibi_table(number_heads):
    closest = 2 ** int(math.floor(math.log2(number_heads)))
    slopes = power_slopes(closest)
    slopes = slopes + power_slopes(2 * closest)[0::2][: number_heads - closest]
    return np.array(slopes, dtype=np.float32)


def norm_rows(values, gain, offset):
    row_mean = jnp.mean(values, axis=-1, keepdims=True)
    centred = values - row_mean
    row_var = jnp.mean(centred * centred, axis=-1, keepdims=True)
    return centred * lax.rsqrt(row_var + NORM_EPSILON) * gain + offset


def gelu_product(gate_part, up_part):
    return jax.nn.gelu(gate_part, approximate=False) * up_part


def dot(a, b, ca, cb):
    return lax.dot_general(a, b, (((ca,), (cb,)), ((), ())), preferred_element_type=F32)


def exchange(block, section_mask=0, dp_masks=(0, 0), tensor_mask=0):
    dp = lax.axis_size("dp")
    tensor = lax.axis_size("tensor")
    pairs = []
    for s in range(lax.axis_size("section")):
        for d in range(dp):
            for t in range(tensor):
                target = ((s ^ section_mask) * dp + (d ^ dp_masks[s])) * tensor + (t ^ tensor_mask)
                pairs.append(((s * dp + d) * tensor + t, target))
    return lax.ppermute(block, AXES, pairs)


def swap(block):
    return exchange(block, section_mask=1)


FIRST = (1, 2)
SECOND = (2, 1)
PLANE = 4
DEPTH = 4


def contract(a, b, ca, cb):
    return lax.dot_general(a, b, (((ca,), (cb,)), ((), ())), preferred_element_type=F32)


def head_masks(length):
    lane = lax.broadcasted_iota(jnp.int32, (length, LANES), 1)
    return [lane // HEAD_DIM == index for index in range(LANES // HEAD_DIM)]


def distances(length):
    across = lax.broadcasted_iota(jnp.int32, (length, length), 0)
    along = lax.broadcasted_iota(jnp.int32, (length, length), 1)
    return jnp.abs(across - along).astype(F32)


def attend_kernel(group, slopes_ref, projected_ref, context_ref):
    length, features = context_ref.shape
    masks = head_masks(length)
    distance = distances(length)
    per = len(masks)
    pairs = features // LANES
    for first in range(0, pairs, group):
        heads = [(pair, index) for pair in range(first, first + group) for index in range(per)]
        parts = {p: [slice(i * features + p * LANES, i * features + (p + 1) * LANES) for i in range(3)] for p, _ in heads}
        scores = []
        for pair, index in heads:
            key = projected_ref[:, parts[pair][1]]
            own = jnp.where(masks[index], key, jnp.zeros_like(key))
            scores.append(contract(own, projected_ref[:, parts[pair][0]], 1, 1))
        weights = []
        for (pair, index), score in zip(heads, scores):
            score = score * HEAD_DIM ** (-0.5) - slopes_ref[pair * per + index] * distance
            weight = jnp.exp(score - jnp.max(score, axis=0, keepdims=True))
            weight = weight * (1.0 / jnp.sum(weight, axis=0, keepdims=True))
            weights.append(weight.astype(BF16))
        for pair in range(first, first + group):
            value = projected_ref[:, parts[pair][2]]
            context = jnp.zeros((length, LANES), F32)
            for (other, index), weight in zip(heads, weights):
                if other == pair:
                    context = jnp.where(masks[index], contract(weight, value, 0, 0), context)
            context_ref[:, parts[pair][0]] = context.astype(BF16)


def attend_back_kernel(group, slopes_ref, projected_ref, context_grad_ref, grad_ref):
    length, features = context_grad_ref.shape
    masks = head_masks(length)
    distance = distances(length)
    per = len(masks)
    pairs = features // LANES
    for first in range(0, pairs, group):
        heads = [(pair, index) for pair in range(first, first + group) for index in range(per)]
        parts = {p: [slice(i * features + p * LANES, i * features + (p + 1) * LANES) for i in range(3)] for p, _ in heads}
        scores, weights_grads = [], []
        for pair, index in heads:
            key, value = projected_ref[:, parts[pair][1]], projected_ref[:, parts[pair][2]]
            own = jnp.where(masks[index], key, jnp.zeros_like(key))
            scores.append(contract(own, projected_ref[:, parts[pair][0]], 1, 1))
            own = jnp.where(masks[index], value, jnp.zeros_like(value))
            weights_grads.append(contract(own, context_grad_ref[:, parts[pair][0]], 1, 1))
        weights, score_grads = [], []
        for (pair, index), score, weights_grad in zip(heads, scores, weights_grads):
            score = score * HEAD_DIM ** (-0.5) - slopes_ref[pair * per + index] * distance
            weight = jnp.exp(score - jnp.max(score, axis=0, keepdims=True))
            weight = weight * (1.0 / jnp.sum(weight, axis=0, keepdims=True))
            mean_grad = jnp.sum(weight * weights_grad, axis=0, keepdims=True)
            score_grads.append((weight * (weights_grad - mean_grad)).astype(BF16))
            weights.append(weight.astype(BF16))
        for pair in range(first, first + group):
            query, key = projected_ref[:, parts[pair][0]], projected_ref[:, parts[pair][1]]
            context_grad = context_grad_ref[:, parts[pair][0]]
            grads = [jnp.zeros((length, LANES), F32)] * 3
            for (other, index), weight, score_grad in zip(heads, weights, score_grads):
                if other == pair:
                    new = [
                        contract(score_grad, key, 0, 0) * HEAD_DIM ** (-0.5),
                        contract(score_grad, query, 1, 0) * HEAD_DIM ** (-0.5),
                        contract(weight, context_grad, 1, 0),
                    ]
                    grads = [jnp.where(masks[index], n, g) for n, g in zip(new, grads)]
            for part, grad in zip(parts[pair], grads):
                grad_ref[:, part] = grad.astype(BF16)


def row_block(length, width):
    return pl.BlockSpec((length, width), lambda index: (index, 0))


def attend(projected, slopes, seqs):
    rows, width = projected.shape
    length, features = rows // seqs, width // 3
    return pl.pallas_call(
        functools.partial(attend_kernel, GROUP),
        grid=(seqs,),
        in_specs=[pl.BlockSpec(memory_space=pltpu.SMEM), row_block(length, width)],
        out_specs=row_block(length, features),
        out_shape=jax.ShapeDtypeStruct((rows, features), BF16),
        cost_estimate=pl.CostEstimate(
            flops=4 * rows * length * features, bytes_accessed=2 * rows * (width + features), transcendentals=rows * length * features // HEAD_DIM
        ),
        name="attend",
    )(slopes, projected)


def attend_back(projected, context_grad, slopes, seqs):
    rows, width = projected.shape
    length, features = rows // seqs, width // 3
    return pl.pallas_call(
        functools.partial(attend_back_kernel, GROUP_BACK),
        grid=(seqs,),
        in_specs=[
            pl.BlockSpec(memory_space=pltpu.SMEM),
            row_block(length, width),
            row_block(length, features),
        ],
        out_specs=row_block(length, width),
        out_shape=jax.ShapeDtypeStruct((rows, width), BF16),
        cost_estimate=pl.CostEstimate(
            flops=10 * rows * length * features, bytes_accessed=2 * rows * (2 * width + features), transcendentals=rows * length * features // HEAD_DIM
        ),
        name="attend_back",
    )(slopes, projected, context_grad)


def settle_kernel(chunks, kinds, part, flags_ref, *refs):
    *pieces, gate_up_ref, down_ref, held = refs
    first = flags_ref[0] == 1
    count = len(pieces) // 4
    half_rows = chunks * count * part
    for half in range(2):
        for index in range(count):
            mine = pieces[half * count + index]
            other = pieces[(2 + half) * count + index]
            place = flags_ref[1 + half * count + index]
            for chunk in range(chunks):
                base = pl.multiple_of(half * half_rows + chunk * count * part + place * part, part)
                for kind in range(kinds):
                    start = (chunk * kinds + kind) * part
                    rows = jnp.where(first, mine[start : start + part, :], other[start : start + part, :]).astype(F32)
                    if kind < kinds - 1:
                        held[kind, pl.ds(base, part), :] = rows
                    else:
                        down_ref[pl.ds(base, part), :] = rows
    for kind in range(kinds - 1):
        gate_up_ref[:, kind, :] = jnp.transpose(held[kind])


def settle(pieces, flags, chunks, kinds, part):
    rows, features = pieces[0].shape
    units = 2 * (len(pieces) // 4) * chunks * part
    width = 2 * LANES
    return pl.pallas_call(
        functools.partial(settle_kernel, chunks, kinds, part),
        grid=(features // width,),
        in_specs=[pl.BlockSpec(memory_space=pltpu.SMEM)]
        + [pl.BlockSpec((rows, width), lambda index: (0, index))] * len(pieces),
        out_specs=[
            pl.BlockSpec((width, kinds - 1, units), lambda index: (index, 0, 0)),
            pl.BlockSpec((units, width), lambda index: (0, index)),
        ],
        out_shape=[
            jax.ShapeDtypeStruct((features, kinds - 1, units), F32),
            jax.ShapeDtypeStruct((units, features), F32),
        ],
        scratch_shapes=[pltpu.VMEM((kinds - 1, units, width), F32)],
        name="settle",
    )(flags, *pieces)


def together(*trees):
    return lax.optimization_barrier(trees)


def near(chunk):
    return dict(chunk, near=exchange(chunk["own"][0], tensor_mask=1))


def far(chunk):
    return dict(chunk, far=exchange(jnp.stack([chunk["own"][0], chunk["near"]]), tensor_mask=2))


def first(chunk):
    remote = jnp.concatenate([chunk["near"][None], chunk["far"]])
    return dict(
        chunk,
        remote=remote,
        first=exchange(remote, dp_masks=FIRST),
        second=exchange(remote, dp_masks=SECOND),
    )


def second(chunk):
    return dict(chunk, third=exchange(chunk["first"], dp_masks=SECOND))


def assemble(chunk):
    rest = [chunk["remote"], chunk["first"], chunk["second"], chunk["third"]]
    return jnp.stack([jnp.concatenate([own[None], r]) for own, r in zip(chunk["own"], rest)])


def add_low(a, b):
    return (a.astype(F32) + b.astype(F32)).astype(BF16)


def total_low(*parts):
    return sum(part.astype(F32) for part in parts).astype(BF16)


def reduce_open(terms):
    return (
        terms[0],
        terms[1],
        exchange(terms[3], dp_masks=SECOND),
        exchange(terms[2], dp_masks=SECOND),
    )


def reduce_turn(parts):
    return parts[0], exchange(total_low(parts[1], parts[2]), dp_masks=FIRST)


def reduce_near(own, turned, opened):
    pairs = total_low(own, turned, opened)
    pairs = pairs.reshape((2, 2) + pairs.shape[1:])
    return pairs[:, 0], exchange(pairs[:, 1], tensor_mask=1)


def reduce_far(pair):
    terms = total_low(*pair)
    return terms[0], exchange(terms[1], tensor_mask=2)


def reduce_last(pair):
    one = total_low(*pair)
    mask = PLANE
    while mask < lax.axis_size("dp"):
        one = total_low(one, exchange(one, dp_masks=(mask, mask)))
        mask *= 2
    return one


def attn_forward(own_low, weights, norms, slopes, seqs):
    wqkv, wo = weights
    projected = dot(own_low, wqkv, 1, 1).astype(BF16)
    context = attend(projected, slopes, seqs)
    first_sum = own_low.astype(F32) + dot(context, wo, 1, 0)
    first_norm = norm_rows(first_sum, norms[0], norms[1])
    return projected, context, first_sum, first_norm


def both_rows(rows_low):
    return jnp.concatenate([rows_low, swap(rows_low)])


def join_rows(terms):
    rows = terms.shape[0] // 2
    return terms[:rows] + swap(terms[rows:].astype(BF16)).astype(F32)


def feed_forward(first_all, weights):
    gate_up, down = weights
    gated = dot(first_all, gate_up, 1, 1)
    gate_part, up_part = jnp.split(gated, 2, axis=-1)
    hidden = gelu_product(gate_part, up_part).astype(BF16)
    return gated, hidden, dot(hidden, down, 1, 0)


def feed_backward(mixed_all, weights, gated):
    hidden_grad = dot(mixed_all, weights[1], 1, 1)
    gate_part, up_part = jnp.split(gated, 2, axis=-1)
    _, gelu_back = jax.vjp(gelu_product, gate_part, up_part)
    gate_grad, up_grad = gelu_back(hidden_grad)
    return jnp.concatenate([gate_grad, up_grad], axis=-1).astype(BF16)


def feed_weight_grads(mixed_all, first_all, gated_grad, hidden):
    return dot(gated_grad, first_all, 0, 0).astype(BF16), dot(hidden, mixed_all, 0, 0).astype(BF16)


def norm_backward(total, gain, offset, grad):
    _, back = jax.vjp(norm_rows, total, gain, offset)
    return back(grad)


def context_backward(sum_grad, weights, context):
    attended_low = sum_grad.astype(BF16)
    context_grad = dot(attended_low, weights[1], 1, 1).astype(BF16)
    return context_grad, dot(context, attended_low, 0, 0).astype(BF16)


def body(
    layer_input,
    out_grad,
    loss_mask,
    query_key_value_weight,
    attention_output_weight,
    gate_up_weight,
    down_weight,
    norm1_gain,
    norm1_bias,
    norm2_gain,
    norm2_bias,
):
    core = lax.axis_index("section")
    plane = lax.axis_index("dp")
    depth = lax.axis_index("tensor")
    is_first = core == 0
    micro, own_seqs, length, features = layer_input.shape
    local = query_key_value_weight.shape[-1]
    local_heads = local // HEAD_DIM
    units = down_weight.shape[1]
    part = HEAD_DIM // PLANE
    unit_part = units // 2 // PLANE // FEED_CHUNKS
    seqs = micro * own_seqs // 2
    rows = seqs * length

    in_plane = jnp.bitwise_and(plane, PLANE - 1)

    def crossed(e):
        return (e & 1) * 2 + (e >> 1)

    def relative(slab):
        return [
            lax.dynamic_index_in_dim(
                slab, jnp.bitwise_xor(in_plane, jnp.where(is_first, e, crossed(e))), 0, keepdims=False
            )
            for e in range(PLANE)
        ]

    def share(slab):
        keep = lax.dynamic_index_in_dim(slab, core, 0, keepdims=False)
        got = swap(lax.dynamic_index_in_dim(slab, 1 - core, 0, keepdims=False))
        return jnp.where(is_first, keep, got), jnp.where(is_first, got, keep)

    qkv_rows = jnp.transpose(query_key_value_weight[0], (1, 2, 0))
    attn_rows = jnp.concatenate([qkv_rows, attention_output_weight], axis=0)
    attn_slab = attn_rows.reshape(2, 2, local_heads, PLANE, part, features)
    attn_slab = jnp.transpose(attn_slab, (0, 3, 1, 2, 4, 5)).reshape(2, PLANE, -1, features)
    attn_in = [{"own": relative(own)} for own in share(attn_slab)]
    attn_in[0] = near(attn_in[0])
    attn_in, gate_up_weight, down_weight = together(attn_in, gate_up_weight, down_weight)
    gate_up_rows = jnp.transpose(gate_up_weight[0], (1, 2, 0))
    feed_rows = jnp.concatenate([gate_up_rows, down_weight], axis=0)
    feed_slab = feed_rows.reshape(3, 2, FEED_CHUNKS, PLANE, unit_part, features)
    feed_slab = jnp.transpose(feed_slab, (2, 1, 3, 0, 4, 5)).reshape(FEED_CHUNKS, 2, PLANE, -1, features)

    feed_in = [[{"own": relative(own)} for own in share(feed_slab[k])] for k in range(FEED_CHUNKS)]
    a0, a1 = attn_in
    (p0, p1), (q0, q1) = feed_in


    norm_table = jnp.concatenate([norm1_gain, norm1_bias, norm2_gain, norm2_bias])
    norm_other = swap(norm_table)
    norm_first = jnp.where(is_first, norm_table, norm_other)
    norm_second = jnp.where(is_first, norm_other, norm_table)
    norms = [tuple(table[i] for i in range(4)) for table in (norm_first, norm_second)]

    slope_table = jnp.asarray(alibi_table(HEADS)).reshape(DEPTH, local_heads)
    slopes = jnp.concatenate(
        [lax.dynamic_index_in_dim(slope_table, jnp.bitwise_xor(depth, j), 0, keepdims=False) for j in range(DEPTH)]
    )

    def own_half(whole):
        flat = whole.reshape((2, rows) + whole.shape[3:])
        return lax.dynamic_index_in_dim(flat, core, 0, keepdims=False)

    start = own_half(layer_input)
    seed = own_half(out_grad).astype(F32) * own_half(loss_mask).astype(F32)[..., None]


    def attn_weights(chunk):
        full = assemble(chunk).reshape(PLANE, DEPTH, 2, local_heads, part, features)
        mine = jnp.transpose(full, (2, 1, 3, 0, 4, 5)).reshape(2, -1, features)
        other = swap(mine)
        qk = jnp.where(is_first, mine, other)
        vo = jnp.where(is_first, other, mine)
        wqkv = jnp.concatenate([qk.reshape(-1, features), vo[0]])
        return wqkv, vo[1]

    def feed_weights(chunk):
        full = assemble(chunk).reshape(PLANE * DEPTH, 3, unit_part, features)
        full = jnp.transpose(full, (1, 0, 2, 3)).reshape(3, -1, features)
        return full[:2].reshape(-1, features), full[2]

    a0, p0 = far(a0), near(p0)
    a0, p0, q0 = together(a0, p0, q0)
    a0, p0, q0 = first(a0), far(p0), near(q0)
    a0, p0, q0, a1 = together(a0, p0, q0, a1)
    a0, p0, q0, a1 = second(a0), first(p0), far(q0), near(a1)
    places = [jnp.bitwise_xor(in_plane, e) for e in range(PLANE)]
    places += [jnp.bitwise_xor(in_plane, crossed(e)) for e in range(PLANE)]
    flags = jnp.stack([is_first.astype(jnp.int32)] + places)
    a0, p0, q0, a1, p1, norms, seed, flags = together(a0, p0, q0, a1, p1, norms, seed, flags)
    p0, q0, a1, p1 = second(p0), first(q0), far(a1), near(p1)
    attn0 = attn_weights(a0)
    projected0, context0, sum0, norm0 = attn_forward(start, attn0, norms[0], slopes, seqs)
    low0, p0, q0, a1, p1, q1 = together(norm0.astype(BF16), p0, q0, a1, p1, q1)
    q0, a1, p1, q1 = second(q0), first(a1), far(p1), near(q1)
    all0 = both_rows(low0)
    feed_p0 = feed_weights(p0)
    gated_p0, hidden_p0, mixed = feed_forward(all0, feed_p0)
    mixed, q0, a1, p1, q1 = together(mixed, q0, a1, p1, q1)
    a1, p1, q1 = second(a1), first(p1), far(q1)
    feed_q0 = feed_weights(q0)
    gated_q0, hidden_q0, more = feed_forward(all0, feed_q0)
    mixed = mixed + more
    mixed, a1, p1, q1 = together(mixed, a1, p1, q1)
    p1, q1 = second(p1), first(q1)
    attn1 = attn_weights(a1)
    total0 = norm0 + join_rows(mixed)
    middle_low = norm_rows(total0, norms[0][2], norms[0][3]).astype(BF16)
    projected1, context1, sum1, norm1 = attn_forward(middle_low, attn1, norms[1], slopes, seqs)
    low1, p1, q1 = together(norm1.astype(BF16), p1, q1)
    q1 = second(q1)
    all1 = both_rows(low1)
    feed_p1 = feed_weights(p1)
    gated_p1, hidden_p1, mixed = feed_forward(all1, feed_p1)
    mixed, q1 = together(mixed, q1)
    feed_q1 = feed_weights(q1)
    gated_q1, hidden_q1, more = feed_forward(all1, feed_q1)
    total1 = norm1 + join_rows(mixed + more)
    final_low = norm_rows(total1, norms[1][2], norms[1][3]).astype(BF16)

    def give(early, late):
        mine = jnp.where(is_first, early, late)
        got = swap(jnp.where(is_first, late, early))
        both = jnp.concatenate([jnp.where(is_first, mine, got), jnp.where(is_first, got, mine)])
        return both.reshape((1, micro, own_seqs, length, features))

    def feed_terms(gate_up, down):
        full = jnp.concatenate([gate_up, down]).reshape(3, PLANE, DEPTH, unit_part, features)
        full = jnp.transpose(full, (1, 2, 0, 3, 4)).reshape(PLANE, DEPTH, -1, features)
        return [full[e] for e in range(PLANE)]

    def attn_terms(qkv, out, vectors):
        spread = jnp.pad(jnp.stack(vectors).astype(BF16), ((0, NORM_ROWS - len(vectors)), (0, 0)))
        spread = jnp.broadcast_to(spread, (2, PLANE, DEPTH, NORM_ROWS, features))
        full = jnp.concatenate([qkv, out]).reshape(2, 2, DEPTH, local_heads, PLANE, part, features)
        full = jnp.transpose(full, (0, 4, 2, 1, 3, 5, 6)).reshape(2, PLANE, DEPTH, -1, features)
        return jnp.concatenate([full, spread], axis=3)

    def attn_swap(full):
        keep = lax.dynamic_index_in_dim(full, core, 0, keepdims=False)
        return keep, swap(lax.dynamic_index_in_dim(full, 1 - core, 0, keepdims=False))

    def attn_pieces(pair):
        full = total_low(*pair)
        return [full[e] for e in range(PLANE)]

    def hand_over(block, source):
        planes, depths = lax.axis_size("dp"), lax.axis_size("tensor")
        count = planes * depths
        pairs = [(source * count + i, (1 - source) * count + i) for i in range(count)]
        return lax.ppermute(block, AXES, pairs)

    second_grad, gain_two1, offset_two1 = norm_backward(total1, norms[1][2], norms[1][3], seed)
    mixed_all = both_rows(second_grad.astype(BF16))
    grad_p = feed_backward(mixed_all, feed_p1, gated_p1)
    p1 = feed_terms(*feed_weight_grads(mixed_all, all1, grad_p, hidden_p1))
    mixed_all, grad_p, p1 = together(mixed_all, grad_p, p1)

    p1_own, p1_half, p1_a, p1_b = reduce_open(p1)
    terms = dot(grad_p, feed_p1[0], 1, 0)
    grad_q = feed_backward(mixed_all, feed_q1, gated_q1)
    terms = terms + dot(grad_q, feed_q1[0], 1, 0)
    q1 = feed_terms(*feed_weight_grads(mixed_all, all1, grad_q, hidden_q1))
    layer_out = give(middle_low, final_low)
    terms, q1, p1_a, layer_out = together(terms, q1, p1_a, layer_out)

    p1_own, p1_c = reduce_turn((p1_own, p1_half, p1_a))
    first_grad = join_rows(terms) + second_grad
    sum_grad, gain_one1, offset_one1 = norm_backward(sum1, norms[1][0], norms[1][1], first_grad)
    context_grad, out = context_backward(sum_grad, attn1, context1)
    context_grad, out, q1, p1_b = together(context_grad, out, q1, p1_b)

    q1_own, q1_half, q1_a, q1_b = reduce_open(q1)
    projected_grad = attend_back(projected1, context_grad, slopes, seqs)
    qkv = dot(projected_grad, middle_low, 0, 0).astype(BF16)
    a1 = attn_terms(qkv, out, [gain_one1, offset_one1, gain_two1, offset_two1])
    projected_grad, a1, q1_a, p1_c = together(projected_grad, a1, q1_a, p1_c)

    a1 = attn_swap(a1)
    q1_own, q1_c = reduce_turn((q1_own, q1_half, q1_a))
    p1 = reduce_near(p1_own, p1_c, p1_b)
    middle_grad = dot(projected_grad, attn1[0], 1, 0) + sum_grad
    second_grad, gain_two0, offset_two0 = norm_backward(total0, norms[0][2], norms[0][3], middle_grad)
    mixed_low = second_grad.astype(BF16)
    mixed_low, a1, q1_b, p1 = together(mixed_low, a1, q1_b, p1)

    mixed_all = both_rows(mixed_low)
    a1_own, a1_half, a1_a, a1_b = reduce_open(attn_pieces(a1))
    p1 = reduce_far(p1)
    grad_p = feed_backward(mixed_all, feed_p0, gated_p0)
    mixed_all, grad_p, a1_a, q1_c, p1 = together(mixed_all, grad_p, a1_a, q1_c, p1)

    a1_own, a1_c = reduce_turn((a1_own, a1_half, a1_a))
    q1 = reduce_near(q1_own, q1_c, q1_b)
    p0 = feed_terms(*feed_weight_grads(mixed_all, all0, grad_p, hidden_p0))
    terms = dot(grad_p, feed_p0[0], 1, 0)
    mixed_all, terms, p0, a1_b, q1 = together(mixed_all, terms, p0, a1_b, q1)

    p0_own, p0_half, p0_a, p0_b = reduce_open(p0)
    q1 = reduce_far(q1)
    grad_q = feed_backward(mixed_all, feed_q0, gated_q0)
    terms = terms + dot(grad_q, feed_q0[0], 1, 0)
    terms, grad_q, p0_a, a1_c, q1 = together(terms, grad_q, p0_a, a1_c, q1)

    p0_own, p0_c = reduce_turn((p0_own, p0_half, p0_a))
    a1 = reduce_near(a1_own, a1_c, a1_b)
    late = jnp.concatenate([reduce_last(p1), reduce_last(q1)])
    late_first = exchange(late, dp_masks=FIRST)
    q0 = feed_terms(*feed_weight_grads(mixed_all, all0, grad_q, hidden_q0))
    first_grad = join_rows(terms) + second_grad
    sum_grad, gain_one0, offset_one0 = norm_backward(sum0, norms[0][0], norms[0][1], first_grad)
    sum_grad, q0, p0_b, a1, late, late_first = together(sum_grad, q0, p0_b, a1, late, late_first)

    q0_own, q0_half, q0_a, q0_b = reduce_open(q0)
    a1 = reduce_far(a1)
    context_grad, out = context_backward(sum_grad, attn0, context0)
    projected_grad = attend_back(projected0, context_grad, slopes, seqs)
    qkv = dot(projected_grad, start, 0, 0).astype(BF16)
    a0 = attn_terms(qkv, out, [gain_one0, offset_one0, gain_two0, offset_two0])
    late_second = exchange(late, dp_masks=SECOND)
    projected_grad, a0, q0_a, p0_c, a1, late_second = together(projected_grad, a0, q0_a, p0_c, a1, late_second)

    a0 = attn_swap(a0)
    q0_own, q0_c = reduce_turn((q0_own, q0_half, q0_a))
    start_grad = dot(projected_grad, attn0[0], 1, 0) + sum_grad
    start_grad, a0, q0_b = together(start_grad, a0, q0_b)

    a0 = attn_pieces(a0)
    a0_got = exchange(jnp.stack(a0[2:]), dp_masks=SECOND)
    p0 = reduce_near(p0_own, p0_c, p0_b)
    input_grad = give(start_grad, middle_grad)
    a0_got, q0_c, p0, input_grad = together(a0_got, q0_c, p0, input_grad)

    a0_c = exchange(total_low(a0[1], a0_got[1]), dp_masks=FIRST)
    q0 = reduce_near(q0_own, q0_c, q0_b)
    p0 = reduce_far(p0)
    late_third = exchange(late_first, dp_masks=SECOND)
    late_got = [hand_over(late, 0), hand_over(late_first, 0)]
    a0_c, q0, p0, late_third, late_got = together(a0_c, q0, p0, late_third, late_got)

    a0 = reduce_near(a0[0], a0_got[0], a0_c)
    q0 = reduce_far(q0)
    attn_late = reduce_last(a1)
    attn = attn_late[:-NORM_ROWS]
    late_attn = [attn, exchange(attn, dp_masks=FIRST), exchange(attn, dp_masks=SECOND)]
    late_got += [hand_over(late_second, 0), hand_over(late_third, 0)]
    a0, q0, late_attn, late_got = together(a0, q0, late_attn, late_got)

    a0 = reduce_far(a0)
    late_attn.append(exchange(late_attn[1], dp_masks=SECOND))
    feed = jnp.concatenate([reduce_last(p0), reduce_last(q0)])
    feed_first = exchange(feed, dp_masks=FIRST)
    feed_got = [hand_over(feed, 1)]
    a0, late_attn, feed, feed_first, feed_got = together(a0, late_attn, feed, feed_first, feed_got)

    attn_early = reduce_last(a0)
    attn = attn_early[:-NORM_ROWS]
    attn_first, attn_second = exchange(attn, dp_masks=FIRST), exchange(attn, dp_masks=SECOND)
    feed_second = exchange(feed, dp_masks=SECOND)
    attn_late_all = jnp.stack(late_attn)
    attn_late_got = hand_over(attn_late_all, 0)
    feed_got.append(hand_over(feed_first, 1))
    attn_first, attn_second, feed_second, attn_late_got, feed_got = together(
        attn_first, attn_second, feed_second, attn_late_got, feed_got
    )

    attn_third, feed_third = exchange(attn_first, dp_masks=SECOND), exchange(feed_first, dp_masks=SECOND)
    feed_got.append(hand_over(feed_second, 1))
    attn_early_all = jnp.stack([attn, attn_first, attn_second, attn_third])
    attn_got = hand_over(attn_early_all, 1)
    feed_got.append(hand_over(feed_third, 1))

    feed_early = [feed, feed_first, feed_second, feed_third]
    feed_late = [late, late_first, late_second, late_third]
    grad_in, grad_down = settle(
        feed_early + feed_got + late_got + feed_late, flags, FEED_CHUNKS, 3, unit_part
    )
    parts = [jnp.where(is_first, attn_early_all, attn_late_got), jnp.where(is_first, attn_got, attn_late_all)]
    attn_total = jnp.stack(
        [
            jnp.stack(
                [
                    lax.dynamic_index_in_dim(parts[0], jnp.bitwise_xor(in_plane, index), 0, keepdims=False),
                    lax.dynamic_index_in_dim(parts[1], crossed(jnp.bitwise_xor(in_plane, index)), 0, keepdims=False),
                ]
            )
            for index in range(PLANE)
        ]
    )
    attn_total = attn_total.reshape(PLANE, 2, 2, local_heads, part, features)
    attn_total = jnp.transpose(attn_total, (1, 2, 3, 0, 4, 5)).reshape(4, local, features).astype(F32)
    grad_qkv = jnp.transpose(attn_total[:3], (2, 0, 1))
    grad_out = attn_total[3]

    vectors = jnp.where(is_first, attn_early[-NORM_ROWS:], attn_late[-NORM_ROWS:]).astype(F32)
    vectors = lax.dynamic_slice_in_dim(vectors, depth * local, local, 1)

    return (
        layer_out,
        input_grad,
        grad_qkv[None],
        grad_out[None],
        grad_in[None],
        grad_down[None],
        vectors[0][None],
        vectors[1][None],
        vectors[2][None],
        vectors[3][None],
    )


def solution(mesh):
    placed = (
        P(None, ("dp", "tensor"), None, None),
        P(None, ("dp", "tensor"), None, None),
        P(None, ("dp", "tensor"), None),
        P("section", None, None, "tensor"),
        P("section", "tensor", None),
        P("section", None, None, "tensor"),
        P("section", "tensor", None),
        P("section", None),
        P("section", None),
        P("section", None),
        P("section", None),
    )
    return jax.shard_map(
        body,
        mesh=mesh,
        in_specs=placed,
        out_specs=(
            P("section", None, ("dp", "tensor"), None, None),
            P("section", None, ("dp", "tensor"), None, None),
            P("section", None, None, "tensor"),
            P("section", "tensor", None),
            P("section", None, None, "tensor"),
            P("section", "tensor", None),
            P("section", "tensor"),
            P("section", "tensor"),
            P("section", "tensor"),
            P("section", "tensor"),
        ),
        check_vma=False,
    )
```

```python
import functools
import math

import jax
import jax.numpy as jnp
import numpy as np
from jax import lax
from jax.experimental import pallas as pl
from jax.experimental.pallas import tpu as pltpu
from jax.sharding import PartitionSpec as P

HEADS = 12
HEAD_DIM = 64
NORM_EPSILON = 1e-05
AXES = ("section", "dp", "tensor")
FEED_CHUNKS = 2
NORM_ROWS = 16
LANES = 128
GROUP = 3
GROUP_BACK = 3

F32 = jnp.float32
BF16 = jnp.bfloat16


def power_slopes(total_heads):
    return [2.0 ** (-8.0 * (index + 1) / total_heads) for index in range(total_heads)]


def alibi_table(number_heads):
    closest = 2 ** int(math.floor(math.log2(number_heads)))
    slopes = power_slopes(closest)
    slopes = slopes + power_slopes(2 * closest)[0::2][: number_heads - closest]
    return np.array(slopes, dtype=np.float32)


def norm_rows(values, gain, offset):
    row_mean = jnp.mean(values, axis=-1, keepdims=True)
    centred = values - row_mean
    row_var = jnp.mean(centred * centred, axis=-1, keepdims=True)
    return centred * lax.rsqrt(row_var + NORM_EPSILON) * gain + offset


def gelu_product(gate_part, up_part):
    return jax.nn.gelu(gate_part, approximate=False) * up_part


def dot(a, b, ca, cb):
    return lax.dot_general(a, b, (((ca,), (cb,)), ((), ())), preferred_element_type=F32)


def exchange(block, section_mask=0, dp_masks=(0, 0), tensor_mask=0):
    dp = lax.axis_size("dp")
    tensor = lax.axis_size("tensor")
    pairs = []
    for s in range(lax.axis_size("section")):
        for d in range(dp):
            for t in range(tensor):
                target = ((s ^ section_mask) * dp + (d ^ dp_masks[s])) * tensor + (t ^ tensor_mask)
                pairs.append(((s * dp + d) * tensor + t, target))
    return lax.ppermute(block, AXES, pairs)


def swap(block):
    return exchange(block, section_mask=1)


FIRST = (1, 2)
SECOND = (2, 1)
PLANE = 4
DEPTH = 4


def contract(a, b, ca, cb):
    return lax.dot_general(a, b, (((ca,), (cb,)), ((), ())), preferred_element_type=F32)


def head_masks(length):
    lane = lax.broadcasted_iota(jnp.int32, (length, LANES), 1)
    return [lane // HEAD_DIM == index for index in range(LANES // HEAD_DIM)]


def distances(length):
    across = lax.broadcasted_iota(jnp.int32, (length, length), 0)
    along = lax.broadcasted_iota(jnp.int32, (length, length), 1)
    return jnp.abs(across - along).astype(F32)


def attend_kernel(group, slopes_ref, projected_ref, context_ref):
    length, features = context_ref.shape
    masks = head_masks(length)
    distance = distances(length)
    per = len(masks)
    pairs = features // LANES
    for first in range(0, pairs, group):
        heads = [(pair, index) for pair in range(first, first + group) for index in range(per)]
        parts = {p: [slice(i * features + p * LANES, i * features + (p + 1) * LANES) for i in range(3)] for p, _ in heads}
        scores = []
        for pair, index in heads:
            key = projected_ref[:, parts[pair][1]]
            own = jnp.where(masks[index], key, jnp.zeros_like(key))
            scores.append(contract(own, projected_ref[:, parts[pair][0]], 1, 1))
        weights = []
        for (pair, index), score in zip(heads, scores):
            score = score * HEAD_DIM ** (-0.5) - slopes_ref[pair * per + index] * distance
            weight = jnp.exp(score - jnp.max(score, axis=0, keepdims=True))
            weight = weight * (1.0 / jnp.sum(weight, axis=0, keepdims=True))
            weights.append(weight.astype(BF16))
        for pair in range(first, first + group):
            value = projected_ref[:, parts[pair][2]]
            context = jnp.zeros((length, LANES), F32)
            for (other, index), weight in zip(heads, weights):
                if other == pair:
                    context = jnp.where(masks[index], contract(weight, value, 0, 0), context)
            context_ref[:, parts[pair][0]] = context.astype(BF16)


def attend_back_kernel(group, slopes_ref, projected_ref, context_grad_ref, grad_ref):
    length, features = context_grad_ref.shape
    masks = head_masks(length)
    distance = distances(length)
    per = len(masks)
    pairs = features // LANES
    for first in range(0, pairs, group):
        heads = [(pair, index) for pair in range(first, first + group) for index in range(per)]
        parts = {p: [slice(i * features + p * LANES, i * features + (p + 1) * LANES) for i in range(3)] for p, _ in heads}
        scores, weights_grads = [], []
        for pair, index in heads:
            key, value = projected_ref[:, parts[pair][1]], projected_ref[:, parts[pair][2]]
            own = jnp.where(masks[index], key, jnp.zeros_like(key))
            scores.append(contract(own, projected_ref[:, parts[pair][0]], 1, 1))
            own = jnp.where(masks[index], value, jnp.zeros_like(value))
            weights_grads.append(contract(own, context_grad_ref[:, parts[pair][0]], 1, 1))
        weights, score_grads = [], []
        for (pair, index), score, weights_grad in zip(heads, scores, weights_grads):
            score = score * HEAD_DIM ** (-0.5) - slopes_ref[pair * per + index] * distance
            weight = jnp.exp(score - jnp.max(score, axis=0, keepdims=True))
            weight = weight * (1.0 / jnp.sum(weight, axis=0, keepdims=True))
            mean_grad = jnp.sum(weight * weights_grad, axis=0, keepdims=True)
            score_grads.append((weight * (weights_grad - mean_grad)).astype(BF16))
            weights.append(weight.astype(BF16))
        for pair in range(first, first + group):
            query, key = projected_ref[:, parts[pair][0]], projected_ref[:, parts[pair][1]]
            context_grad = context_grad_ref[:, parts[pair][0]]
            grads = [jnp.zeros((length, LANES), F32)] * 3
            for (other, index), weight, score_grad in zip(heads, weights, score_grads):
                if other == pair:
                    new = [
                        contract(score_grad, key, 0, 0) * HEAD_DIM ** (-0.5),
                        contract(score_grad, query, 1, 0) * HEAD_DIM ** (-0.5),
                        contract(weight, context_grad, 1, 0),
                    ]
                    grads = [jnp.where(masks[index], n, g) for n, g in zip(new, grads)]
            for part, grad in zip(parts[pair], grads):
                grad_ref[:, part] = grad.astype(BF16)


def row_block(length, width):
    return pl.BlockSpec((length, width), lambda index: (index, 0))


def attend(projected, slopes, seqs):
    rows, width = projected.shape
    length, features = rows // seqs, width // 3
    return pl.pallas_call(
        functools.partial(attend_kernel, GROUP),
        grid=(seqs,),
        in_specs=[pl.BlockSpec(memory_space=pltpu.SMEM), row_block(length, width)],
        out_specs=row_block(length, features),
        out_shape=jax.ShapeDtypeStruct((rows, features), BF16),
        cost_estimate=pl.CostEstimate(
            flops=4 * rows * length * features, bytes_accessed=2 * rows * (width + features), transcendentals=rows * length * features // HEAD_DIM
        ),
        name="attend",
    )(slopes, projected)


def attend_back(projected, context_grad, slopes, seqs):
    rows, width = projected.shape
    length, features = rows // seqs, width // 3
    return pl.pallas_call(
        functools.partial(attend_back_kernel, GROUP_BACK),
        grid=(seqs,),
        in_specs=[
            pl.BlockSpec(memory_space=pltpu.SMEM),
            row_block(length, width),
            row_block(length, features),
        ],
        out_specs=row_block(length, width),
        out_shape=jax.ShapeDtypeStruct((rows, width), BF16),
        cost_estimate=pl.CostEstimate(
            flops=10 * rows * length * features, bytes_accessed=2 * rows * (2 * width + features), transcendentals=rows * length * features // HEAD_DIM
        ),
        name="attend_back",
    )(slopes, projected, context_grad)


def settle_kernel(chunks, kinds, part, flags_ref, *refs):
    *pieces, gate_up_ref, down_ref, held = refs
    first = flags_ref[0] == 1
    count = len(pieces) // 4
    half_rows = chunks * count * part
    for half in range(2):
        for index in range(count):
            mine = pieces[half * count + index]
            other = pieces[(2 + half) * count + index]
            place = flags_ref[1 + half * count + index]
            for chunk in range(chunks):
                base = pl.multiple_of(half * half_rows + chunk * count * part + place * part, part)
                for kind in range(kinds):
                    start = (chunk * kinds + kind) * part
                    rows = jnp.where(first, mine[start : start + part, :], other[start : start + part, :]).astype(F32)
                    if kind < kinds - 1:
                        held[kind, pl.ds(base, part), :] = rows
                    else:
                        down_ref[pl.ds(base, part), :] = rows
    for kind in range(kinds - 1):
        gate_up_ref[:, kind, :] = jnp.transpose(held[kind])


def settle(pieces, flags, chunks, kinds, part):
    rows, features = pieces[0].shape
    units = 2 * (len(pieces) // 4) * chunks * part
    width = 2 * LANES
    return pl.pallas_call(
        functools.partial(settle_kernel, chunks, kinds, part),
        grid=(features // width,),
        in_specs=[pl.BlockSpec(memory_space=pltpu.SMEM)]
        + [pl.BlockSpec((rows, width), lambda index: (0, index))] * len(pieces),
        out_specs=[
            pl.BlockSpec((width, kinds - 1, units), lambda index: (index, 0, 0)),
            pl.BlockSpec((units, width), lambda index: (0, index)),
        ],
        out_shape=[
            jax.ShapeDtypeStruct((features, kinds - 1, units), F32),
            jax.ShapeDtypeStruct((units, features), F32),
        ],
        scratch_shapes=[pltpu.VMEM((kinds - 1, units, width), F32)],
        name="settle",
    )(flags, *pieces)


def together(*trees):
    return lax.optimization_barrier(trees)


def near(chunk):
    return dict(chunk, near=exchange(chunk["own"][0], tensor_mask=1))


def far(chunk):
    return dict(chunk, far=exchange(jnp.stack([chunk["own"][0], chunk["near"]]), tensor_mask=2))


def first(chunk):
    remote = jnp.concatenate([chunk["near"][None], chunk["far"]])
    return dict(
        chunk,
        remote=remote,
        first=exchange(remote, dp_masks=FIRST),
        second=exchange(remote, dp_masks=SECOND),
    )


def second(chunk):
    return dict(chunk, third=exchange(chunk["first"], dp_masks=SECOND))


def assemble(chunk):
    rest = [chunk["remote"], chunk["first"], chunk["second"], chunk["third"]]
    return jnp.stack([jnp.concatenate([own[None], r]) for own, r in zip(chunk["own"], rest)])


def add_low(a, b):
    return (a.astype(F32) + b.astype(F32)).astype(BF16)


def total_low(*parts):
    return sum(part.astype(F32) for part in parts).astype(BF16)


def reduce_open(terms):
    return (
        terms[0],
        terms[1],
        exchange(terms[3], dp_masks=SECOND),
        exchange(terms[2], dp_masks=SECOND),
    )


def reduce_turn(parts):
    return parts[0], exchange(total_low(parts[1], parts[2]), dp_masks=FIRST)


def reduce_near(own, turned, opened):
    pairs = total_low(own, turned, opened)
    pairs = pairs.reshape((2, 2) + pairs.shape[1:])
    return pairs[:, 0], exchange(pairs[:, 1], tensor_mask=1)


def reduce_far(pair):
    terms = total_low(*pair)
    return terms[0], exchange(terms[1], tensor_mask=2)


def reduce_last(pair):
    one = total_low(*pair)
    mask = PLANE
    while mask < lax.axis_size("dp"):
        one = total_low(one, exchange(one, dp_masks=(mask, mask)))
        mask *= 2
    return one


def attn_forward(own_low, weights, norms, slopes, seqs):
    wqkv, wo = weights
    projected = dot(own_low, wqkv, 1, 1).astype(BF16)
    context = attend(projected, slopes, seqs)
    first_sum = own_low.astype(F32) + dot(context, wo, 1, 0)
    first_norm = norm_rows(first_sum, norms[0], norms[1])
    return projected, context, first_sum, first_norm


def both_rows(rows_low):
    return jnp.concatenate([rows_low, swap(rows_low)])


def join_rows(terms):
    rows = terms.shape[0] // 2
    return terms[:rows] + swap(terms[rows:].astype(BF16)).astype(F32)


def feed_forward(first_all, weights):
    gate_up, down = weights
    gated = dot(first_all, gate_up, 1, 1)
    gate_part, up_part = jnp.split(gated, 2, axis=-1)
    hidden = gelu_product(gate_part, up_part).astype(BF16)
    return gated, hidden, dot(hidden, down, 1, 0)


def feed_backward(mixed_all, weights, gated):
    hidden_grad = dot(mixed_all, weights[1], 1, 1)
    gate_part, up_part = jnp.split(gated, 2, axis=-1)
    _, gelu_back = jax.vjp(gelu_product, gate_part, up_part)
    gate_grad, up_grad = gelu_back(hidden_grad)
    return jnp.concatenate([gate_grad, up_grad], axis=-1).astype(BF16)


def feed_weight_grads(mixed_all, first_all, gated_grad, hidden):
    return dot(gated_grad, first_all, 0, 0).astype(BF16), dot(hidden, mixed_all, 0, 0).astype(BF16)


def norm_backward(total, gain, offset, grad):
    _, back = jax.vjp(norm_rows, total, gain, offset)
    return back(grad)


def context_backward(sum_grad, weights, context):
    attended_low = sum_grad.astype(BF16)
    context_grad = dot(attended_low, weights[1], 1, 1).astype(BF16)
    return context_grad, dot(context, attended_low, 0, 0).astype(BF16)


def body(
    layer_input,
    out_grad,
    loss_mask,
    query_key_value_weight,
    attention_output_weight,
    gate_up_weight,
    down_weight,
    norm1_gain,
    norm1_bias,
    norm2_gain,
    norm2_bias,
):
    core = lax.axis_index("section")
    plane = lax.axis_index("dp")
    depth = lax.axis_index("tensor")
    is_first = core == 0
    micro, own_seqs, length, features = layer_input.shape
    local = query_key_value_weight.shape[-1]
    local_heads = local // HEAD_DIM
    units = down_weight.shape[1]
    part = HEAD_DIM // PLANE
    unit_part = units // 2 // PLANE // FEED_CHUNKS
    seqs = micro * own_seqs // 2
    rows = seqs * length

    in_plane = jnp.bitwise_and(plane, PLANE - 1)

    def crossed(e):
        return (e & 1) * 2 + (e >> 1)

    def relative(slab):
        return [
            lax.dynamic_index_in_dim(
                slab, jnp.bitwise_xor(in_plane, jnp.where(is_first, e, crossed(e))), 0, keepdims=False
            )
            for e in range(PLANE)
        ]

    def share(slab):
        keep = lax.dynamic_index_in_dim(slab, core, 0, keepdims=False)
        got = swap(lax.dynamic_index_in_dim(slab, 1 - core, 0, keepdims=False))
        return jnp.where(is_first, keep, got), jnp.where(is_first, got, keep)

    qkv_rows = jnp.transpose(query_key_value_weight[0], (1, 2, 0))
    attn_rows = jnp.concatenate([qkv_rows, attention_output_weight], axis=0)
    attn_slab = attn_rows.reshape(2, 2, local_heads, PLANE, part, features)
    attn_slab = jnp.transpose(attn_slab, (0, 3, 1, 2, 4, 5)).reshape(2, PLANE, -1, features)
    attn_in = [{"own": relative(own)} for own in share(attn_slab)]
    attn_in[0] = near(attn_in[0])
    attn_in, gate_up_weight, down_weight = together(attn_in, gate_up_weight, down_weight)
    gate_up_rows = jnp.transpose(gate_up_weight[0], (1, 2, 0))
    feed_rows = jnp.concatenate([gate_up_rows, down_weight], axis=0)
    feed_slab = feed_rows.reshape(3, 2, FEED_CHUNKS, PLANE, unit_part, features)
    feed_slab = jnp.transpose(feed_slab, (2, 1, 3, 0, 4, 5)).reshape(FEED_CHUNKS, 2, PLANE, -1, features)

    feed_in = [[{"own": relative(own)} for own in share(feed_slab[k])] for k in range(FEED_CHUNKS)]
    a0, a1 = attn_in
    (p0, p1), (q0, q1) = feed_in


    norm_table = jnp.concatenate([norm1_gain, norm1_bias, norm2_gain, norm2_bias])
    norm_other = swap(norm_table)
    norm_first = jnp.where(is_first, norm_table, norm_other)
    norm_second = jnp.where(is_first, norm_other, norm_table)
    norms = [tuple(table[i] for i in range(4)) for table in (norm_first, norm_second)]

    slope_table = jnp.asarray(alibi_table(HEADS)).reshape(DEPTH, local_heads)
    slopes = jnp.concatenate(
        [lax.dynamic_index_in_dim(slope_table, jnp.bitwise_xor(depth, j), 0, keepdims=False) for j in range(DEPTH)]
    )

    def own_half(whole):
        flat = whole.reshape((2, rows) + whole.shape[3:])
        return lax.dynamic_index_in_dim(flat, core, 0, keepdims=False)

    start = own_half(layer_input)
    seed = own_half(out_grad).astype(F32) * own_half(loss_mask).astype(F32)[..., None]


    def attn_weights(chunk):
        full = assemble(chunk).reshape(PLANE, DEPTH, 2, local_heads, part, features)
        mine = jnp.transpose(full, (2, 1, 3, 0, 4, 5)).reshape(2, -1, features)
        other = swap(mine)
        qk = jnp.where(is_first, mine, other)
        vo = jnp.where(is_first, other, mine)
        wqkv = jnp.concatenate([qk.reshape(-1, features), vo[0]])
        return wqkv, vo[1]

    def feed_weights(chunk):
        full = assemble(chunk).reshape(PLANE * DEPTH, 3, unit_part, features)
        full = jnp.transpose(full, (1, 0, 2, 3)).reshape(3, -1, features)
        return full[:2].reshape(-1, features), full[2]

    a0, p0 = far(a0), near(p0)
    a0, p0, q0, norms = together(a0, p0, q0, norms)
    a0, p0, q0 = first(a0), far(p0), near(q0)
    a0, p0, q0, a1 = together(a0, p0, q0, a1)
    a0, p0, q0, a1 = second(a0), first(p0), far(q0), near(a1)
    a0, p0, q0, a1, p1 = together(a0, p0, q0, a1, p1)
    p0, q0, a1, p1 = second(p0), first(q0), far(a1), near(p1)
    attn0 = attn_weights(a0)
    projected0, context0, sum0, norm0 = attn_forward(start, attn0, norms[0], slopes, seqs)
    low0, p0, q0, a1, p1, q1 = together(norm0.astype(BF16), p0, q0, a1, p1, q1)
    q0, a1, p1, q1 = second(q0), first(a1), far(p1), near(q1)
    all0 = both_rows(low0)
    feed_p0 = feed_weights(p0)
    gated_p0, hidden_p0, mixed = feed_forward(all0, feed_p0)
    mixed, q0, a1, p1, q1 = together(mixed, q0, a1, p1, q1)
    a1, p1, q1 = second(a1), first(p1), far(q1)
    feed_q0 = feed_weights(q0)
    gated_q0, hidden_q0, more = feed_forward(all0, feed_q0)
    mixed = mixed + more
    places = [jnp.bitwise_xor(in_plane, e) for e in range(PLANE)]
    places += [jnp.bitwise_xor(in_plane, crossed(e)) for e in range(PLANE)]
    flags = jnp.stack([is_first.astype(jnp.int32)] + places)
    mixed, a1, p1, q1, seed, flags = together(mixed, a1, p1, q1, seed, flags)
    p1, q1 = second(p1), first(q1)
    attn1 = attn_weights(a1)
    total0 = norm0 + join_rows(mixed)
    middle_low = norm_rows(total0, norms[0][2], norms[0][3]).astype(BF16)
    projected1, context1, sum1, norm1 = attn_forward(middle_low, attn1, norms[1], slopes, seqs)
    low1, p1, q1 = together(norm1.astype(BF16), p1, q1)
    q1 = second(q1)
    all1 = both_rows(low1)
    feed_p1 = feed_weights(p1)
    gated_p1, hidden_p1, mixed = feed_forward(all1, feed_p1)
    mixed, q1 = together(mixed, q1)
    feed_q1 = feed_weights(q1)
    gated_q1, hidden_q1, more = feed_forward(all1, feed_q1)
    total1 = norm1 + join_rows(mixed + more)
    final_low = norm_rows(total1, norms[1][2], norms[1][3]).astype(BF16)

    def give(early, late):
        mine = jnp.where(is_first, early, late)
        got = swap(jnp.where(is_first, late, early))
        both = jnp.concatenate([jnp.where(is_first, mine, got), jnp.where(is_first, got, mine)])
        return both.reshape((1, micro, own_seqs, length, features))

    def feed_terms(gate_up, down):
        full = jnp.concatenate([gate_up, down]).reshape(3, PLANE, DEPTH, unit_part, features)
        full = jnp.transpose(full, (1, 2, 0, 3, 4)).reshape(PLANE, DEPTH, -1, features)
        return [full[e] for e in range(PLANE)]

    def attn_terms(qkv, out, vectors):
        spread = jnp.pad(jnp.stack(vectors).astype(BF16), ((0, NORM_ROWS - len(vectors)), (0, 0)))
        spread = jnp.broadcast_to(spread, (2, PLANE, DEPTH, NORM_ROWS, features))
        full = jnp.concatenate([qkv, out]).reshape(2, 2, DEPTH, local_heads, PLANE, part, features)
        full = jnp.transpose(full, (0, 4, 2, 1, 3, 5, 6)).reshape(2, PLANE, DEPTH, -1, features)
        return jnp.concatenate([full, spread], axis=3)

    def attn_swap(full):
        keep = lax.dynamic_index_in_dim(full, core, 0, keepdims=False)
        return keep, swap(lax.dynamic_index_in_dim(full, 1 - core, 0, keepdims=False))

    def attn_pieces(pair):
        full = total_low(*pair)
        return [full[e] for e in range(PLANE)]

    def hand_over(block, source):
        planes, depths = lax.axis_size("dp"), lax.axis_size("tensor")
        count = planes * depths
        pairs = [(source * count + i, (1 - source) * count + i) for i in range(count)]
        return lax.ppermute(block, AXES, pairs)

    second_grad, gain_two1, offset_two1 = norm_backward(total1, norms[1][2], norms[1][3], seed)
    mixed_all = both_rows(second_grad.astype(BF16))
    grad_p = feed_backward(mixed_all, feed_p1, gated_p1)
    p1 = feed_terms(*feed_weight_grads(mixed_all, all1, grad_p, hidden_p1))
    mixed_all, grad_p, p1 = together(mixed_all, grad_p, p1)

    p1_own, p1_half, p1_a, p1_b = reduce_open(p1)
    terms = dot(grad_p, feed_p1[0], 1, 0)
    grad_q = feed_backward(mixed_all, feed_q1, gated_q1)
    terms = terms + dot(grad_q, feed_q1[0], 1, 0)
    q1 = feed_terms(*feed_weight_grads(mixed_all, all1, grad_q, hidden_q1))
    layer_out = give(middle_low, final_low)
    terms, q1, p1_a, layer_out = together(terms, q1, p1_a, layer_out)

    p1_own, p1_c = reduce_turn((p1_own, p1_half, p1_a))
    first_grad = join_rows(terms) + second_grad
    sum_grad, gain_one1, offset_one1 = norm_backward(sum1, norms[1][0], norms[1][1], first_grad)
    context_grad, out = context_backward(sum_grad, attn1, context1)
    context_grad, out, q1, p1_b = together(context_grad, out, q1, p1_b)

    q1_own, q1_half, q1_a, q1_b = reduce_open(q1)
    projected_grad = attend_back(projected1, context_grad, slopes, seqs)
    qkv = dot(projected_grad, middle_low, 0, 0).astype(BF16)
    a1 = attn_terms(qkv, out, [gain_one1, offset_one1, gain_two1, offset_two1])
    projected_grad, a1, q1_a, p1_c = together(projected_grad, a1, q1_a, p1_c)

    a1 = attn_swap(a1)
    q1_own, q1_c = reduce_turn((q1_own, q1_half, q1_a))
    p1 = reduce_near(p1_own, p1_c, p1_b)
    middle_grad = dot(projected_grad, attn1[0], 1, 0) + sum_grad
    second_grad, gain_two0, offset_two0 = norm_backward(total0, norms[0][2], norms[0][3], middle_grad)
    mixed_low = second_grad.astype(BF16)
    mixed_low, a1, q1_b, p1 = together(mixed_low, a1, q1_b, p1)

    mixed_all = both_rows(mixed_low)
    a1_own, a1_half, a1_a, a1_b = reduce_open(attn_pieces(a1))
    p1 = reduce_far(p1)
    grad_p = feed_backward(mixed_all, feed_p0, gated_p0)
    mixed_all, grad_p, a1_a, q1_c, p1 = together(mixed_all, grad_p, a1_a, q1_c, p1)

    a1_own, a1_c = reduce_turn((a1_own, a1_half, a1_a))
    q1 = reduce_near(q1_own, q1_c, q1_b)
    p0 = feed_terms(*feed_weight_grads(mixed_all, all0, grad_p, hidden_p0))
    terms = dot(grad_p, feed_p0[0], 1, 0)
    mixed_all, terms, p0, a1_b, q1 = together(mixed_all, terms, p0, a1_b, q1)

    p0_own, p0_half, p0_a, p0_b = reduce_open(p0)
    q1 = reduce_far(q1)
    grad_q = feed_backward(mixed_all, feed_q0, gated_q0)
    terms = terms + dot(grad_q, feed_q0[0], 1, 0)
    terms, grad_q, p0_a, a1_c, q1 = together(terms, grad_q, p0_a, a1_c, q1)

    p0_own, p0_c = reduce_turn((p0_own, p0_half, p0_a))
    a1 = reduce_near(a1_own, a1_c, a1_b)
    late = jnp.concatenate([reduce_last(p1), reduce_last(q1)])
    late_first = exchange(late, dp_masks=FIRST)
    q0 = feed_terms(*feed_weight_grads(mixed_all, all0, grad_q, hidden_q0))
    first_grad = join_rows(terms) + second_grad
    sum_grad, gain_one0, offset_one0 = norm_backward(sum0, norms[0][0], norms[0][1], first_grad)
    sum_grad, q0, p0_b, a1, late, late_first = together(sum_grad, q0, p0_b, a1, late, late_first)

    q0_own, q0_half, q0_a, q0_b = reduce_open(q0)
    a1 = reduce_far(a1)
    context_grad, out = context_backward(sum_grad, attn0, context0)
    projected_grad = attend_back(projected0, context_grad, slopes, seqs)
    qkv = dot(projected_grad, start, 0, 0).astype(BF16)
    a0 = attn_terms(qkv, out, [gain_one0, offset_one0, gain_two0, offset_two0])
    late_second = exchange(late, dp_masks=SECOND)
    projected_grad, a0, q0_a, p0_c, a1, late_second = together(projected_grad, a0, q0_a, p0_c, a1, late_second)

    a0 = attn_swap(a0)
    q0_own, q0_c = reduce_turn((q0_own, q0_half, q0_a))
    start_grad = dot(projected_grad, attn0[0], 1, 0) + sum_grad
    start_grad, a0, q0_b = together(start_grad, a0, q0_b)

    a0 = attn_pieces(a0)
    a0_got = exchange(jnp.stack(a0[2:]), dp_masks=SECOND)
    p0 = reduce_near(p0_own, p0_c, p0_b)
    input_grad = give(start_grad, middle_grad)
    a0_got, q0_c, p0, input_grad = together(a0_got, q0_c, p0, input_grad)

    a0_c = exchange(total_low(a0[1], a0_got[1]), dp_masks=FIRST)
    q0 = reduce_near(q0_own, q0_c, q0_b)
    p0 = reduce_far(p0)
    late_third = exchange(late_first, dp_masks=SECOND)
    late_got = [hand_over(late, 0), hand_over(late_first, 0)]
    a0_c, q0, p0, late_third, late_got = together(a0_c, q0, p0, late_third, late_got)

    a0 = reduce_near(a0[0], a0_got[0], a0_c)
    q0 = reduce_far(q0)
    attn_late = reduce_last(a1)
    attn = attn_late[:-NORM_ROWS]
    late_attn = [attn, exchange(attn, dp_masks=FIRST), exchange(attn, dp_masks=SECOND)]
    late_got += [hand_over(late_second, 0), hand_over(late_third, 0)]
    a0, q0, late_attn, late_got = together(a0, q0, late_attn, late_got)

    a0 = reduce_far(a0)
    late_attn.append(exchange(late_attn[1], dp_masks=SECOND))
    feed = jnp.concatenate([reduce_last(p0), reduce_last(q0)])
    feed_first = exchange(feed, dp_masks=FIRST)
    feed_got = [hand_over(feed, 1)]
    a0, late_attn, feed, feed_first, feed_got = together(a0, late_attn, feed, feed_first, feed_got)

    attn_early = reduce_last(a0)
    attn = attn_early[:-NORM_ROWS]
    attn_first, attn_second = exchange(attn, dp_masks=FIRST), exchange(attn, dp_masks=SECOND)
    feed_second = exchange(feed, dp_masks=SECOND)
    attn_late_all = jnp.stack(late_attn)
    attn_late_got = hand_over(attn_late_all, 0)
    feed_got.append(hand_over(feed_first, 1))
    attn_first, attn_second, feed_second, attn_late_got, feed_got = together(
        attn_first, attn_second, feed_second, attn_late_got, feed_got
    )

    attn_third, feed_third = exchange(attn_first, dp_masks=SECOND), exchange(feed_first, dp_masks=SECOND)
    feed_got.append(hand_over(feed_second, 1))
    attn_early_all = jnp.stack([attn, attn_first, attn_second, attn_third])
    attn_got = hand_over(attn_early_all, 1)
    feed_got.append(hand_over(feed_third, 1))

    feed_early = [feed, feed_first, feed_second, feed_third]
    feed_late = [late, late_first, late_second, late_third]
    grad_in, grad_down = settle(
        feed_early + feed_got + late_got + feed_late, flags, FEED_CHUNKS, 3, unit_part
    )
    parts = [jnp.where(is_first, attn_early_all, attn_late_got), jnp.where(is_first, attn_got, attn_late_all)]
    attn_total = jnp.stack(
        [
            jnp.stack(
                [
                    lax.dynamic_index_in_dim(parts[0], jnp.bitwise_xor(in_plane, index), 0, keepdims=False),
                    lax.dynamic_index_in_dim(parts[1], crossed(jnp.bitwise_xor(in_plane, index)), 0, keepdims=False),
                ]
            )
            for index in range(PLANE)
        ]
    )
    attn_total = attn_total.reshape(PLANE, 2, 2, local_heads, part, features)
    attn_total = jnp.transpose(attn_total, (1, 2, 3, 0, 4, 5)).reshape(4, local, features).astype(F32)
    grad_qkv = jnp.transpose(attn_total[:3], (2, 0, 1))
    grad_out = attn_total[3]

    vectors = jnp.where(is_first, attn_early[-NORM_ROWS:], attn_late[-NORM_ROWS:]).astype(F32)
    vectors = lax.dynamic_slice_in_dim(vectors, depth * local, local, 1)

    return (
        layer_out,
        input_grad,
        grad_qkv[None],
        grad_out[None],
        grad_in[None],
        grad_down[None],
        vectors[0][None],
        vectors[1][None],
        vectors[2][None],
        vectors[3][None],
    )


def solution(mesh):
    placed = (
        P(None, ("dp", "tensor"), None, None),
        P(None, ("dp", "tensor"), None, None),
        P(None, ("dp", "tensor"), None),
        P("section", None, None, "tensor"),
        P("section", "tensor", None),
        P("section", None, None, "tensor"),
        P("section", "tensor", None),
        P("section", None),
        P("section", None),
        P("section", None),
        P("section", None),
    )
    return jax.shard_map(
        body,
        mesh=mesh,
        in_specs=placed,
        out_specs=(
            P("section", None, ("dp", "tensor"), None, None),
            P("section", None, ("dp", "tensor"), None, None),
            P("section", None, None, "tensor"),
            P("section", "tensor", None),
            P("section", None, None, "tensor"),
            P("section", "tensor", None),
            P("section", "tensor"),
            P("section", "tensor"),
            P("section", "tensor"),
            P("section", "tensor"),
        ),
        check_vma=False,
    )
```

```python
import functools
import math

import jax
import jax.numpy as jnp
import numpy as np
from jax import lax
from jax.experimental import pallas as pl
from jax.experimental.pallas import tpu as pltpu
from jax.sharding import PartitionSpec as P

HEADS = 12
HEAD_DIM = 64
NORM_EPSILON = 1e-05
AXES = ("section", "dp", "tensor")
FEED_CHUNKS = 2
NORM_ROWS = 16
LANES = 128
GROUP = 3
GROUP_BACK = 3

F32 = jnp.float32
BF16 = jnp.bfloat16


def power_slopes(total_heads):
    return [2.0 ** (-8.0 * (index + 1) / total_heads) for index in range(total_heads)]


def alibi_table(number_heads):
    closest = 2 ** int(math.floor(math.log2(number_heads)))
    slopes = power_slopes(closest)
    slopes = slopes + power_slopes(2 * closest)[0::2][: number_heads - closest]
    return np.array(slopes, dtype=np.float32)


def norm_rows(values, gain, offset):
    row_mean = jnp.mean(values, axis=-1, keepdims=True)
    centred = values - row_mean
    row_var = jnp.mean(centred * centred, axis=-1, keepdims=True)
    return centred * lax.rsqrt(row_var + NORM_EPSILON) * gain + offset


def gelu_product(gate_part, up_part):
    return jax.nn.gelu(gate_part, approximate=False) * up_part


def dot(a, b, ca, cb):
    return lax.dot_general(a, b, (((ca,), (cb,)), ((), ())), preferred_element_type=F32)


def exchange(block, section_mask=0, dp_masks=(0, 0), tensor_mask=0):
    dp = lax.axis_size("dp")
    tensor = lax.axis_size("tensor")
    pairs = []
    for s in range(lax.axis_size("section")):
        for d in range(dp):
            for t in range(tensor):
                target = ((s ^ section_mask) * dp + (d ^ dp_masks[s])) * tensor + (t ^ tensor_mask)
                pairs.append(((s * dp + d) * tensor + t, target))
    return lax.ppermute(block, AXES, pairs)


def swap(block):
    return exchange(block, section_mask=1)


FIRST = (1, 2)
SECOND = (2, 1)
PLANE = 4
DEPTH = 4


def contract(a, b, ca, cb):
    return lax.dot_general(a, b, (((ca,), (cb,)), ((), ())), preferred_element_type=F32)


def head_masks(length):
    lane = lax.broadcasted_iota(jnp.int32, (length, LANES), 1)
    return [lane // HEAD_DIM == index for index in range(LANES // HEAD_DIM)]


def distances(length):
    across = lax.broadcasted_iota(jnp.int32, (length, length), 0)
    along = lax.broadcasted_iota(jnp.int32, (length, length), 1)
    return jnp.abs(across - along).astype(F32)


def attend_kernel(group, slopes_ref, projected_ref, context_ref):
    length, features = context_ref.shape
    masks = head_masks(length)
    distance = distances(length)
    per = len(masks)
    pairs = features // LANES
    for first in range(0, pairs, group):
        heads = [(pair, index) for pair in range(first, first + group) for index in range(per)]
        parts = {p: [slice(i * features + p * LANES, i * features + (p + 1) * LANES) for i in range(3)] for p, _ in heads}
        scores = []
        for pair, index in heads:
            key = projected_ref[:, parts[pair][1]]
            own = jnp.where(masks[index], key, jnp.zeros_like(key))
            scores.append(contract(own, projected_ref[:, parts[pair][0]], 1, 1))
        weights = []
        for (pair, index), score in zip(heads, scores):
            score = score * HEAD_DIM ** (-0.5) - slopes_ref[pair * per + index] * distance
            weight = jnp.exp(score - jnp.max(score, axis=0, keepdims=True))
            weight = weight * (1.0 / jnp.sum(weight, axis=0, keepdims=True))
            weights.append(weight.astype(BF16))
        for pair in range(first, first + group):
            value = projected_ref[:, parts[pair][2]]
            context = jnp.zeros((length, LANES), F32)
            for (other, index), weight in zip(heads, weights):
                if other == pair:
                    context = jnp.where(masks[index], contract(weight, value, 0, 0), context)
            context_ref[:, parts[pair][0]] = context.astype(BF16)


def attend_back_kernel(group, slopes_ref, projected_ref, context_grad_ref, grad_ref):
    length, features = context_grad_ref.shape
    masks = head_masks(length)
    distance = distances(length)
    per = len(masks)
    pairs = features // LANES
    for first in range(0, pairs, group):
        heads = [(pair, index) for pair in range(first, first + group) for index in range(per)]
        parts = {p: [slice(i * features + p * LANES, i * features + (p + 1) * LANES) for i in range(3)] for p, _ in heads}
        scores, weights_grads = [], []
        for pair, index in heads:
            key, value = projected_ref[:, parts[pair][1]], projected_ref[:, parts[pair][2]]
            own = jnp.where(masks[index], key, jnp.zeros_like(key))
            scores.append(contract(own, projected_ref[:, parts[pair][0]], 1, 1))
            own = jnp.where(masks[index], value, jnp.zeros_like(value))
            weights_grads.append(contract(own, context_grad_ref[:, parts[pair][0]], 1, 1))
        weights, score_grads = [], []
        for (pair, index), score, weights_grad in zip(heads, scores, weights_grads):
            score = score * HEAD_DIM ** (-0.5) - slopes_ref[pair * per + index] * distance
            weight = jnp.exp(score - jnp.max(score, axis=0, keepdims=True))
            weight = weight * (1.0 / jnp.sum(weight, axis=0, keepdims=True))
            mean_grad = jnp.sum(weight * weights_grad, axis=0, keepdims=True)
            score_grads.append((weight * (weights_grad - mean_grad)).astype(BF16))
            weights.append(weight.astype(BF16))
        for pair in range(first, first + group):
            query, key = projected_ref[:, parts[pair][0]], projected_ref[:, parts[pair][1]]
            context_grad = context_grad_ref[:, parts[pair][0]]
            grads = [jnp.zeros((length, LANES), F32)] * 3
            for (other, index), weight, score_grad in zip(heads, weights, score_grads):
                if other == pair:
                    new = [
                        contract(score_grad, key, 0, 0) * HEAD_DIM ** (-0.5),
                        contract(score_grad, query, 1, 0) * HEAD_DIM ** (-0.5),
                        contract(weight, context_grad, 1, 0),
                    ]
                    grads = [jnp.where(masks[index], n, g) for n, g in zip(new, grads)]
            for part, grad in zip(parts[pair], grads):
                grad_ref[:, part] = grad.astype(BF16)


def row_block(length, width):
    return pl.BlockSpec((length, width), lambda index: (index, 0))


def attend(projected, slopes, seqs):
    rows, width = projected.shape
    length, features = rows // seqs, width // 3
    return pl.pallas_call(
        functools.partial(attend_kernel, GROUP),
        grid=(seqs,),
        in_specs=[pl.BlockSpec(memory_space=pltpu.SMEM), row_block(length, width)],
        out_specs=row_block(length, features),
        out_shape=jax.ShapeDtypeStruct((rows, features), BF16),
        cost_estimate=pl.CostEstimate(flops=rows, bytes_accessed=rows, transcendentals=0),
        name="attend",
    )(slopes, projected)


def attend_back(projected, context_grad, slopes, seqs):
    rows, width = projected.shape
    length, features = rows // seqs, width // 3
    return pl.pallas_call(
        functools.partial(attend_back_kernel, GROUP_BACK),
        grid=(seqs,),
        in_specs=[
            pl.BlockSpec(memory_space=pltpu.SMEM),
            row_block(length, width),
            row_block(length, features),
        ],
        out_specs=row_block(length, width),
        out_shape=jax.ShapeDtypeStruct((rows, width), BF16),
        cost_estimate=pl.CostEstimate(flops=rows, bytes_accessed=rows, transcendentals=0),
        name="attend_back",
    )(slopes, projected, context_grad)


def settle_kernel(chunks, kinds, part, flags_ref, *refs):
    *pieces, gate_up_ref, down_ref, held = refs
    first = flags_ref[0] == 1
    count = len(pieces) // 4
    half_rows = chunks * count * part
    for half in range(2):
        for index in range(count):
            mine = pieces[half * count + index]
            other = pieces[(2 + half) * count + index]
            place = flags_ref[1 + half * count + index]
            for chunk in range(chunks):
                base = pl.multiple_of(half * half_rows + chunk * count * part + place * part, part)
                for kind in range(kinds):
                    start = (chunk * kinds + kind) * part
                    rows = jnp.where(first, mine[start : start + part, :], other[start : start + part, :]).astype(F32)
                    if kind < kinds - 1:
                        held[kind, pl.ds(base, part), :] = rows
                    else:
                        down_ref[pl.ds(base, part), :] = rows
    for kind in range(kinds - 1):
        gate_up_ref[:, kind, :] = jnp.transpose(held[kind])


def settle(pieces, flags, chunks, kinds, part):
    rows, features = pieces[0].shape
    units = 2 * (len(pieces) // 4) * chunks * part
    width = 2 * LANES
    return pl.pallas_call(
        functools.partial(settle_kernel, chunks, kinds, part),
        grid=(features // width,),
        in_specs=[pl.BlockSpec(memory_space=pltpu.SMEM)]
        + [pl.BlockSpec((rows, width), lambda index: (0, index))] * len(pieces),
        out_specs=[
            pl.BlockSpec((width, kinds - 1, units), lambda index: (index, 0, 0)),
            pl.BlockSpec((units, width), lambda index: (0, index)),
        ],
        out_shape=[
            jax.ShapeDtypeStruct((features, kinds - 1, units), F32),
            jax.ShapeDtypeStruct((units, features), F32),
        ],
        scratch_shapes=[pltpu.VMEM((kinds - 1, units, width), F32)],
        name="settle",
    )(flags, *pieces)


def together(*trees):
    return lax.optimization_barrier(trees)


def near(chunk):
    return dict(chunk, near=exchange(chunk["own"][0], tensor_mask=1))


def far(chunk):
    return dict(chunk, far=exchange(jnp.stack([chunk["own"][0], chunk["near"]]), tensor_mask=2))


def first(chunk):
    remote = jnp.concatenate([chunk["near"][None], chunk["far"]])
    return dict(
        chunk,
        remote=remote,
        first=exchange(remote, dp_masks=FIRST),
        second=exchange(remote, dp_masks=SECOND),
    )


def second(chunk):
    return dict(chunk, third=exchange(chunk["first"], dp_masks=SECOND))


def assemble(chunk):
    rest = [chunk["remote"], chunk["first"], chunk["second"], chunk["third"]]
    return jnp.stack([jnp.concatenate([own[None], r]) for own, r in zip(chunk["own"], rest)])


def add_low(a, b):
    return (a.astype(F32) + b.astype(F32)).astype(BF16)


def total_low(*parts):
    return sum(part.astype(F32) for part in parts).astype(BF16)


def reduce_open(terms):
    return (
        terms[0],
        terms[1],
        exchange(terms[3], dp_masks=SECOND),
        exchange(terms[2], dp_masks=SECOND),
    )


def reduce_turn(parts):
    return parts[0], exchange(total_low(parts[1], parts[2]), dp_masks=FIRST)


def reduce_near(own, turned, opened):
    pairs = total_low(own, turned, opened)
    pairs = pairs.reshape((2, 2) + pairs.shape[1:])
    return pairs[:, 0], exchange(pairs[:, 1], tensor_mask=1)


def reduce_far(pair):
    terms = total_low(*pair)
    return terms[0], exchange(terms[1], tensor_mask=2)


def reduce_last(pair):
    one = total_low(*pair)
    mask = PLANE
    while mask < lax.axis_size("dp"):
        one = total_low(one, exchange(one, dp_masks=(mask, mask)))
        mask *= 2
    return one


def attn_forward(own_low, weights, norms, slopes, seqs):
    wqkv, wo = weights
    projected = dot(own_low, wqkv, 1, 1).astype(BF16)
    context = attend(projected, slopes, seqs)
    first_sum = own_low.astype(F32) + dot(context, wo, 1, 0)
    first_norm = norm_rows(first_sum, norms[0], norms[1])
    return projected, context, first_sum, first_norm


def both_rows(rows_low):
    return jnp.concatenate([rows_low, swap(rows_low)])


def join_rows(terms):
    rows = terms.shape[0] // 2
    return terms[:rows] + swap(terms[rows:].astype(BF16)).astype(F32)


def feed_forward(first_all, weights):
    gate_up, down = weights
    gated = dot(first_all, gate_up, 1, 1)
    gate_part, up_part = jnp.split(gated, 2, axis=-1)
    hidden = gelu_product(gate_part, up_part).astype(BF16)
    return gated, hidden, dot(hidden, down, 1, 0)


def feed_backward(mixed_all, weights, gated):
    hidden_grad = dot(mixed_all, weights[1], 1, 1)
    gate_part, up_part = jnp.split(gated, 2, axis=-1)
    _, gelu_back = jax.vjp(gelu_product, gate_part, up_part)
    gate_grad, up_grad = gelu_back(hidden_grad)
    return jnp.concatenate([gate_grad, up_grad], axis=-1).astype(BF16)


def feed_weight_grads(mixed_all, first_all, gated_grad, hidden):
    return dot(gated_grad, first_all, 0, 0).astype(BF16), dot(hidden, mixed_all, 0, 0).astype(BF16)


def norm_backward(total, gain, offset, grad):
    _, back = jax.vjp(norm_rows, total, gain, offset)
    return back(grad)


def context_backward(sum_grad, weights, context):
    attended_low = sum_grad.astype(BF16)
    context_grad = dot(attended_low, weights[1], 1, 1).astype(BF16)
    return context_grad, dot(context, attended_low, 0, 0).astype(BF16)


def body(
    layer_input,
    out_grad,
    loss_mask,
    query_key_value_weight,
    attention_output_weight,
    gate_up_weight,
    down_weight,
    norm1_gain,
    norm1_bias,
    norm2_gain,
    norm2_bias,
):
    core = lax.axis_index("section")
    plane = lax.axis_index("dp")
    depth = lax.axis_index("tensor")
    is_first = core == 0
    micro, own_seqs, length, features = layer_input.shape
    local = query_key_value_weight.shape[-1]
    local_heads = local // HEAD_DIM
    units = down_weight.shape[1]
    part = HEAD_DIM // PLANE
    unit_part = units // 2 // PLANE // FEED_CHUNKS
    seqs = micro * own_seqs // 2
    rows = seqs * length

    in_plane = jnp.bitwise_and(plane, PLANE - 1)

    def crossed(e):
        return (e & 1) * 2 + (e >> 1)

    def relative(slab):
        return [
            lax.dynamic_index_in_dim(
                slab, jnp.bitwise_xor(in_plane, jnp.where(is_first, e, crossed(e))), 0, keepdims=False
            )
            for e in range(PLANE)
        ]

    def share(slab):
        keep = lax.dynamic_index_in_dim(slab, core, 0, keepdims=False)
        got = swap(lax.dynamic_index_in_dim(slab, 1 - core, 0, keepdims=False))
        return jnp.where(is_first, keep, got), jnp.where(is_first, got, keep)

    qkv_rows = jnp.transpose(query_key_value_weight[0], (1, 2, 0))
    attn_rows = jnp.concatenate([qkv_rows, attention_output_weight], axis=0)
    attn_slab = attn_rows.reshape(2, 2, local_heads, PLANE, part, features)
    attn_slab = jnp.transpose(attn_slab, (0, 3, 1, 2, 4, 5)).reshape(2, PLANE, -1, features)
    attn_in = [{"own": relative(own)} for own in share(attn_slab)]
    attn_in[0] = near(attn_in[0])
    attn_in, gate_up_weight, down_weight = together(attn_in, gate_up_weight, down_weight)
    gate_up_rows = jnp.transpose(gate_up_weight[0], (1, 2, 0))
    feed_rows = jnp.concatenate([gate_up_rows, down_weight], axis=0)
    feed_slab = feed_rows.reshape(3, 2, FEED_CHUNKS, PLANE, unit_part, features)
    feed_slab = jnp.transpose(feed_slab, (2, 1, 3, 0, 4, 5)).reshape(FEED_CHUNKS, 2, PLANE, -1, features)

    feed_in = [[{"own": relative(own)} for own in share(feed_slab[k])] for k in range(FEED_CHUNKS)]
    a0, a1 = attn_in
    (p0, p1), (q0, q1) = feed_in


    norm_table = jnp.concatenate([norm1_gain, norm1_bias, norm2_gain, norm2_bias])
    norm_other = swap(norm_table)
    norm_first = jnp.where(is_first, norm_table, norm_other)
    norm_second = jnp.where(is_first, norm_other, norm_table)
    norms = [tuple(table[i] for i in range(4)) for table in (norm_first, norm_second)]

    slope_table = jnp.asarray(alibi_table(HEADS)).reshape(DEPTH, local_heads)
    slopes = jnp.concatenate(
        [lax.dynamic_index_in_dim(slope_table, jnp.bitwise_xor(depth, j), 0, keepdims=False) for j in range(DEPTH)]
    )

    def own_half(whole):
        flat = whole.reshape((2, rows) + whole.shape[3:])
        return lax.dynamic_index_in_dim(flat, core, 0, keepdims=False)

    start = own_half(layer_input)
    seed = own_half(out_grad).astype(F32) * own_half(loss_mask).astype(F32)[..., None]


    def attn_weights(chunk):
        full = assemble(chunk).reshape(PLANE, DEPTH, 2, local_heads, part, features)
        mine = jnp.transpose(full, (2, 1, 3, 0, 4, 5)).reshape(2, -1, features)
        other = swap(mine)
        qk = jnp.where(is_first, mine, other)
        vo = jnp.where(is_first, other, mine)
        wqkv = jnp.concatenate([qk.reshape(-1, features), vo[0]])
        return wqkv, vo[1]

    def feed_weights(chunk):
        full = assemble(chunk).reshape(PLANE * DEPTH, 3, unit_part, features)
        full = jnp.transpose(full, (1, 0, 2, 3)).reshape(3, -1, features)
        return full[:2].reshape(-1, features), full[2]

    a0, p0 = far(a0), near(p0)
    a0, p0, q0, norms = together(a0, p0, q0, norms)
    a0, p0, q0 = first(a0), far(p0), near(q0)
    a0, p0, q0, a1 = together(a0, p0, q0, a1)
    a0, p0, q0, a1 = second(a0), first(p0), far(q0), near(a1)
    a0, p0, q0, a1, p1 = together(a0, p0, q0, a1, p1)
    p0, q0, a1, p1 = second(p0), first(q0), far(a1), near(p1)
    attn0 = attn_weights(a0)
    projected0, context0, sum0, norm0 = attn_forward(start, attn0, norms[0], slopes, seqs)
    low0, p0, q0, a1, p1, q1 = together(norm0.astype(BF16), p0, q0, a1, p1, q1)
    q0, a1, p1, q1 = second(q0), first(a1), far(p1), near(q1)
    all0 = both_rows(low0)
    feed_p0 = feed_weights(p0)
    gated_p0, hidden_p0, mixed = feed_forward(all0, feed_p0)
    mixed, q0, a1, p1, q1 = together(mixed, q0, a1, p1, q1)
    a1, p1, q1 = second(a1), first(p1), far(q1)
    feed_q0 = feed_weights(q0)
    gated_q0, hidden_q0, more = feed_forward(all0, feed_q0)
    mixed = mixed + more
    places = [jnp.bitwise_xor(in_plane, e) for e in range(PLANE)]
    places += [jnp.bitwise_xor(in_plane, crossed(e)) for e in range(PLANE)]
    flags = jnp.stack([is_first.astype(jnp.int32)] + places)
    mixed, a1, p1, q1, seed, flags = together(mixed, a1, p1, q1, seed, flags)
    p1, q1 = second(p1), first(q1)
    attn1 = attn_weights(a1)
    total0 = norm0 + join_rows(mixed)
    middle_low = norm_rows(total0, norms[0][2], norms[0][3]).astype(BF16)
    projected1, context1, sum1, norm1 = attn_forward(middle_low, attn1, norms[1], slopes, seqs)
    low1, p1, q1 = together(norm1.astype(BF16), p1, q1)
    q1 = second(q1)
    all1 = both_rows(low1)
    feed_p1 = feed_weights(p1)
    gated_p1, hidden_p1, mixed = feed_forward(all1, feed_p1)
    mixed, q1 = together(mixed, q1)
    feed_q1 = feed_weights(q1)
    gated_q1, hidden_q1, more = feed_forward(all1, feed_q1)
    total1 = norm1 + join_rows(mixed + more)
    final_low = norm_rows(total1, norms[1][2], norms[1][3]).astype(BF16)

    def give(early, late):
        mine = jnp.where(is_first, early, late)
        got = swap(jnp.where(is_first, late, early))
        both = jnp.concatenate([jnp.where(is_first, mine, got), jnp.where(is_first, got, mine)])
        return both.reshape((1, micro, own_seqs, length, features))

    def feed_terms(gate_up, down):
        full = jnp.concatenate([gate_up, down]).reshape(3, PLANE, DEPTH, unit_part, features)
        full = jnp.transpose(full, (1, 2, 0, 3, 4)).reshape(PLANE, DEPTH, -1, features)
        return [full[e] for e in range(PLANE)]

    def attn_terms(qkv, out, vectors):
        spread = jnp.pad(jnp.stack(vectors).astype(BF16), ((0, NORM_ROWS - len(vectors)), (0, 0)))
        spread = jnp.broadcast_to(spread, (2, PLANE, DEPTH, NORM_ROWS, features))
        full = jnp.concatenate([qkv, out]).reshape(2, 2, DEPTH, local_heads, PLANE, part, features)
        full = jnp.transpose(full, (0, 4, 2, 1, 3, 5, 6)).reshape(2, PLANE, DEPTH, -1, features)
        return jnp.concatenate([full, spread], axis=3)

    def attn_swap(full):
        keep = lax.dynamic_index_in_dim(full, core, 0, keepdims=False)
        return keep, swap(lax.dynamic_index_in_dim(full, 1 - core, 0, keepdims=False))

    def attn_pieces(pair):
        full = total_low(*pair)
        return [full[e] for e in range(PLANE)]

    def hand_over(block, source):
        planes, depths = lax.axis_size("dp"), lax.axis_size("tensor")
        count = planes * depths
        pairs = [(source * count + i, (1 - source) * count + i) for i in range(count)]
        return lax.ppermute(block, AXES, pairs)

    second_grad, gain_two1, offset_two1 = norm_backward(total1, norms[1][2], norms[1][3], seed)
    mixed_all = both_rows(second_grad.astype(BF16))
    grad_p = feed_backward(mixed_all, feed_p1, gated_p1)
    p1 = feed_terms(*feed_weight_grads(mixed_all, all1, grad_p, hidden_p1))
    mixed_all, grad_p, p1 = together(mixed_all, grad_p, p1)

    p1_own, p1_half, p1_a, p1_b = reduce_open(p1)
    terms = dot(grad_p, feed_p1[0], 1, 0)
    grad_q = feed_backward(mixed_all, feed_q1, gated_q1)
    terms = terms + dot(grad_q, feed_q1[0], 1, 0)
    q1 = feed_terms(*feed_weight_grads(mixed_all, all1, grad_q, hidden_q1))
    layer_out = give(middle_low, final_low)
    terms, q1, p1_a, layer_out = together(terms, q1, p1_a, layer_out)

    p1_own, p1_c = reduce_turn((p1_own, p1_half, p1_a))
    first_grad = join_rows(terms) + second_grad
    sum_grad, gain_one1, offset_one1 = norm_backward(sum1, norms[1][0], norms[1][1], first_grad)
    context_grad, out = context_backward(sum_grad, attn1, context1)
    context_grad, out, q1, p1_b = together(context_grad, out, q1, p1_b)

    q1_own, q1_half, q1_a, q1_b = reduce_open(q1)
    projected_grad = attend_back(projected1, context_grad, slopes, seqs)
    projected_grad, q1_a, p1_c = together(projected_grad, q1_a, p1_c)

    qkv = dot(projected_grad, middle_low, 0, 0).astype(BF16)
    a1 = attn_swap(attn_terms(qkv, out, [gain_one1, offset_one1, gain_two1, offset_two1]))
    q1_own, q1_c = reduce_turn((q1_own, q1_half, q1_a))
    p1 = reduce_near(p1_own, p1_c, p1_b)
    middle_grad = dot(projected_grad, attn1[0], 1, 0) + sum_grad
    second_grad, gain_two0, offset_two0 = norm_backward(total0, norms[0][2], norms[0][3], middle_grad)
    mixed_low = second_grad.astype(BF16)
    mixed_low, a1, q1_b, p1 = together(mixed_low, a1, q1_b, p1)

    mixed_all = both_rows(mixed_low)
    a1_own, a1_half, a1_a, a1_b = reduce_open(attn_pieces(a1))
    p1 = reduce_far(p1)
    grad_p = feed_backward(mixed_all, feed_p0, gated_p0)
    mixed_all, grad_p, a1_a, q1_c, p1 = together(mixed_all, grad_p, a1_a, q1_c, p1)

    a1_own, a1_c = reduce_turn((a1_own, a1_half, a1_a))
    q1 = reduce_near(q1_own, q1_c, q1_b)
    p0 = feed_terms(*feed_weight_grads(mixed_all, all0, grad_p, hidden_p0))
    terms = dot(grad_p, feed_p0[0], 1, 0)
    mixed_all, terms, p0, a1_b, q1 = together(mixed_all, terms, p0, a1_b, q1)

    p0_own, p0_half, p0_a, p0_b = reduce_open(p0)
    q1 = reduce_far(q1)
    grad_q = feed_backward(mixed_all, feed_q0, gated_q0)
    terms = terms + dot(grad_q, feed_q0[0], 1, 0)
    terms, grad_q, p0_a, a1_c, q1 = together(terms, grad_q, p0_a, a1_c, q1)

    p0_own, p0_c = reduce_turn((p0_own, p0_half, p0_a))
    a1 = reduce_near(a1_own, a1_c, a1_b)
    late = jnp.concatenate([reduce_last(p1), reduce_last(q1)])
    late_first = exchange(late, dp_masks=FIRST)
    q0 = feed_terms(*feed_weight_grads(mixed_all, all0, grad_q, hidden_q0))
    first_grad = join_rows(terms) + second_grad
    sum_grad, gain_one0, offset_one0 = norm_backward(sum0, norms[0][0], norms[0][1], first_grad)
    sum_grad, q0, p0_b, a1, late, late_first = together(sum_grad, q0, p0_b, a1, late, late_first)

    q0_own, q0_half, q0_a, q0_b = reduce_open(q0)
    a1 = reduce_far(a1)
    context_grad, out = context_backward(sum_grad, attn0, context0)
    projected_grad = attend_back(projected0, context_grad, slopes, seqs)
    late_second = exchange(late, dp_masks=SECOND)
    projected_grad, q0_a, p0_c, a1, late_second = together(projected_grad, q0_a, p0_c, a1, late_second)

    qkv = dot(projected_grad, start, 0, 0).astype(BF16)
    a0 = attn_swap(attn_terms(qkv, out, [gain_one0, offset_one0, gain_two0, offset_two0]))
    q0_own, q0_c = reduce_turn((q0_own, q0_half, q0_a))
    start_grad = dot(projected_grad, attn0[0], 1, 0) + sum_grad
    start_grad, a0, q0_b = together(start_grad, a0, q0_b)

    a0 = attn_pieces(a0)
    a0_got = exchange(jnp.stack(a0[2:]), dp_masks=SECOND)
    p0 = reduce_near(p0_own, p0_c, p0_b)
    input_grad = give(start_grad, middle_grad)
    a0_got, q0_c, p0, input_grad = together(a0_got, q0_c, p0, input_grad)

    a0_c = exchange(total_low(a0[1], a0_got[1]), dp_masks=FIRST)
    q0 = reduce_near(q0_own, q0_c, q0_b)
    p0 = reduce_far(p0)
    late_third = exchange(late_first, dp_masks=SECOND)
    late_got = [hand_over(late, 0), hand_over(late_first, 0)]
    a0_c, q0, p0, late_third, late_got = together(a0_c, q0, p0, late_third, late_got)

    a0 = reduce_near(a0[0], a0_got[0], a0_c)
    q0 = reduce_far(q0)
    attn_late = reduce_last(a1)
    attn = attn_late[:-NORM_ROWS]
    late_attn = [attn, exchange(attn, dp_masks=FIRST), exchange(attn, dp_masks=SECOND)]
    late_got += [hand_over(late_second, 0), hand_over(late_third, 0)]
    a0, q0, late_attn, late_got = together(a0, q0, late_attn, late_got)

    a0 = reduce_far(a0)
    late_attn.append(exchange(late_attn[1], dp_masks=SECOND))
    feed = jnp.concatenate([reduce_last(p0), reduce_last(q0)])
    feed_first = exchange(feed, dp_masks=FIRST)
    feed_got = [hand_over(feed, 1)]
    a0, late_attn, feed, feed_first, feed_got = together(a0, late_attn, feed, feed_first, feed_got)

    attn_early = reduce_last(a0)
    attn = attn_early[:-NORM_ROWS]
    attn_first, attn_second = exchange(attn, dp_masks=FIRST), exchange(attn, dp_masks=SECOND)
    feed_second = exchange(feed, dp_masks=SECOND)
    attn_late_all = jnp.stack(late_attn)
    attn_late_got = hand_over(attn_late_all, 0)
    feed_got.append(hand_over(feed_first, 1))
    attn_first, attn_second, feed_second, attn_late_got, feed_got = together(
        attn_first, attn_second, feed_second, attn_late_got, feed_got
    )

    attn_third, feed_third = exchange(attn_first, dp_masks=SECOND), exchange(feed_first, dp_masks=SECOND)
    feed_got.append(hand_over(feed_second, 1))
    attn_early_all = jnp.stack([attn, attn_first, attn_second, attn_third])
    attn_got = hand_over(attn_early_all, 1)
    feed_got.append(hand_over(feed_third, 1))

    feed_early = [feed, feed_first, feed_second, feed_third]
    feed_late = [late, late_first, late_second, late_third]
    grad_in, grad_down = settle(
        feed_early + feed_got + late_got + feed_late, flags, FEED_CHUNKS, 3, unit_part
    )
    parts = [jnp.where(is_first, attn_early_all, attn_late_got), jnp.where(is_first, attn_got, attn_late_all)]
    attn_total = jnp.stack(
        [
            jnp.stack(
                [
                    lax.dynamic_index_in_dim(parts[0], jnp.bitwise_xor(in_plane, index), 0, keepdims=False),
                    lax.dynamic_index_in_dim(parts[1], crossed(jnp.bitwise_xor(in_plane, index)), 0, keepdims=False),
                ]
            )
            for index in range(PLANE)
        ]
    )
    attn_total = attn_total.reshape(PLANE, 2, 2, local_heads, part, features)
    attn_total = jnp.transpose(attn_total, (1, 2, 3, 0, 4, 5)).reshape(4, local, features).astype(F32)
    grad_qkv = jnp.transpose(attn_total[:3], (2, 0, 1))
    grad_out = attn_total[3]

    vectors = jnp.where(is_first, attn_early[-NORM_ROWS:], attn_late[-NORM_ROWS:]).astype(F32)
    vectors = lax.dynamic_slice_in_dim(vectors, depth * local, local, 1)

    return (
        layer_out,
        input_grad,
        grad_qkv[None],
        grad_out[None],
        grad_in[None],
        grad_down[None],
        vectors[0][None],
        vectors[1][None],
        vectors[2][None],
        vectors[3][None],
    )


def solution(mesh):
    placed = (
        P(None, ("dp", "tensor"), None, None),
        P(None, ("dp", "tensor"), None, None),
        P(None, ("dp", "tensor"), None),
        P("section", None, None, "tensor"),
        P("section", "tensor", None),
        P("section", None, None, "tensor"),
        P("section", "tensor", None),
        P("section", None),
        P("section", None),
        P("section", None),
        P("section", None),
    )
    return jax.shard_map(
        body,
        mesh=mesh,
        in_specs=placed,
        out_specs=(
            P("section", None, ("dp", "tensor"), None, None),
            P("section", None, ("dp", "tensor"), None, None),
            P("section", None, None, "tensor"),
            P("section", "tensor", None),
            P("section", None, None, "tensor"),
            P("section", "tensor", None),
            P("section", "tensor"),
            P("section", "tensor"),
            P("section", "tensor"),
            P("section", "tensor"),
        ),
        check_vma=False,
    )
```
